32 devices in a mesh: seg: 16 (over z, y, core), head: 2 (over x).
Axes of the slice: x: 2, y: 2, z: 4, core: 2. Of those that a mesh axis runs over, the one named last changes fastest.
Arguments:
- tokens: bfloat16 [16384, 1024], P('seg'), may hold values from -6 to 6
- document_ids: int32 [16, 1024], P('seg'), may hold values from 0 to 3, never falling along the last dimension, each value on 1 to 512 neighbouring positions
- memory_picks: int32 [16, 8, 8, 6144], P('seg', 'head'), may hold values from 0 to 1, as said below
- partner_ids: int32 [16], P('seg'), may hold values from 0 to 15, as said below
- memory_keys: bfloat16 [16, 3072, 1024], P('seg', None, 'head'), may hold values from -6 to 6
- memory_values: bfloat16 [16, 3072, 1024], P('seg', None, 'head'), may hold values from -6 to 6
- first_gain: float32 [1024], replicated, may hold values from 0.1 to 1.9
- query_weight: bfloat16 [1024, 1024], P(None, 'head'), may hold values from -0.1875 to 0.1875
- key_weight: bfloat16 [1024, 1024], P(None, 'head'), may hold values from -0.1875 to 0.1875
- value_weight: bfloat16 [1024, 1024], P(None, 'head'), may hold values from -0.1875 to 0.1875
- out_weight: bfloat16 [1024, 1024], P('head'), may hold values from -0.75 to 0.75
- second_gain: float32 [1024], replicated, may hold values from 0.1 to 1.9
- gate_weight: bfloat16 [1024, 2816], P(None, 'head'), may hold values from -0.1875 to 0.1875
- up_weight: bfloat16 [1024, 2816], P(None, 'head'), may hold values from -0.1875 to 0.1875
- down_weight: bfloat16 [2816, 1024], P('head'), may hold values from -0.21875 to 0.21875
- cotangent: bfloat16 [16384, 1024], P('seg'), may hold values from -6 to 6
Outputs:
- output: bfloat16 [16384, 1024], P('seg')
- tokens_grad: bfloat16 [16384, 1024], P('seg')
- first_gain_grad: float32 [1024], replicated
- query_grad: float32 [1024, 1024], P(None, 'head')
- key_grad: float32 [1024, 1024], P(None, 'head')
- value_grad: float32 [1024, 1024], P(None, 'head')
- out_grad: float32 [1024, 1024], P('head')
- second_gain_grad: float32 [1024], replicated
- gate_grad: float32 [1024, 2816], P(None, 'head')
- up_grad: float32 [1024, 2816], P(None, 'head')
- down_grad: float32 [2816, 1024], P('head')
The draws below stay inside these ranges and needn't reach their ends.
Inputs may be any that keep to these rules, and one draw needn't show every extreme that they name: `memory_picks`: each row of the last dimension holds exactly 128 ones, the rest zeros. partner_ids[s] = p + s % 1, where p differs from s // 1 in exactly one binary digit.
All inputs are finite; a program needn't handle non-finite values.
Results may differ from the reference program's by a relative error of at most 0.028.
Values may be sent and summed in bfloat16 or wider, within the bound.
No kernel may reach another device: no remote copies, remote signals or barrier semaphores. Data moves between devices by JAX's collectives and lax.ppermute only.
A program may use at most 192 MiB of HBM per device.

```python
import math
import jax
import jax.numpy as jnp
import numpy as np
from jax import lax

D = 1024
H = 8
HEAD_DIM = 128
FF = 2816
SEG_LEN = 1024
MEM = 3072
KPICK = 128
PICK_BLOCK = 128
DOCS = 4
SEGS_DEV = 1
DOC_MOST = 512
SEGS = 16
TOKENS = 16384
N_SEG = 16
N_HEAD = 2


def draw_memory_picks(key, part):
    shape = (SEGS, H, SEG_LEN // PICK_BLOCK, 2 * MEM)
    raw_scores = jax.random.randint(key, shape, 0, 2 ** 18, dtype=jnp.int32)
    distinct = raw_scores * (2 * MEM) + jnp.arange(2 * MEM, dtype=jnp.int32)
    top_values = lax.top_k(distinct, KPICK)[0]
    cutoff = top_values[..., KPICK - 1:KPICK]
    return (distinct >= cutoff).astype(jnp.int32)


def draw_partner_ids(key, part):
    digit_count = N_SEG.bit_length() - 1
    segment_index = jnp.arange(SEGS, dtype=jnp.int32)
    flipped = jax.random.randint(key, (SEGS,), 0, digit_count, dtype=jnp.int32)
    device_index = segment_index // SEGS_DEV
    partner_device = jnp.bitwise_xor(device_index, jnp.left_shift(jnp.ones_like(flipped), flipped))
    return partner_device * SEGS_DEV + segment_index % SEGS_DEV


def shard_levels(key, dims, split, low, largest):
    factor_of = 1.0
    for axis_at, shards_of in split:
        heights = jax.random.uniform(jax.random.fold_in(jax.random.fold_in(key, 6), axis_at), (shards_of,), jnp.float32, low / len(split), largest / len(split))
        factor_of = factor_of * jnp.repeat(jnp.exp(heights), dims[axis_at] // shards_of).reshape((-1,) + (1,) * (len(dims) - 1 - axis_at))
    return factor_of


def length_profile(count, total, limit, slope):
    loads = [(1 << 20) // math.isqrt(standing ** slope) + 1 for standing in range(2, count + 1)]
    surplus, given = total - limit - (count - 1), [1] * (count - 1)
    while surplus > 0:
        free = [i for i in range(count - 1) if given[i] < limit]
        pool, left = sum([loads[i] for i in free]), surplus
        for i in free:
            addition = min(limit - given[i], max(1, left * loads[i] // pool), surplus)
            given[i] = given[i] + addition
            surplus = surplus - addition
    return np.array([limit] + given)


def uneven_parts(stream_key, number_of, total, most, skew):
    if number_of == 2:
        one = jax.random.randint(stream_key, (), max(1, total - most), min(most, total - 1) + 1)
        return jnp.stack([one, total - one])
    lengths = jnp.asarray(length_profile(number_of, total, most, skew), jnp.int32)
    couples = (number_of - 1) // 2
    donor, taker = lengths[1:1 + 2 * couples:2], lengths[2:2 + 2 * couples:2]
    slack = jnp.minimum(donor - 1, most - taker)
    passed = jax.random.randint(jax.random.fold_in(stream_key, 1), (couples,), 0, 1 << 20) % (slack + 1)
    lengths = lengths.at[1:1 + 2 * couples:2].set(donor - passed).at[2:2 + 2 * couples:2].set(taker + passed)
    return lengths[jax.random.permutation(jax.random.fold_in(stream_key, 2), number_of)]


def bell_draw(own_key, dims, spread, bound, cuts=(), held_as=jnp.bfloat16):
    loudness = shard_levels(own_key, dims, cuts, -0.22, 0.18) if cuts else 1.0
    entries = jax.random.normal(own_key, dims, jnp.float32) * spread * loudness
    return jnp.minimum(jnp.maximum(entries, -bound), bound).astype(held_as)


def setup_inputs(seed: int = 0) -> dict:
    arg_keys = jax.random.split(jax.random.key(seed), 17)
    tokens = bell_draw(arg_keys[0], (TOKENS, D), 1.0, 6.0, ((0, 16),))
    document_ids = jax.vmap(lambda own: jnp.searchsorted(jnp.cumsum(uneven_parts(own, DOCS, SEG_LEN, DOC_MOST, 1)), jnp.arange(SEG_LEN), side="right"))(jax.random.split(arg_keys[1], SEGS)).reshape((SEGS, SEG_LEN)).astype(jnp.int32)
    memory_picks = draw_memory_picks(jax.random.fold_in(arg_keys[16], 71), 0)
    partner_ids = draw_partner_ids(jax.random.fold_in(arg_keys[16], 71), 0)
    memory_keys = bell_draw(arg_keys[4], (SEGS, MEM, H * HEAD_DIM), 1.0, 6.0, ((0, 16), (2, 2)))
    memory_values = bell_draw(arg_keys[5], (SEGS, MEM, H * HEAD_DIM), 1.0, 6.0, ((0, 16), (2, 2)))
    first_gain = jnp.clip(1.0 + 0.18 * jax.random.normal(arg_keys[6], (D,), jnp.float32), 0.1, 1.9)
    query_weight = bell_draw(arg_keys[7], (D, H * HEAD_DIM), D ** -0.5, 0.1875, ((1, 2),))
    key_weight = bell_draw(arg_keys[8], (D, H * HEAD_DIM), D ** -0.5, 0.1875, ((1, 2),))
    value_weight = bell_draw(arg_keys[9], (D, H * HEAD_DIM), D ** -0.5, 0.1875, ((1, 2),))
    out_weight = bell_draw(arg_keys[10], (H * HEAD_DIM, D), (H * HEAD_DIM // 16) ** -0.5, 0.75, ((0, 2),))
    second_gain = jnp.clip(1.0 + 0.18 * jax.random.normal(arg_keys[11], (D,), jnp.float32), 0.1, 1.9)
    gate_weight = bell_draw(arg_keys[12], (D, FF), D ** -0.5, 0.1875, ((1, 2),))
    up_weight = bell_draw(arg_keys[13], (D, FF), D ** -0.5, 0.1875, ((1, 2),))
    down_weight = bell_draw(arg_keys[14], (FF, D), (FF // 4) ** -0.5, 0.21875, ((0, 2),))
    cotangent = bell_draw(arg_keys[15], (TOKENS, D), 1.0, 6.0, ((0, 16),))
    return {"tokens": tokens, "document_ids": document_ids, "memory_picks": memory_picks, "partner_ids": partner_ids, "memory_keys": memory_keys, "memory_values": memory_values, "first_gain": first_gain, "query_weight": query_weight, "key_weight": key_weight, "value_weight": value_weight, "out_weight": out_weight, "second_gain": second_gain, "gate_weight": gate_weight, "up_weight": up_weight, "down_weight": down_weight, "cotangent": cotangent}


EPS = 1e-05
NEG = -1e+30
THETA = 10000.0
HIGH = lax.Precision.HIGHEST

@jax.custom_vjp
def low(v):
    return lax.optimization_barrier(v.astype(jnp.bfloat16)).astype(jnp.float32)

@jax.custom_vjp
def low_back(v):
    return v

def low_keep(v):
    return (low(v), None)

def low_pass(kept, grad):
    return (grad,)

def back_keep(v):
    return (v, None)

def back_low(kept, grad):
    return (low(grad),)
low.defvjp(low_keep, low_pass)
low_back.defvjp(back_keep, back_low)

def matmul(left, right):
    return jnp.dot(left, right, precision=HIGH, preferred_element_type=jnp.float32)

def rope_tables(length, half_dim):
    position = jnp.arange(length, dtype=jnp.float32)[:, None]
    frequency = THETA ** (-jnp.arange(half_dim, dtype=jnp.float32) / half_dim)
    angles = position * frequency[None, :]
    return (jnp.cos(angles)[:, None, :], jnp.sin(angles)[:, None, :])

def rotate(values, cosine, sine_table):
    half_dim = values.shape[-1] // 2
    first_half = values[..., :half_dim]
    second_half = values[..., half_dim:]
    return jnp.concatenate([first_half * cosine - second_half * sine_table, second_half * cosine + first_half * sine_table], axis=-1)

def rms_scale(token_rows):
    return lax.rsqrt(lax.optimization_barrier(jnp.mean(token_rows * token_rows, axis=-1, keepdims=True)) + EPS)

def segment_forward(segment_tokens, params, cache_keys, cache_values, picks_seg, docs_seg):
    first_gain, query_weight, key_weight, value_weight, out_weight, second_gain, gate_weight, up_weight, down_weight = params
    length = segment_tokens.shape[0]
    cosine, sine_table = rope_tables(length, HEAD_DIM // 2)
    normed_one = low(segment_tokens * rms_scale(segment_tokens) * first_gain)

    def split_heads(flat):
        return flat.reshape(length, H, HEAD_DIM)
    queries = low(rotate(split_heads(low_back(matmul(normed_one, query_weight))), cosine, sine_table))
    keys_rot = low(rotate(split_heads(low_back(matmul(normed_one, key_weight))), cosine, sine_table))
    values = low(split_heads(low_back(matmul(normed_one, value_weight))))
    score_scale = 1.0 / math.sqrt(HEAD_DIM)
    local_scores = jnp.einsum('qhd,khd->hqk', queries, keys_rot, precision=HIGH) * score_scale
    far_scores = jnp.einsum('qhd,khd->hqk', queries, cache_keys, precision=HIGH) * score_scale
    scores = low_back(jnp.concatenate([local_scores, far_scores], axis=2))
    positions = jnp.arange(length)
    local_ok = (positions[None, :] <= positions[:, None]) & (docs_seg[None, :] == docs_seg[:, None])
    first_doc = docs_seg == docs_seg[0]
    picked = jnp.repeat(picks_seg > 0, PICK_BLOCK, axis=1)
    far_ok = picked & first_doc[None, :, None]
    allowed = jnp.concatenate([jnp.broadcast_to(local_ok[None], (H, length, length)), far_ok], axis=2)
    scores = jnp.where(allowed, scores, NEG)
    row_max = lax.optimization_barrier(jnp.max(scores, axis=2, keepdims=True))
    exponent = jnp.exp(scores - row_max)
    soft_weights = low(exponent / lax.optimization_barrier(jnp.sum(exponent, axis=2, keepdims=True)))
    attended = jnp.einsum('hqk,khd->qhd', soft_weights[:, :, :length], values, precision=HIGH)
    attended = attended + jnp.einsum('hqk,khd->qhd', soft_weights[:, :, length:], cache_values, precision=HIGH)
    group_cols = H * HEAD_DIM // N_HEAD
    attended = low(low_back(attended)).reshape(length, N_HEAD, group_cols)
    out_parts = jnp.einsum('lgc,gcd->lgd', attended, out_weight.reshape(N_HEAD, group_cols, D), precision=HIGH)
    mixed = low_back(lax.optimization_barrier(jnp.sum(low(out_parts), axis=1)))
    hidden_in = segment_tokens + mixed
    normed_two = low(hidden_in * rms_scale(hidden_in) * second_gain)
    gate = low_back(matmul(normed_two, gate_weight))
    upper = low_back(matmul(normed_two, up_weight))
    group_units = FF // N_HEAD
    hidden = low(jax.nn.silu(gate) * upper).reshape(length, N_HEAD, group_units)
    down_parts = jnp.einsum('lgf,gfd->lgd', hidden, down_weight.reshape(N_HEAD, group_units, D), precision=HIGH)
    return hidden_in + lax.optimization_barrier(jnp.sum(low(down_parts), axis=1))

def reference(tokens, document_ids, memory_picks, partner_ids, memory_keys, memory_values, first_gain, query_weight, key_weight, value_weight, out_weight, second_gain, gate_weight, up_weight, down_weight, cotangent):
    params = tuple((weight_item.astype(jnp.float32) for weight_item in (first_gain, query_weight, key_weight, value_weight, out_weight, second_gain, gate_weight, up_weight, down_weight)))
    inputs = tokens.astype(jnp.float32).reshape(SEGS, SEG_LEN, D)
    cot_float = cotangent.astype(jnp.float32).reshape(SEGS, SEG_LEN, D)

    def per_segment(grad_carry, segment_item):
        segment_tokens, own_keys, own_values, partner_index, picks_seg, docs_seg, segment_cot = segment_item
        other_keys = lax.dynamic_index_in_dim(memory_keys, partner_index.astype(jnp.int32), axis=0, keepdims=False)
        other_values = lax.dynamic_index_in_dim(memory_values, partner_index.astype(jnp.int32), axis=0, keepdims=False)
        cache_keys = jnp.concatenate([own_keys, other_keys], axis=0).astype(jnp.float32).reshape(2 * MEM, H, HEAD_DIM)
        cache_values = jnp.concatenate([own_values, other_values], axis=0).astype(jnp.float32).reshape(2 * MEM, H, HEAD_DIM)

        def forward_fn(tokens_in, params_in):
            return segment_forward(tokens_in, params_in, cache_keys, cache_values, picks_seg, docs_seg)
        result, pullback = jax.vjp(forward_fn, segment_tokens, params)
        grad_tokens, grad_params = pullback(segment_cot)
        grad_carry = tuple((carried + added for carried, added in zip(grad_carry, grad_params)))
        return (grad_carry, (result, grad_tokens))
    init_grads = tuple((jnp.zeros_like(weight_item) for weight_item in params))
    grad_sums, (results, grad_tokens) = lax.scan(per_segment, init_grads, (inputs, memory_keys, memory_values, partner_ids, memory_picks, document_ids, cot_float))
    output = results.reshape(TOKENS, D).astype(jnp.bfloat16)
    tokens_grad = grad_tokens.reshape(TOKENS, D).astype(jnp.bfloat16)
    return (output, tokens_grad, grad_sums[0], grad_sums[1], grad_sums[2], grad_sums[3], grad_sums[4], grad_sums[5], grad_sums[6], grad_sums[7], grad_sums[8])
```

```python
import functools
import math

import jax
import jax.numpy as jnp
from jax import lax
from jax.experimental import pallas as pl
from jax.experimental.pallas import tpu as pltpu
from jax.sharding import PartitionSpec as P

HEAD_DIM = 128
KPICK = 128
PICK_BLOCK = 128
DOC_MOST = 512
SUB = 256

EPS = 1e-05
NEG = -1e30
THETA = 10000.0
BF = jnp.bfloat16
F32 = jnp.float32


def dot(a, b, ca, cb):
    return lax.dot_general(a, b, (((ca,), (cb,)), ((), ())), preferred_element_type=F32)


def swap(block, bit):
    count = lax.axis_size("seg")
    return lax.ppermute(block, "seg", [(i, i ^ (1 << bit)) for i in range(count)])


def head_swap(block):
    return lax.ppermute(block, "head", [(0, 1), (1, 0)])


def head_sum(part):
    if lax.axis_size("head") == 2:
        return part.astype(F32) + head_swap(part).astype(F32)
    return lax.psum(part, "head").astype(F32)


def head_join(mine, axis):
    got = head_swap(mine)
    first = lax.axis_index("head") == 0
    return jnp.concatenate(
        [jnp.where(first, mine, got), jnp.where(first, got, mine)], axis=axis
    )


def rope_tables(length):
    half_dim = HEAD_DIM // 2
    position = jnp.arange(length, dtype=F32)[:, None]
    frequency = THETA ** (-jnp.arange(half_dim, dtype=F32) / half_dim)
    angles = position * frequency[None, :]
    cosine, sine = jnp.cos(angles), jnp.sin(angles)
    return (
        jnp.concatenate([cosine, cosine], axis=1),
        jnp.concatenate([-sine, sine], axis=1),
    )


def rms_scale(token_rows):
    return lax.rsqrt(jnp.mean(token_rows * token_rows, axis=-1, keepdims=True) + EPS)


def norm_backward(grad_normed, token_rows, row_scale, gain_vec):
    weighted = grad_normed * gain_vec
    inner_mean = jnp.mean(weighted * token_rows, axis=-1, keepdims=True)
    grad_rows = row_scale * weighted - token_rows * row_scale**3 * inner_mean
    grad_gain = jnp.sum(grad_normed * token_rows * row_scale, axis=0)
    return (grad_rows, grad_gain)


def rank_body(picks_ref, out_ref):
    rows, cache_len = picks_ref.shape
    at_row = lax.broadcasted_iota(jnp.int32, (128, 256), 0)
    at_col = lax.broadcasted_iota(jnp.int32, (128, 256), 1)
    table = jnp.where((at_row <= at_col) | (at_col >= 128), 1.0, 0.0).astype(BF)
    carry = jnp.zeros((rows, 128), F32)
    for chunk in range(cache_len // 128):
        cols = slice(chunk * 128, (chunk + 1) * 128)
        picked = picks_ref[:, cols].astype(F32)
        sums = dot(picked.astype(BF), table, 1, 0)
        out_ref[:, cols] = ((sums[:, :128] + carry) * picked).astype(BF)
        carry = carry + sums[:, 128:]


def rank_picks(picks):
    rows, cache_len = picks.shape
    return pl.pallas_call(
        rank_body,
        out_shape=jax.ShapeDtypeStruct((rows, cache_len), BF),
        name="rank_picks",
    )(picks)


def gather_body(*refs):
    asks = (len(refs) - 3) // 2
    keys_ref, values_ref = refs[asks], refs[asks + 1]
    out_refs = refs[asks + 2 : -1]
    table_ref = refs[-1]
    table_ref[:, :HEAD_DIM] = keys_ref[...]
    table_ref[:, HEAD_DIM:] = values_ref[...]
    blocks, mem_len = refs[0].shape[1], refs[0].shape[2]
    slot = lax.broadcasted_iota(jnp.int32, (KPICK, mem_len), 0).astype(F32) + 1.0
    for ask_ref, out_ref in zip(refs[:asks], out_refs):
        ranks = ask_ref[0].astype(F32)
        wanted = jnp.max(ranks) > 0.0

        @pl.when(wanted)
        def _():
            chosen = jnp.concatenate(
                [
                    jnp.where(ranks[block : block + 1] == slot, 1.0, 0.0).astype(BF)
                    for block in range(blocks)
                ],
                axis=0,
            )
            out_ref[0] = dot(chosen, table_ref[...], 1, 0).astype(BF)

        @pl.when(jnp.logical_not(wanted))
        def _():
            out_ref[0] = jnp.zeros(out_ref.shape[1:], BF)


def gather_rows(asked, cache_keys, cache_values):
    heads, blocks, mem_len = asked[0].shape
    return pl.pallas_call(
        gather_body,
        grid=(heads,),
        in_specs=[pl.BlockSpec((1, blocks, mem_len), lambda h: (h, 0, 0))] * len(asked)
        + [pl.BlockSpec((mem_len, HEAD_DIM), lambda h: (0, h))] * 2,
        out_specs=[pl.BlockSpec((1, blocks * KPICK, 2 * HEAD_DIM), lambda h: (h, 0, 0))]
        * len(asked),
        out_shape=[jax.ShapeDtypeStruct((heads, blocks * KPICK, 2 * HEAD_DIM), BF)] * len(asked),
        scratch_shapes=[pltpu.VMEM((mem_len, 2 * HEAD_DIM), BF)],
        name="gather_rows",
    )(*asked, cache_keys, cache_values)


def turn(part, cosine, sine):
    return part * cosine + pltpu.roll(part, HEAD_DIM // 2, 1) * sine


def turn_back(part, cosine, sine):
    return part * cosine - pltpu.roll(part, HEAD_DIM // 2, 1) * sine


def project_body(
    tokens_ref, gain_ref, wq_ref, wk_ref, wv_ref, cos_ref, sin_ref, q_ref, k_ref, v_ref, n_ref
):
    length = tokens_ref.shape[0]
    width = wq_ref.shape[1]
    tile = min(SUB, length)

    @pl.when(pl.program_id(0) == 0)
    def _():
        for start in range(0, length, tile):
            rows = slice(start, start + tile)
            x = tokens_ref[rows].astype(F32)
            scale = lax.rsqrt(jnp.mean(x * x, axis=-1, keepdims=True) + EPS)
            n_ref[rows] = (x * scale * gain_ref[...]).astype(BF)

    for start in range(0, length, tile):
        rows = slice(start, start + tile)
        x = n_ref[rows]
        cosine, sine = cos_ref[rows], sin_ref[rows]
        for w_ref, o_ref in ((wq_ref, q_ref), (wk_ref, k_ref)):
            full = dot(x, w_ref[...], 1, 0)
            for at in range(0, width, HEAD_DIM):
                cols = slice(at, at + HEAD_DIM)
                o_ref[rows, cols] = turn(full[:, cols], cosine, sine).astype(BF)
        v_ref[rows] = dot(x, wv_ref[...], 1, 0).astype(BF)


def project(tokens, gain, wq, wk, wv, cosine, sine):
    length, dim = tokens.shape
    cols = wq.shape[1]
    width = 2 * HEAD_DIM if cols % (2 * HEAD_DIM) == 0 else HEAD_DIM
    whole = lambda shape: pl.BlockSpec(shape, lambda g: (0, 0))
    return pl.pallas_call(
        project_body,
        grid=(cols // width,),
        in_specs=[whole((length, dim)), whole((1, dim))]
        + [pl.BlockSpec((dim, width), lambda g: (0, g))] * 3
        + [whole((length, HEAD_DIM))] * 2,
        out_specs=[pl.BlockSpec((length, width), lambda g: (0, g))] * 3 + [whole((length, dim))],
        out_shape=[jax.ShapeDtypeStruct((length, cols), BF)] * 3
        + [jax.ShapeDtypeStruct((length, dim), BF)],
        name="project",
    )(tokens, gain, wq, wk, wv, cosine, sine)


def window(start, size):
    return max(0, start - DOC_MOST), start + size


def make_bias(bias_ref, index, doc_row_ref, doc_col_ref, row0, start, size):
    low, high = window(row0 + start, size)
    at_query = lax.broadcasted_iota(jnp.int32, (size, high - low), 0) + (row0 + start)
    at_key = lax.broadcasted_iota(jnp.int32, (size, high - low), 1) + low
    same = doc_row_ref[:, low:high] == doc_col_ref[start : start + size]
    bias_ref[index, :, : high - low] = jnp.where(same & (at_key <= at_query), 0.0, NEG)


def forward_body(row0, far_count, *refs):
    q_ref, k_ref, v_ref, doc_row_ref, doc_col_ref = refs[:5]
    far_refs = refs[5 : 5 + far_count]
    outs = refs[5 + far_count :]
    o_ref, lse_ref = outs[:2]
    far_ref = outs[2] if far_count else None
    bias_ref = outs[-1]
    count = q_ref.shape[0]
    size = min(SUB, count)
    scale = 1.0 / math.sqrt(HEAD_DIM)

    @pl.when(pl.program_id(0) == 0)
    def _():
        for index, start in enumerate(range(0, count, size)):
            make_bias(bias_ref, index, doc_row_ref, doc_col_ref, row0, start, size)

    if far_count:
        total = far_refs[0][0]
        for other in far_refs[1:]:
            total = total + other[0]
        far_ref[0] = total
    for index, start in enumerate(range(0, count, size)):
        low, high = window(row0 + start, size)
        rows = slice(start, start + size)
        q = q_ref[rows]
        s = dot(q, k_ref[low:high], 1, 1) * scale + bias_ref[index, :, : high - low]
        m = jnp.max(s, axis=1, keepdims=True)
        if far_count:
            far_bias = jnp.where(doc_col_ref[rows] == doc_row_ref[:, 0:1], 0.0, NEG)
            sf = jnp.concatenate(
                [
                    dot(
                        q[at : at + PICK_BLOCK],
                        far_ref[0, start + at : start + at + PICK_BLOCK, :HEAD_DIM],
                        1,
                        1,
                    )
                    for at in range(0, size, PICK_BLOCK)
                ],
                axis=0,
            )
            sf = sf * scale + far_bias
            m = jnp.maximum(m, jnp.max(sf, axis=1, keepdims=True))
        p = jnp.exp(s - m)
        total = jnp.sum(p, axis=1, keepdims=True)
        o = dot(p.astype(BF), v_ref[low:high], 1, 0)
        if far_count:
            pf = jnp.exp(sf - m)
            total = total + jnp.sum(pf, axis=1, keepdims=True)
            pf = pf.astype(BF)
            o = o + jnp.concatenate(
                [
                    dot(
                        pf[at : at + PICK_BLOCK],
                        far_ref[0, start + at : start + at + PICK_BLOCK, HEAD_DIM:],
                        1,
                        0,
                    )
                    for at in range(0, size, PICK_BLOCK)
                ],
                axis=0,
            )
        o_ref[rows] = (o / total).astype(BF)
        lse_ref[0, rows] = m + jnp.log(total)


def attend_forward(q, k, v, doc_row, doc_col, row0, count, far):
    heads = q.shape[1] // HEAD_DIM
    seg_len = q.shape[0]
    high = row0 + count
    at = row0 // count
    size = min(SUB, count)
    wide = max(w[1] - w[0] for w in (window(row0 + s, size) for s in range(0, count, size)))
    key_spec = pl.BlockSpec((high, HEAD_DIM), lambda h: (0, h))
    far_spec = pl.BlockSpec((1, count, 2 * HEAD_DIM), lambda h: (h, 0, 0))
    far_shape = jax.ShapeDtypeStruct((heads, count, 2 * HEAD_DIM), BF)
    return pl.pallas_call(
        functools.partial(forward_body, row0, len(far)),
        grid=(heads,),
        in_specs=[
            pl.BlockSpec((count, HEAD_DIM), lambda h: (at, h)),
            key_spec,
            key_spec,
            pl.BlockSpec((1, seg_len), lambda h: (0, 0)),
            pl.BlockSpec((count, 1), lambda h: (at, 0)),
        ]
        + [far_spec] * len(far),
        out_specs=[
            pl.BlockSpec((count, HEAD_DIM), lambda h: (0, h)),
            pl.BlockSpec((1, count, 1), lambda h: (h, 0, 0)),
        ]
        + [far_spec] * bool(far),
        out_shape=[
            jax.ShapeDtypeStruct((count, heads * HEAD_DIM), BF),
            jax.ShapeDtypeStruct((heads, count, 1), F32),
        ]
        + [far_shape] * bool(far),
        scratch_shapes=[pltpu.VMEM((count // size, size, wide), F32)],
        name="attend_forward",
    )(q, k, v, doc_row, doc_col, *far)


def backward_body(row0, far_on, *refs):
    (
        q_ref,
        k_ref,
        v_ref,
        doc_row_ref,
        doc_col_ref,
        o_ref,
        do_ref,
        lse_ref,
        cos_ref,
        sin_ref,
    ) = refs[:10]
    rest = list(refs[10:])
    if far_on:
        far_ref = rest.pop(0)
    if row0 == 0:
        add_k_ref, add_v_ref = rest.pop(0), rest.pop(0)
    dq_ref, dk_ref, dv_ref = rest[:3]
    if row0:
        low_k_ref, low_v_ref = rest[3:5]
    bias_ref, acc_k_ref, acc_v_ref = rest[-3:]
    count = q_ref.shape[0]
    size = min(SUB, count)
    scale = 1.0 / math.sqrt(HEAD_DIM)

    @pl.when(pl.program_id(0) == 0)
    def _():
        for index, start in enumerate(range(0, count, size)):
            make_bias(bias_ref, index, doc_row_ref, doc_col_ref, row0, start, size)

    if row0:
        acc_k_ref[...] = jnp.zeros(acc_k_ref.shape, F32)
        acc_v_ref[...] = jnp.zeros(acc_v_ref.shape, F32)
    else:
        acc_k_ref[...] = add_k_ref[...]
        acc_v_ref[...] = add_v_ref[...]
    for index, start in enumerate(range(0, count, size)):
        low, high = window(row0 + start, size)
        rows = slice(start, start + size)
        q, do, lse = q_ref[rows], do_ref[rows], lse_ref[0, rows]
        delta = jnp.sum(do.astype(F32) * o_ref[rows].astype(F32), axis=1, keepdims=True)
        keys, values = k_ref[low:high], v_ref[low:high]
        p = jnp.exp(dot(q, keys, 1, 1) * scale + bias_ref[index, :, : high - low] - lse)
        ds = (p * (dot(do, values, 1, 1) - delta)).astype(BF)
        acc_v_ref[low:high] += dot(p.astype(BF), do, 0, 0)
        acc_k_ref[low:high] += dot(ds, q, 0, 0)
        dq = dot(ds, keys, 1, 0)
        if far_on:
            far_bias = jnp.where(doc_col_ref[rows] == doc_row_ref[:, 0:1], 0.0, NEG) - lse
            parts = []
            for at in range(0, size, PICK_BLOCK):
                cut = slice(at, at + PICK_BLOCK)
                far_keys = far_ref[0, start + at : start + at + PICK_BLOCK, :HEAD_DIM]
                far_values = far_ref[0, start + at : start + at + PICK_BLOCK, HEAD_DIM:]
                pf = jnp.exp(dot(q[cut], far_keys, 1, 1) * scale + far_bias[cut])
                dsf = (pf * (dot(do[cut], far_values, 1, 1) - delta[cut])).astype(BF)
                parts.append(dot(dsf, far_keys, 1, 0))
            dq = dq + jnp.concatenate(parts, axis=0)
        at_rows = slice(row0 + start, row0 + start + size)
        dq_ref[rows] = turn_back(dq * scale, cos_ref[at_rows], sin_ref[at_rows]).astype(BF)
    dv_ref[...] = acc_v_ref[row0 : row0 + count].astype(BF)
    dk_ref[...] = turn_back(
        acc_k_ref[row0 : row0 + count] * scale,
        cos_ref[row0 : row0 + count],
        sin_ref[row0 : row0 + count],
    ).astype(BF)
    if row0:
        low_k_ref[...] = acc_k_ref[:row0]
        low_v_ref[...] = acc_v_ref[:row0]


def attend_backward(
    q, k, v, doc_row, doc_col, out, grad_out, lse, cosine, sine, row0, count, far, low
):
    heads = q.shape[1] // HEAD_DIM
    seg_len = q.shape[0]
    high = row0 + count
    at = row0 // count
    size = min(SUB, count)
    wide = max(w[1] - w[0] for w in (window(row0 + s, size) for s in range(0, count, size)))
    head_cols = lambda n: pl.BlockSpec((n, HEAD_DIM), lambda h: (0, h))
    whole = lambda n, m: pl.BlockSpec((n, m), lambda h: (0, 0))
    in_specs = [
        pl.BlockSpec((count, HEAD_DIM), lambda h: (at, h)),
        head_cols(high),
        head_cols(high),
        whole(1, seg_len),
        pl.BlockSpec((count, 1), lambda h: (at, 0)),
        head_cols(count),
        head_cols(count),
        pl.BlockSpec((1, count, 1), lambda h: (h, 0, 0)),
        whole(high, HEAD_DIM),
        whole(high, HEAD_DIM),
    ]
    args = [q, k, v, doc_row, doc_col, out, grad_out, lse, cosine, sine]
    if far is not None:
        in_specs.append(pl.BlockSpec((1, count, 2 * HEAD_DIM), lambda h: (h, 0, 0)))
        args.append(far)
    if row0 == 0:
        in_specs += [head_cols(count)] * 2
        args += list(low)
    out_specs = [head_cols(count)] * 3
    out_shape = [jax.ShapeDtypeStruct((count, heads * HEAD_DIM), BF)] * 3
    if row0:
        out_specs += [head_cols(row0)] * 2
        out_shape += [jax.ShapeDtypeStruct((row0, heads * HEAD_DIM), F32)] * 2
    return pl.pallas_call(
        functools.partial(backward_body, row0, far is not None),
        grid=(heads,),
        in_specs=in_specs,
        out_specs=out_specs,
        out_shape=out_shape,
        scratch_shapes=[
            pltpu.VMEM((count // size, size, wide), F32),
            pltpu.VMEM((high, HEAD_DIM), F32),
            pltpu.VMEM((high, HEAD_DIM), F32),
        ],
        name="attend_backward",
    )(*args)


def seg_sum(arrays):
    return [lax.psum(a.astype(BF), "seg").astype(F32) for a in arrays]


def butterfly(vec):
    for bit in range(lax.axis_size("seg").bit_length() - 1):
        vec = vec + swap(vec, bit)
    return vec


def shards(
    tokens,
    document_ids,
    memory_picks,
    partner_ids,
    memory_keys,
    memory_values,
    first_gain,
    query_weight,
    key_weight,
    value_weight,
    out_weight,
    second_gain,
    gate_weight,
    up_weight,
    down_weight,
    cotangent,
):
    seg_len = document_ids.shape[1]
    heads = query_weight.shape[1] // HEAD_DIM
    mem_len = memory_keys.shape[1]
    blocks = memory_picks.shape[2]
    near = min(blocks, DOC_MOST // PICK_BLOCK)
    chunk = near * PICK_BLOCK
    me = lax.axis_index("seg")
    bits = lax.axis_size("seg").bit_length() - 1
    partner = partner_ids[0]
    paired = lax.axis_size("head") == 2

    ranks = rank_picks(memory_picks.reshape(heads * blocks, 2 * mem_len))
    ranks = ranks.reshape(heads, blocks, 2 * mem_len)[:, :near]
    first_len = jnp.sum((document_ids[0] == document_ids[0, 0]).astype(jnp.int32))
    used = (jnp.arange(near) * PICK_BLOCK < first_len)[None, :, None]
    ranks = jnp.where(used, ranks, 0)
    own_ranks, far_ranks = ranks[:, :, :mem_len], ranks[:, :, mem_len:]
    asked = [own_ranks]
    for bit in range(bits):
        wanted = partner == jnp.bitwise_xor(me, 1 << bit)
        asked.append(swap(jnp.where(wanted, far_ranks, jnp.zeros_like(far_ranks)), bit))

    cosine, sine = rope_tables(seg_len)
    doc_row = document_ids
    doc_col = document_ids.reshape(seg_len, 1)
    q, k, v, normed_one = project(
        tokens, first_gain.reshape(1, -1), query_weight, key_weight, value_weight, cosine, sine
    )
    if paired:
        out_full = head_join(out_weight, 0)

    rows = gather_rows(asked, memory_keys[0], memory_values[0])
    far = [rows[0]] + [swap(rows[1 + bit], bit) for bit in range(bits)]

    starts = list(range(0, seg_len, chunk))[::-1]
    state = {}
    for row0 in starts:
        part = attend_forward(
            q, k, v, doc_row, doc_col, row0, chunk, far if row0 == 0 else []
        )
        state[row0] = {"att": part[0], "lse": part[1], "far": part[2] if row0 == 0 else None}

    for row0 in starts:
        st = state[row0]
        cut = slice(row0, row0 + chunk)
        inputs = tokens[cut].astype(F32)
        if paired:
            mixed = jnp.dot(head_join(st["att"], 1), out_full, preferred_element_type=F32)
        else:
            part = jnp.dot(st["att"], out_weight, preferred_element_type=F32)
            mixed = head_sum(part.astype(BF))
        hidden_in = inputs + mixed
        second_scale = rms_scale(hidden_in)
        normed_two = (hidden_in * second_scale * second_gain).astype(BF)
        gate = jnp.dot(normed_two, gate_weight, preferred_element_type=F32)
        upper = jnp.dot(normed_two, up_weight, preferred_element_type=F32)
        sigmoid_gate = jax.nn.sigmoid(gate)
        cot = cotangent[cut]
        grad_hidden = dot(cot, down_weight, 1, 1)
        hidden = (gate * sigmoid_gate * upper).astype(BF)
        grad_gate = (
            grad_hidden * upper * sigmoid_gate * (1.0 + gate * (1.0 - sigmoid_gate))
        ).astype(BF)
        grad_upper = (grad_hidden * gate * sigmoid_gate).astype(BF)
        part = dot(grad_gate, gate_weight, 1, 1) + dot(grad_upper, up_weight, 1, 1)
        grad_normed_two = head_sum(part.astype(BF))
        down_part = jnp.dot(hidden, down_weight, preferred_element_type=F32)
        st["output"] = (hidden_in + head_sum(down_part.astype(BF))).astype(BF)
        st["down_grad"] = dot(hidden, cot, 0, 0)
        st["gate_grad"] = dot(normed_two, grad_gate, 0, 0)
        st["up_grad"] = dot(normed_two, grad_upper, 0, 0)
        grad_rows, st["second_gain_grad"] = norm_backward(
            grad_normed_two, hidden_in, second_scale, second_gain
        )
        st["total_grad"] = cot.astype(F32) + grad_rows

    ffn = seg_sum(
        [sum(state[r][name] for r in starts) for name in ("gate_grad", "up_grad", "down_grad")]
    )

    low = None
    for row0 in starts:
        st = state[row0]
        grad_mixed = st["total_grad"].astype(BF)
        st["out_grad"] = dot(st["att"], grad_mixed, 0, 0)
        grad_att = dot(grad_mixed, out_weight, 1, 1).astype(BF)
        parts = attend_backward(
            q, k, v, doc_row, doc_col, st["att"], grad_att, st["lse"], cosine, sine,
            row0, chunk, st["far"], low,
        )
        st["dq"], st["dk"], st["dv"] = parts[:3]
        low = parts[3:]
        cut = slice(row0, row0 + chunk)
        n_cut = normed_one[cut]
        st["query_grad"] = dot(n_cut, st["dq"], 0, 0)
        st["key_grad"] = dot(n_cut, st["dk"], 0, 0)
        st["value_grad"] = dot(n_cut, st["dv"], 0, 0)
        part = (
            dot(st["dq"], query_weight, 1, 1)
            + dot(st["dk"], key_weight, 1, 1)
            + dot(st["dv"], value_weight, 1, 1)
        )
        grad_normed_one = head_sum(part.astype(BF))
        inputs = tokens[cut].astype(F32)
        grad_input, st["first_gain_grad"] = norm_backward(
            grad_normed_one, inputs, rms_scale(inputs), first_gain
        )
        st["tokens_grad"] = (st["total_grad"] + grad_input).astype(BF)

    att = seg_sum(
        [
            sum(state[r][name] for r in starts)
            for name in ("query_grad", "key_grad", "value_grad", "out_grad")
        ]
    )
    gains = butterfly(
        jnp.stack(
            [sum(state[r][n] for r in starts) for n in ("first_gain_grad", "second_gain_grad")]
        )
    )
    order = sorted(starts)
    return (
        jnp.concatenate([state[r]["output"] for r in order]),
        jnp.concatenate([state[r]["tokens_grad"] for r in order]),
        gains[0],
        att[0],
        att[1],
        att[2],
        att[3],
        gains[1],
        ffn[0],
        ffn[1],
        ffn[2],
    )


def solution(mesh):
    placed = (
        P("seg", None),
        P("seg", None),
        P("seg", "head", None, None),
        P("seg"),
        P("seg", None, "head"),
        P("seg", None, "head"),
        P(),
        P(None, "head"),
        P(None, "head"),
        P(None, "head"),
        P("head", None),
        P(),
        P(None, "head"),
        P(None, "head"),
        P("head", None),
        P("seg", None),
    )
    return jax.shard_map(
        shards,
        mesh=mesh,
        in_specs=placed,
        out_specs=(
            P("seg", None),
            P("seg", None),
            P(),
            P(None, "head"),
            P(None, "head"),
            P(None, "head"),
            P("head", None),
            P(),
            P(None, "head"),
            P(None, "head"),
            P("head", None),
        ),
        check_vma=False,
    )
```

```python
import functools
import math

import jax
import jax.numpy as jnp
from jax import lax
from jax.experimental import pallas as pl
from jax.experimental.pallas import tpu as pltpu
from jax.sharding import PartitionSpec as P

HEAD_DIM = 128
KPICK = 128
PICK_BLOCK = 128
DOC_MOST = 512
SUB = 256

EPS = 1e-05
NEG = -1e30
THETA = 10000.0
BF = jnp.bfloat16
F32 = jnp.float32


def dot(a, b, ca, cb):
    return lax.dot_general(a, b, (((ca,), (cb,)), ((), ())), preferred_element_type=F32)


def swap(block, bit):
    count = lax.axis_size("seg")
    return lax.ppermute(block, "seg", [(i, i ^ (1 << bit)) for i in range(count)])


def head_swap(block):
    return lax.ppermute(block, "head", [(0, 1), (1, 0)])


def head_sum(part):
    if lax.axis_size("head") == 2:
        return part.astype(F32) + head_swap(part).astype(F32)
    return lax.psum(part, "head").astype(F32)


def head_join(mine, axis):
    got = head_swap(mine)
    first = lax.axis_index("head") == 0
    return jnp.concatenate(
        [jnp.where(first, mine, got), jnp.where(first, got, mine)], axis=axis
    )


def after(value, *done):
    return lax.optimization_barrier((value, done))[0]


def rope_tables(length):
    half_dim = HEAD_DIM // 2
    position = jnp.arange(length, dtype=F32)[:, None]
    frequency = THETA ** (-jnp.arange(half_dim, dtype=F32) / half_dim)
    angles = position * frequency[None, :]
    cosine, sine = jnp.cos(angles), jnp.sin(angles)
    return (
        jnp.concatenate([cosine, cosine], axis=1),
        jnp.concatenate([-sine, sine], axis=1),
    )


def rms_scale(token_rows):
    return lax.rsqrt(jnp.mean(token_rows * token_rows, axis=-1, keepdims=True) + EPS)


def norm_backward(grad_normed, token_rows, row_scale, gain_vec):
    weighted = grad_normed * gain_vec
    inner_mean = jnp.mean(weighted * token_rows, axis=-1, keepdims=True)
    grad_rows = row_scale * weighted - token_rows * row_scale**3 * inner_mean
    grad_gain = jnp.sum(grad_normed * token_rows * row_scale, axis=0)
    return (grad_rows, grad_gain)


def rank_body(picks_ref, out_ref):
    rows, cache_len = picks_ref.shape
    at_row = lax.broadcasted_iota(jnp.int32, (128, 256), 0)
    at_col = lax.broadcasted_iota(jnp.int32, (128, 256), 1)
    table = jnp.where((at_row <= at_col) | (at_col >= 128), 1.0, 0.0).astype(BF)
    carry = jnp.zeros((rows, 128), F32)
    for chunk in range(cache_len // 128):
        cols = slice(chunk * 128, (chunk + 1) * 128)
        picked = picks_ref[:, cols].astype(F32)
        sums = dot(picked.astype(BF), table, 1, 0)
        out_ref[:, cols] = ((sums[:, :128] + carry) * picked).astype(BF)
        carry = carry + sums[:, 128:]


def rank_picks(picks):
    rows, cache_len = picks.shape
    return pl.pallas_call(
        rank_body,
        out_shape=jax.ShapeDtypeStruct((rows, cache_len), BF),
        name="rank_picks",
    )(picks)


def gather_body(*refs):
    asks = (len(refs) - 3) // 2
    keys_ref, values_ref = refs[asks], refs[asks + 1]
    out_refs = refs[asks + 2 : -1]
    table_ref = refs[-1]
    table_ref[:, :HEAD_DIM] = keys_ref[...]
    table_ref[:, HEAD_DIM:] = values_ref[...]
    blocks, mem_len = refs[0].shape[1], refs[0].shape[2]
    slot = lax.broadcasted_iota(jnp.int32, (KPICK, mem_len), 0).astype(F32) + 1.0
    for ask_ref, out_ref in zip(refs[:asks], out_refs):
        ranks = ask_ref[0].astype(F32)
        wanted = jnp.max(ranks) > 0.0

        @pl.when(wanted)
        def _():
            chosen = jnp.concatenate(
                [
                    jnp.where(ranks[block : block + 1] == slot, 1.0, 0.0).astype(BF)
                    for block in range(blocks)
                ],
                axis=0,
            )
            out_ref[0] = dot(chosen, table_ref[...], 1, 0).astype(BF)

        @pl.when(jnp.logical_not(wanted))
        def _():
            out_ref[0] = jnp.zeros(out_ref.shape[1:], BF)


def gather_rows(asked, cache_keys, cache_values):
    heads, blocks, mem_len = asked[0].shape
    return pl.pallas_call(
        gather_body,
        grid=(heads,),
        in_specs=[pl.BlockSpec((1, blocks, mem_len), lambda h: (h, 0, 0))] * len(asked)
        + [pl.BlockSpec((mem_len, HEAD_DIM), lambda h: (0, h))] * 2,
        out_specs=[pl.BlockSpec((1, blocks * KPICK, 2 * HEAD_DIM), lambda h: (h, 0, 0))]
        * len(asked),
        out_shape=[jax.ShapeDtypeStruct((heads, blocks * KPICK, 2 * HEAD_DIM), BF)] * len(asked),
        scratch_shapes=[pltpu.VMEM((mem_len, 2 * HEAD_DIM), BF)],
        name="gather_rows",
    )(*asked, cache_keys, cache_values)


def turn(part, cosine, sine):
    return part * cosine + pltpu.roll(part, HEAD_DIM // 2, 1) * sine


def turn_back(part, cosine, sine):
    return part * cosine - pltpu.roll(part, HEAD_DIM // 2, 1) * sine


def project_body(
    tokens_ref, gain_ref, wq_ref, wk_ref, wv_ref, cos_ref, sin_ref, q_ref, k_ref, v_ref, n_ref
):
    length = tokens_ref.shape[0]
    width = wq_ref.shape[1]
    tile = min(SUB, length)

    @pl.when(pl.program_id(0) == 0)
    def _():
        for start in range(0, length, tile):
            rows = slice(start, start + tile)
            x = tokens_ref[rows].astype(F32)
            scale = lax.rsqrt(jnp.mean(x * x, axis=-1, keepdims=True) + EPS)
            n_ref[rows] = (x * scale * gain_ref[...]).astype(BF)

    for start in range(0, length, tile):
        rows = slice(start, start + tile)
        x = n_ref[rows]
        cosine, sine = cos_ref[rows], sin_ref[rows]
        for w_ref, o_ref in ((wq_ref, q_ref), (wk_ref, k_ref)):
            full = dot(x, w_ref[...], 1, 0)
            for at in range(0, width, HEAD_DIM):
                cols = slice(at, at + HEAD_DIM)
                o_ref[rows, cols] = turn(full[:, cols], cosine, sine).astype(BF)
        v_ref[rows] = dot(x, wv_ref[...], 1, 0).astype(BF)


def project(tokens, gain, wq, wk, wv, cosine, sine):
    length, dim = tokens.shape
    cols = wq.shape[1]
    width = 2 * HEAD_DIM if cols % (2 * HEAD_DIM) == 0 else HEAD_DIM
    whole = lambda shape: pl.BlockSpec(shape, lambda g: (0, 0))
    return pl.pallas_call(
        project_body,
        grid=(cols // width,),
        in_specs=[whole((length, dim)), whole((1, dim))]
        + [pl.BlockSpec((dim, width), lambda g: (0, g))] * 3
        + [whole((length, HEAD_DIM))] * 2,
        out_specs=[pl.BlockSpec((length, width), lambda g: (0, g))] * 3 + [whole((length, dim))],
        out_shape=[jax.ShapeDtypeStruct((length, cols), BF)] * 3
        + [jax.ShapeDtypeStruct((length, dim), BF)],
        name="project",
    )(tokens, gain, wq, wk, wv, cosine, sine)


def window(start, size):
    return max(0, start - DOC_MOST), start + size


def make_bias(bias_ref, index, doc_row_ref, doc_col_ref, row0, start, size):
    low, high = window(row0 + start, size)
    at_query = lax.broadcasted_iota(jnp.int32, (size, high - low), 0) + (row0 + start)
    at_key = lax.broadcasted_iota(jnp.int32, (size, high - low), 1) + low
    same = doc_row_ref[:, low:high] == doc_col_ref[start : start + size]
    bias_ref[index, :, : high - low] = jnp.where(same & (at_key <= at_query), 0.0, NEG)


def forward_body(row0, far_count, *refs):
    q_ref, k_ref, v_ref, doc_row_ref, doc_col_ref = refs[:5]
    far_refs = refs[5 : 5 + far_count]
    outs = refs[5 + far_count :]
    o_ref, lse_ref = outs[:2]
    far_ref = outs[2] if far_count else None
    bias_ref = outs[-1]
    count = q_ref.shape[0]
    size = min(SUB, count)
    scale = 1.0 / math.sqrt(HEAD_DIM)

    @pl.when(pl.program_id(0) == 0)
    def _():
        for index, start in enumerate(range(0, count, size)):
            make_bias(bias_ref, index, doc_row_ref, doc_col_ref, row0, start, size)

    if far_count:
        total = far_refs[0][0]
        for other in far_refs[1:]:
            total = total + other[0]
        far_ref[0] = total
    for index, start in enumerate(range(0, count, size)):
        low, high = window(row0 + start, size)
        rows = slice(start, start + size)
        q = q_ref[rows]
        s = dot(q, k_ref[low:high], 1, 1) * scale + bias_ref[index, :, : high - low]
        m = jnp.max(s, axis=1, keepdims=True)
        if far_count:
            far_bias = jnp.where(doc_col_ref[rows] == doc_row_ref[:, 0:1], 0.0, NEG)
            sf = jnp.concatenate(
                [
                    dot(
                        q[at : at + PICK_BLOCK],
                        far_ref[0, start + at : start + at + PICK_BLOCK, :HEAD_DIM],
                        1,
                        1,
                    )
                    for at in range(0, size, PICK_BLOCK)
                ],
                axis=0,
            )
            sf = sf * scale + far_bias
            m = jnp.maximum(m, jnp.max(sf, axis=1, keepdims=True))
        p = jnp.exp(s - m)
        total = jnp.sum(p, axis=1, keepdims=True)
        o = dot(p.astype(BF), v_ref[low:high], 1, 0)
        if far_count:
            pf = jnp.exp(sf - m)
            total = total + jnp.sum(pf, axis=1, keepdims=True)
            pf = pf.astype(BF)
            o = o + jnp.concatenate(
                [
                    dot(
                        pf[at : at + PICK_BLOCK],
                        far_ref[0, start + at : start + at + PICK_BLOCK, HEAD_DIM:],
                        1,
                        0,
                    )
                    for at in range(0, size, PICK_BLOCK)
                ],
                axis=0,
            )
        o_ref[rows] = (o / total).astype(BF)
        lse_ref[0, rows] = m + jnp.log(total)


def attend_forward(q, k, v, doc_row, doc_col, row0, count, far):
    heads = q.shape[1] // HEAD_DIM
    seg_len = q.shape[0]
    high = row0 + count
    at = row0 // count
    size = min(SUB, count)
    wide = max(w[1] - w[0] for w in (window(row0 + s, size) for s in range(0, count, size)))
    key_spec = pl.BlockSpec((high, HEAD_DIM), lambda h: (0, h))
    far_spec = pl.BlockSpec((1, count, 2 * HEAD_DIM), lambda h: (h, 0, 0))
    far_shape = jax.ShapeDtypeStruct((heads, count, 2 * HEAD_DIM), BF)
    return pl.pallas_call(
        functools.partial(forward_body, row0, len(far)),
        grid=(heads,),
        in_specs=[
            pl.BlockSpec((count, HEAD_DIM), lambda h: (at, h)),
            key_spec,
            key_spec,
            pl.BlockSpec((1, seg_len), lambda h: (0, 0)),
            pl.BlockSpec((count, 1), lambda h: (at, 0)),
        ]
        + [far_spec] * len(far),
        out_specs=[
            pl.BlockSpec((count, HEAD_DIM), lambda h: (0, h)),
            pl.BlockSpec((1, count, 1), lambda h: (h, 0, 0)),
        ]
        + [far_spec] * bool(far),
        out_shape=[
            jax.ShapeDtypeStruct((count, heads * HEAD_DIM), BF),
            jax.ShapeDtypeStruct((heads, count, 1), F32),
        ]
        + [far_shape] * bool(far),
        scratch_shapes=[pltpu.VMEM((count // size, size, wide), F32)],
        name="attend_forward",
    )(q, k, v, doc_row, doc_col, *far)


def backward_body(row0, far_on, *refs):
    (
        q_ref,
        k_ref,
        v_ref,
        doc_row_ref,
        doc_col_ref,
        o_ref,
        do_ref,
        lse_ref,
        cos_ref,
        sin_ref,
    ) = refs[:10]
    rest = list(refs[10:])
    if far_on:
        far_ref = rest.pop(0)
    if row0 == 0:
        add_k_ref, add_v_ref = rest.pop(0), rest.pop(0)
    grad_ref = rest[0]
    dq_ref, dk_ref, dv_ref = (
        grad_ref.at[:, at : at + HEAD_DIM] for at in range(0, 3 * HEAD_DIM, HEAD_DIM)
    )
    if row0:
        low_k_ref, low_v_ref = rest[1:3]
    bias_ref, acc_k_ref, acc_v_ref = rest[-3:]
    count = q_ref.shape[0]
    size = min(SUB, count)
    scale = 1.0 / math.sqrt(HEAD_DIM)

    @pl.when(pl.program_id(0) == 0)
    def _():
        for index, start in enumerate(range(0, count, size)):
            make_bias(bias_ref, index, doc_row_ref, doc_col_ref, row0, start, size)

    if row0:
        acc_k_ref[...] = jnp.zeros(acc_k_ref.shape, F32)
        acc_v_ref[...] = jnp.zeros(acc_v_ref.shape, F32)
    else:
        acc_k_ref[...] = add_k_ref[...]
        acc_v_ref[...] = add_v_ref[...]
    for index, start in enumerate(range(0, count, size)):
        low, high = window(row0 + start, size)
        rows = slice(start, start + size)
        q, do, lse = q_ref[rows], do_ref[rows], lse_ref[0, rows]
        delta = jnp.sum(do.astype(F32) * o_ref[rows].astype(F32), axis=1, keepdims=True)
        keys, values = k_ref[low:high], v_ref[low:high]
        p = jnp.exp(dot(q, keys, 1, 1) * scale + bias_ref[index, :, : high - low] - lse)
        ds = (p * (dot(do, values, 1, 1) - delta)).astype(BF)
        acc_v_ref[low:high] += dot(p.astype(BF), do, 0, 0)
        acc_k_ref[low:high] += dot(ds, q, 0, 0)
        dq = dot(ds, keys, 1, 0)
        if far_on:
            far_bias = jnp.where(doc_col_ref[rows] == doc_row_ref[:, 0:1], 0.0, NEG) - lse
            parts = []
            for at in range(0, size, PICK_BLOCK):
                cut = slice(at, at + PICK_BLOCK)
                far_keys = far_ref[0, start + at : start + at + PICK_BLOCK, :HEAD_DIM]
                far_values = far_ref[0, start + at : start + at + PICK_BLOCK, HEAD_DIM:]
                pf = jnp.exp(dot(q[cut], far_keys, 1, 1) * scale + far_bias[cut])
                dsf = (pf * (dot(do[cut], far_values, 1, 1) - delta[cut])).astype(BF)
                parts.append(dot(dsf, far_keys, 1, 0))
            dq = dq + jnp.concatenate(parts, axis=0)
        at_rows = slice(row0 + start, row0 + start + size)
        dq_ref[rows] = turn_back(dq * scale, cos_ref[at_rows], sin_ref[at_rows]).astype(BF)
    dv_ref[...] = acc_v_ref[row0 : row0 + count].astype(BF)
    dk_ref[...] = turn_back(
        acc_k_ref[row0 : row0 + count] * scale,
        cos_ref[row0 : row0 + count],
        sin_ref[row0 : row0 + count],
    ).astype(BF)
    if row0:
        low_k_ref[...] = acc_k_ref[:row0]
        low_v_ref[...] = acc_v_ref[:row0]


def attend_backward(
    q, k, v, doc_row, doc_col, out, grad_out, lse, cosine, sine, row0, count, far, low
):
    heads = q.shape[1] // HEAD_DIM
    seg_len = q.shape[0]
    high = row0 + count
    at = row0 // count
    size = min(SUB, count)
    wide = max(w[1] - w[0] for w in (window(row0 + s, size) for s in range(0, count, size)))
    head_cols = lambda n: pl.BlockSpec((n, HEAD_DIM), lambda h: (0, h))
    whole = lambda n, m: pl.BlockSpec((n, m), lambda h: (0, 0))
    in_specs = [
        pl.BlockSpec((count, HEAD_DIM), lambda h: (at, h)),
        head_cols(high),
        head_cols(high),
        whole(1, seg_len),
        pl.BlockSpec((count, 1), lambda h: (at, 0)),
        head_cols(count),
        head_cols(count),
        pl.BlockSpec((1, count, 1), lambda h: (h, 0, 0)),
        whole(high, HEAD_DIM),
        whole(high, HEAD_DIM),
    ]
    args = [q, k, v, doc_row, doc_col, out, grad_out, lse, cosine, sine]
    if far is not None:
        in_specs.append(pl.BlockSpec((1, count, 2 * HEAD_DIM), lambda h: (h, 0, 0)))
        args.append(far)
    if row0 == 0:
        in_specs += [head_cols(count)] * 2
        args += list(low)
    out_specs = [pl.BlockSpec((count, 3 * HEAD_DIM), lambda h: (0, h))]
    out_shape = [jax.ShapeDtypeStruct((count, 3 * heads * HEAD_DIM), BF)]
    if row0:
        out_specs += [head_cols(row0)] * 2
        out_shape += [jax.ShapeDtypeStruct((row0, heads * HEAD_DIM), F32)] * 2
    return pl.pallas_call(
        functools.partial(backward_body, row0, far is not None),
        grid=(heads,),
        in_specs=in_specs,
        out_specs=out_specs,
        out_shape=out_shape,
        scratch_shapes=[
            pltpu.VMEM((count // size, size, wide), F32),
            pltpu.VMEM((high, HEAD_DIM), F32),
            pltpu.VMEM((high, HEAD_DIM), F32),
        ],
        name="attend_backward",
    )(*args)


def halve(part, bit):
    size = part.shape[0] // 2
    mine = (lax.axis_index("seg") >> bit) & 1
    keep = lax.dynamic_slice_in_dim(part, mine * size, size)
    send = lax.dynamic_slice_in_dim(part, (1 - mine) * size, size)
    return (keep.astype(F32) + swap(send, bit).astype(F32)).astype(BF)


def double(part, bit):
    mine = (lax.axis_index("seg") >> bit) & 1
    got = swap(part, bit)
    return jnp.concatenate([jnp.where(mine == 0, part, got), jnp.where(mine == 0, got, part)])


def seg_sum(part, order):
    part = part.astype(BF)
    for bit in order:
        part = halve(part, bit)
    for bit in order[::-1]:
        part = double(part, bit)
    return part


def butterfly(vec):
    for bit in range(lax.axis_size("seg").bit_length() - 1):
        vec = vec + swap(vec, bit)
    return vec


def shards(
    tokens,
    document_ids,
    memory_picks,
    partner_ids,
    memory_keys,
    memory_values,
    first_gain,
    query_weight,
    key_weight,
    value_weight,
    out_weight,
    second_gain,
    gate_weight,
    up_weight,
    down_weight,
    cotangent,
):
    seg_len = document_ids.shape[1]
    heads = query_weight.shape[1] // HEAD_DIM
    mem_len = memory_keys.shape[1]
    blocks = memory_picks.shape[2]
    near = min(blocks, DOC_MOST // PICK_BLOCK)
    chunk = near * PICK_BLOCK
    me = lax.axis_index("seg")
    bits = lax.axis_size("seg").bit_length() - 1
    partner = partner_ids[0]
    paired = lax.axis_size("head") == 2

    ranks = rank_picks(memory_picks.reshape(heads * blocks, 2 * mem_len))
    ranks = ranks.reshape(heads, blocks, 2 * mem_len)[:, :near]
    first_len = jnp.sum((document_ids[0] == document_ids[0, 0]).astype(jnp.int32))
    used = (jnp.arange(near) * PICK_BLOCK < first_len)[None, :, None]
    ranks = jnp.where(used, ranks, 0)
    own_ranks, far_ranks = ranks[:, :, :mem_len], ranks[:, :, mem_len:]
    asked = [own_ranks]
    for bit in range(bits):
        wanted = partner == jnp.bitwise_xor(me, 1 << bit)
        asked.append(swap(jnp.where(wanted, far_ranks, jnp.zeros_like(far_ranks)), bit))

    cosine, sine = rope_tables(seg_len)
    doc_row = document_ids
    doc_col = document_ids.reshape(seg_len, 1)
    dim = tokens.shape[1]
    cosine, sine, doc_col = after((cosine, sine, doc_col), *asked[:1])
    q, k, v, normed_one = project(
        tokens, first_gain.reshape(1, -1), query_weight, key_weight, value_weight, cosine, sine
    )
    out_full = head_join(out_weight, 0) if paired else None
    by_head = lambda w: w.reshape(dim, heads, 1, HEAD_DIM)
    joint_weight = jnp.concatenate(
        [by_head(query_weight), by_head(key_weight), by_head(value_weight)], axis=2
    ).reshape(dim, 3 * heads * HEAD_DIM)

    rows = gather_rows(asked[:1] + after(asked[1:], q), memory_keys[0], memory_values[0])
    far = [rows[0]] + [swap(rows[1 + bit], bit) for bit in range(bits)]

    def mix(st):
        if paired:
            return jnp.dot(head_join(st["att"], 1), out_full, preferred_element_type=F32)
        return head_sum(jnp.dot(st["att"], out_weight, preferred_element_type=F32).astype(BF))

    def feed(st, cut):
        st["hidden_in"] = tokens[cut].astype(F32) + st["mixed"]
        st["scale"] = rms_scale(st["hidden_in"])
        normed_two = (st["hidden_in"] * st["scale"] * second_gain).astype(BF)
        gate = jnp.dot(normed_two, gate_weight, preferred_element_type=F32)
        upper = jnp.dot(normed_two, up_weight, preferred_element_type=F32)
        sigmoid_gate = jax.nn.sigmoid(gate)
        grad_hidden = dot(cotangent[cut], down_weight, 1, 1)
        st["hidden"] = (gate * sigmoid_gate * upper).astype(BF)
        st["grad_gate"] = (
            grad_hidden * upper * sigmoid_gate * (1.0 + gate * (1.0 - sigmoid_gate))
        ).astype(BF)
        st["grad_upper"] = (grad_hidden * gate * sigmoid_gate).astype(BF)
        st["normed_two"] = normed_two
        st["part_two"] = (
            dot(st["grad_gate"], gate_weight, 1, 1) + dot(st["grad_upper"], up_weight, 1, 1)
        ).astype(BF)

    def feed_grads(st, cut):
        return (
            dot(st["hidden"], cotangent[cut], 0, 0),
            dot(st["normed_two"], st["grad_gate"], 0, 0),
            dot(st["normed_two"], st["grad_upper"], 0, 0),
        )

    def feed_out(st):
        down_part = jnp.dot(st["hidden"], down_weight, preferred_element_type=F32)
        st["output"] = (st["hidden_in"] + head_sum(down_part.astype(BF))).astype(BF)

    def norm_two(st, cut):
        rows, st["second_gain_grad"] = norm_backward(
            st["grad_normed_two"], st["hidden_in"], st["scale"], second_gain
        )
        st["total_grad"] = cotangent[cut].astype(F32) + rows
        st["grad_mixed"] = st["total_grad"].astype(BF)
        st["grad_att"] = dot(st["grad_mixed"], out_weight, 1, 1).astype(BF)

    def back(st, row0, low):
        parts = attend_backward(
            q, k, v, doc_row, doc_col, st["att"], st["grad_att"], st["lse"], cosine, sine,
            row0, chunk, st.get("far"), low,
        )
        st["joint"] = parts[0]
        return parts[1:]

    def norm_one(st, cut):
        inputs = tokens[cut].astype(F32)
        rows, st["first_gain_grad"] = norm_backward(
            st["grad_normed_one"], inputs, rms_scale(inputs), first_gain
        )
        st["tokens_grad"] = (st["total_grad"] + rows).astype(BF)

    late, early = slice(chunk, 2 * chunk), slice(0, chunk)
    b, a = {}, {}
    b["att"], b["lse"] = attend_forward(
        after(q, rows), k, v, doc_row, doc_col, chunk, chunk, []
    )
    b["mixed"] = mix(b)
    feed(b, late)
    b["grad_normed_two"] = head_sum(b["part_two"])
    b_grads = feed_grads(b, late)
    b_grads, far = after((b_grads, far), b["part_two"])
    a["att"], a["lse"], a["far"] = attend_forward(q, k, v, doc_row, doc_col, 0, chunk, far)
    a["mixed"] = mix(a)
    b["grad_normed_two"] = after(b["grad_normed_two"], a["att"])
    norm_two(b, late)
    low = back(b, chunk, None)
    a["mixed"] = after(a["mixed"], b["joint"])
    feed(a, early)
    a["grad_normed_two"] = head_sum(a["part_two"])
    a_grads = feed_grads(a, early)
    down_grad, gate_grad, up_grad = (
        (one + two).astype(BF) for one, two in zip(b_grads, a_grads)
    )
    backwards = list(range(bits))
    z_first = [0] + backwards[2:] + [1]
    down_grad = lax.psum(down_grad, "seg").astype(F32)
    gate_grad = seg_sum(gate_grad, backwards).astype(F32)
    up_grad = seg_sum(up_grad, z_first).astype(F32)

    b["joint"] = after(b["joint"], a["part_two"])
    b["grad_normed_one"] = head_sum(dot(b["joint"], joint_weight, 1, 1).astype(BF))
    joint_grad = dot(normed_one[late], b["joint"], 0, 0)
    b["hidden"], a["hidden"] = after((b["hidden"], a["hidden"]), a["part_two"])
    feed_out(b)
    feed_out(a)
    norm_two(a, early)
    out_grad = dot(b["att"], b["grad_mixed"], 0, 0) + dot(a["att"], a["grad_mixed"], 0, 0)
    out_grad = seg_sum(out_grad, backwards).astype(F32)
    back(a, 0, low)
    joint_grad = (joint_grad + dot(normed_one[early], a["joint"], 0, 0)).astype(BF)
    half = dim // 2
    joint_grad = jnp.concatenate(
        [seg_sum(joint_grad[:half], backwards), seg_sum(joint_grad[half:], z_first)]
    )
    joint_grad = joint_grad.reshape(dim, heads, 3, HEAD_DIM).astype(F32)
    query_grad, key_grad, value_grad = (
        joint_grad[:, :, i].reshape(dim, heads * HEAD_DIM) for i in range(3)
    )
    a["grad_normed_one"] = head_sum(dot(a["joint"], joint_weight, 1, 1).astype(BF))
    norm_one(b, late)
    norm_one(a, early)
    gains = butterfly(
        jnp.stack([a[n] + b[n] for n in ("first_gain_grad", "second_gain_grad")])
    )
    return (
        jnp.concatenate([a["output"], b["output"]]),
        jnp.concatenate([a["tokens_grad"], b["tokens_grad"]]),
        gains[0],
        query_grad,
        key_grad,
        value_grad,
        out_grad,
        gains[1],
        gate_grad,
        up_grad,
        down_grad,
    )


def solution(mesh):
    placed = (
        P("seg", None),
        P("seg", None),
        P("seg", "head", None, None),
        P("seg"),
        P("seg", None, "head"),
        P("seg", None, "head"),
        P(),
        P(None, "head"),
        P(None, "head"),
        P(None, "head"),
        P("head", None),
        P(),
        P(None, "head"),
        P(None, "head"),
        P("head", None),
        P("seg", None),
    )
    return jax.shard_map(
        shards,
        mesh=mesh,
        in_specs=placed,
        out_specs=(
            P("seg", None),
            P("seg", None),
            P(),
            P(None, "head"),
            P(None, "head"),
            P(None, "head"),
            P("head", None),
            P(),
            P(None, "head"),
            P(None, "head"),
            P("head", None),
        ),
        check_vma=False,
    )
```

```python
import functools
import math

import jax
import jax.numpy as jnp
from jax import lax
from jax.experimental import pallas as pl
from jax.experimental.pallas import tpu as pltpu
from jax.sharding import PartitionSpec as P

HEAD_DIM = 128
KPICK = 128
PICK_BLOCK = 128
DOC_MOST = 512
SUB = 256

EPS = 1e-05
NEG = -1e30
THETA = 10000.0
BF = jnp.bfloat16
F32 = jnp.float32


def dot(a, b, ca, cb):
    return lax.dot_general(a, b, (((ca,), (cb,)), ((), ())), preferred_element_type=F32)


def swap(block, bit):
    count = lax.axis_size("seg")
    return lax.ppermute(block, "seg", [(i, i ^ (1 << bit)) for i in range(count)])


def head_swap(block):
    return lax.ppermute(block, "head", [(0, 1), (1, 0)])


def head_sum(part):
    if lax.axis_size("head") == 2:
        return part.astype(F32) + head_swap(part).astype(F32)
    return lax.psum(part, "head").astype(F32)


def head_join(mine, axis):
    got = head_swap(mine)
    first = lax.axis_index("head") == 0
    return jnp.concatenate(
        [jnp.where(first, mine, got), jnp.where(first, got, mine)], axis=axis
    )


def after(value, *done):
    return lax.optimization_barrier((value, done))[0]


def rope_tables(length):
    half_dim = HEAD_DIM // 2
    position = jnp.arange(length, dtype=F32)[:, None]
    frequency = THETA ** (-jnp.arange(half_dim, dtype=F32) / half_dim)
    angles = position * frequency[None, :]
    cosine, sine = jnp.cos(angles), jnp.sin(angles)
    return (
        jnp.concatenate([cosine, cosine], axis=1),
        jnp.concatenate([-sine, sine], axis=1),
    )


def rms_scale(token_rows):
    return lax.rsqrt(jnp.mean(token_rows * token_rows, axis=-1, keepdims=True) + EPS)


def norm_backward(grad_normed, token_rows, row_scale, gain_vec):
    weighted = grad_normed * gain_vec
    inner_mean = jnp.mean(weighted * token_rows, axis=-1, keepdims=True)
    grad_rows = row_scale * weighted - token_rows * row_scale**3 * inner_mean
    grad_gain = jnp.sum(grad_normed * token_rows * row_scale, axis=0)
    return (grad_rows, grad_gain)


def rank_body(picks_ref, out_ref):
    rows, cache_len = picks_ref.shape
    at_row = lax.broadcasted_iota(jnp.int32, (128, 256), 0)
    at_col = lax.broadcasted_iota(jnp.int32, (128, 256), 1)
    table = jnp.where((at_row <= at_col) | (at_col >= 128), 1.0, 0.0).astype(BF)
    carry = jnp.zeros((rows, 128), F32)
    for chunk in range(cache_len // 128):
        cols = slice(chunk * 128, (chunk + 1) * 128)
        picked = picks_ref[:, cols].astype(F32)
        sums = dot(picked.astype(BF), table, 1, 0)
        out_ref[:, cols] = ((sums[:, :128] + carry) * picked).astype(BF)
        carry = carry + sums[:, 128:]


def rank_picks(picks):
    rows, cache_len = picks.shape
    return pl.pallas_call(
        rank_body,
        out_shape=jax.ShapeDtypeStruct((rows, cache_len), BF),
        name="rank_picks",
    )(picks)


def gather_body(*refs):
    asks = (len(refs) - 3) // 2
    keys_ref, values_ref = refs[asks], refs[asks + 1]
    out_refs = refs[asks + 2 : -1]
    table_ref = refs[-1]
    table_ref[:, :HEAD_DIM] = keys_ref[...]
    table_ref[:, HEAD_DIM:] = values_ref[...]
    blocks, mem_len = refs[0].shape[1], refs[0].shape[2]
    slot = lax.broadcasted_iota(jnp.int32, (KPICK, mem_len), 0).astype(F32) + 1.0
    for ask_ref, out_ref in zip(refs[:asks], out_refs):
        ranks = ask_ref[0].astype(F32)
        wanted = jnp.max(ranks) > 0.0

        @pl.when(wanted)
        def _():
            chosen = jnp.concatenate(
                [
                    jnp.where(ranks[block : block + 1] == slot, 1.0, 0.0).astype(BF)
                    for block in range(blocks)
                ],
                axis=0,
            )
            out_ref[0] = dot(chosen, table_ref[...], 1, 0).astype(BF)

        @pl.when(jnp.logical_not(wanted))
        def _():
            out_ref[0] = jnp.zeros(out_ref.shape[1:], BF)


def gather_rows(asked, cache_keys, cache_values):
    heads, blocks, mem_len = asked[0].shape
    return pl.pallas_call(
        gather_body,
        grid=(heads,),
        in_specs=[pl.BlockSpec((1, blocks, mem_len), lambda h: (h, 0, 0))] * len(asked)
        + [pl.BlockSpec((mem_len, HEAD_DIM), lambda h: (0, h))] * 2,
        out_specs=[pl.BlockSpec((1, blocks * KPICK, 2 * HEAD_DIM), lambda h: (h, 0, 0))]
        * len(asked),
        out_shape=[jax.ShapeDtypeStruct((heads, blocks * KPICK, 2 * HEAD_DIM), BF)] * len(asked),
        scratch_shapes=[pltpu.VMEM((mem_len, 2 * HEAD_DIM), BF)],
        name="gather_rows",
    )(*asked, cache_keys, cache_values)


def turn(part, cosine, sine):
    return part * cosine + pltpu.roll(part, HEAD_DIM // 2, 1) * sine


def turn_back(part, cosine, sine):
    return part * cosine - pltpu.roll(part, HEAD_DIM // 2, 1) * sine


def project_body(
    tokens_ref, gain_ref, wq_ref, wk_ref, wv_ref, cos_ref, sin_ref, q_ref, k_ref, v_ref, n_ref
):
    length = tokens_ref.shape[0]
    width = wq_ref.shape[1]
    tile = min(SUB, length)

    @pl.when(pl.program_id(0) == 0)
    def _():
        for start in range(0, length, tile):
            rows = slice(start, start + tile)
            x = tokens_ref[rows].astype(F32)
            scale = lax.rsqrt(jnp.mean(x * x, axis=-1, keepdims=True) + EPS)
            n_ref[rows] = (x * scale * gain_ref[...]).astype(BF)

    for start in range(0, length, tile):
        rows = slice(start, start + tile)
        x = n_ref[rows]
        cosine, sine = cos_ref[rows], sin_ref[rows]
        for w_ref, o_ref in ((wq_ref, q_ref), (wk_ref, k_ref)):
            full = dot(x, w_ref[...], 1, 0)
            for at in range(0, width, HEAD_DIM):
                cols = slice(at, at + HEAD_DIM)
                o_ref[rows, cols] = turn(full[:, cols], cosine, sine).astype(BF)
        v_ref[rows] = dot(x, wv_ref[...], 1, 0).astype(BF)


def project(tokens, gain, wq, wk, wv, cosine, sine):
    length, dim = tokens.shape
    cols = wq.shape[1]
    width = 2 * HEAD_DIM if cols % (2 * HEAD_DIM) == 0 else HEAD_DIM
    whole = lambda shape: pl.BlockSpec(shape, lambda g: (0, 0))
    return pl.pallas_call(
        project_body,
        grid=(cols // width,),
        in_specs=[whole((length, dim)), whole((1, dim))]
        + [pl.BlockSpec((dim, width), lambda g: (0, g))] * 3
        + [whole((length, HEAD_DIM))] * 2,
        out_specs=[pl.BlockSpec((length, width), lambda g: (0, g))] * 3 + [whole((length, dim))],
        out_shape=[jax.ShapeDtypeStruct((length, cols), BF)] * 3
        + [jax.ShapeDtypeStruct((length, dim), BF)],
        name="project",
    )(tokens, gain, wq, wk, wv, cosine, sine)


def window(start, size):
    return max(0, start - DOC_MOST), start + size


def make_bias(bias_ref, index, doc_row_ref, doc_col_ref, row0, start, size):
    low, high = window(row0 + start, size)
    at_query = lax.broadcasted_iota(jnp.int32, (size, high - low), 0) + (row0 + start)
    at_key = lax.broadcasted_iota(jnp.int32, (size, high - low), 1) + low
    same = doc_row_ref[:, low:high] == doc_col_ref[start : start + size]
    bias_ref[index, :, : high - low] = jnp.where(same & (at_key <= at_query), 0.0, NEG)


def forward_body(row0, far_count, *refs):
    q_ref, k_ref, v_ref, doc_row_ref, doc_col_ref = refs[:5]
    far_refs = refs[5 : 5 + far_count]
    outs = refs[5 + far_count :]
    o_ref, lse_ref = outs[:2]
    far_ref = outs[2] if far_count else None
    bias_ref = outs[-1]
    count = q_ref.shape[0]
    size = min(SUB, count)
    scale = 1.0 / math.sqrt(HEAD_DIM)

    @pl.when(pl.program_id(0) == 0)
    def _():
        for index, start in enumerate(range(0, count, size)):
            make_bias(bias_ref, index, doc_row_ref, doc_col_ref, row0, start, size)

    if far_count:
        total = far_refs[0][0]
        for other in far_refs[1:]:
            total = total + other[0]
        far_ref[0] = total
    for index, start in enumerate(range(0, count, size)):
        low, high = window(row0 + start, size)
        rows = slice(start, start + size)
        q = q_ref[rows]
        s = dot(q, k_ref[low:high], 1, 1) * scale + bias_ref[index, :, : high - low]
        m = jnp.max(s, axis=1, keepdims=True)
        if far_count:
            far_bias = jnp.where(doc_col_ref[rows] == doc_row_ref[:, 0:1], 0.0, NEG)
            sf = jnp.concatenate(
                [
                    dot(
                        q[at : at + PICK_BLOCK],
                        far_ref[0, start + at : start + at + PICK_BLOCK, :HEAD_DIM],
                        1,
                        1,
                    )
                    for at in range(0, size, PICK_BLOCK)
                ],
                axis=0,
            )
            sf = sf * scale + far_bias
            m = jnp.maximum(m, jnp.max(sf, axis=1, keepdims=True))
        p = jnp.exp(s - m)
        total = jnp.sum(p, axis=1, keepdims=True)
        o = dot(p.astype(BF), v_ref[low:high], 1, 0)
        if far_count:
            pf = jnp.exp(sf - m)
            total = total + jnp.sum(pf, axis=1, keepdims=True)
            pf = pf.astype(BF)
            o = o + jnp.concatenate(
                [
                    dot(
                        pf[at : at + PICK_BLOCK],
                        far_ref[0, start + at : start + at + PICK_BLOCK, HEAD_DIM:],
                        1,
                        0,
                    )
                    for at in range(0, size, PICK_BLOCK)
                ],
                axis=0,
            )
        o_ref[rows] = (o / total).astype(BF)
        lse_ref[0, rows] = m + jnp.log(total)


def attend_forward(q, k, v, doc_row, doc_col, row0, count, far):
    heads = q.shape[1] // HEAD_DIM
    seg_len = q.shape[0]
    high = row0 + count
    at = row0 // count
    size = min(SUB, count)
    wide = max(w[1] - w[0] for w in (window(row0 + s, size) for s in range(0, count, size)))
    key_spec = pl.BlockSpec((high, HEAD_DIM), lambda h: (0, h))
    far_spec = pl.BlockSpec((1, count, 2 * HEAD_DIM), lambda h: (h, 0, 0))
    far_shape = jax.ShapeDtypeStruct((heads, count, 2 * HEAD_DIM), BF)
    return pl.pallas_call(
        functools.partial(forward_body, row0, len(far)),
        grid=(heads,),
        in_specs=[
            pl.BlockSpec((count, HEAD_DIM), lambda h: (at, h)),
            key_spec,
            key_spec,
            pl.BlockSpec((1, seg_len), lambda h: (0, 0)),
            pl.BlockSpec((count, 1), lambda h: (at, 0)),
        ]
        + [far_spec] * len(far),
        out_specs=[
            pl.BlockSpec((count, HEAD_DIM), lambda h: (0, h)),
            pl.BlockSpec((1, count, 1), lambda h: (h, 0, 0)),
        ]
        + [far_spec] * bool(far),
        out_shape=[
            jax.ShapeDtypeStruct((count, heads * HEAD_DIM), BF),
            jax.ShapeDtypeStruct((heads, count, 1), F32),
        ]
        + [far_shape] * bool(far),
        scratch_shapes=[pltpu.VMEM((count // size, size, wide), F32)],
        name="attend_forward",
    )(q, k, v, doc_row, doc_col, *far)


def backward_body(row0, far_on, *refs):
    (
        q_ref,
        k_ref,
        v_ref,
        doc_row_ref,
        doc_col_ref,
        o_ref,
        do_ref,
        lse_ref,
        cos_ref,
        sin_ref,
    ) = refs[:10]
    rest = list(refs[10:])
    if far_on:
        far_ref = rest.pop(0)
    if row0 == 0:
        add_k_ref, add_v_ref = rest.pop(0), rest.pop(0)
    grad_ref = rest[0]
    heads = grad_ref.shape[1] // (3 * HEAD_DIM)
    dq_ref, dk_ref, dv_ref = (
        grad_ref.at[
            :, pl.ds(pl.multiple_of((i * heads + pl.program_id(0)) * HEAD_DIM, HEAD_DIM), HEAD_DIM)
        ]
        for i in range(3)
    )
    if row0:
        low_k_ref, low_v_ref = rest[1:3]
    bias_ref, acc_k_ref, acc_v_ref = rest[-3:]
    count = q_ref.shape[0]
    size = min(SUB, count)
    scale = 1.0 / math.sqrt(HEAD_DIM)

    @pl.when(pl.program_id(0) == 0)
    def _():
        for index, start in enumerate(range(0, count, size)):
            make_bias(bias_ref, index, doc_row_ref, doc_col_ref, row0, start, size)

    if row0:
        acc_k_ref[...] = jnp.zeros(acc_k_ref.shape, F32)
        acc_v_ref[...] = jnp.zeros(acc_v_ref.shape, F32)
    else:
        acc_k_ref[...] = add_k_ref[...]
        acc_v_ref[...] = add_v_ref[...]
    for index, start in enumerate(range(0, count, size)):
        low, high = window(row0 + start, size)
        rows = slice(start, start + size)
        q, do, lse = q_ref[rows], do_ref[rows], lse_ref[0, rows]
        delta = jnp.sum(do.astype(F32) * o_ref[rows].astype(F32), axis=1, keepdims=True)
        keys, values = k_ref[low:high], v_ref[low:high]
        p = jnp.exp(dot(q, keys, 1, 1) * scale + bias_ref[index, :, : high - low] - lse)
        ds = (p * (dot(do, values, 1, 1) - delta)).astype(BF)
        acc_v_ref[low:high] += dot(p.astype(BF), do, 0, 0)
        acc_k_ref[low:high] += dot(ds, q, 0, 0)
        dq = dot(ds, keys, 1, 0)
        if far_on:
            far_bias = jnp.where(doc_col_ref[rows] == doc_row_ref[:, 0:1], 0.0, NEG) - lse
            parts = []
            for at in range(0, size, PICK_BLOCK):
                cut = slice(at, at + PICK_BLOCK)
                far_keys = far_ref[0, start + at : start + at + PICK_BLOCK, :HEAD_DIM]
                far_values = far_ref[0, start + at : start + at + PICK_BLOCK, HEAD_DIM:]
                pf = jnp.exp(dot(q[cut], far_keys, 1, 1) * scale + far_bias[cut])
                dsf = (pf * (dot(do[cut], far_values, 1, 1) - delta[cut])).astype(BF)
                parts.append(dot(dsf, far_keys, 1, 0))
            dq = dq + jnp.concatenate(parts, axis=0)
        at_rows = slice(row0 + start, row0 + start + size)
        dq_ref[rows] = turn_back(dq * scale, cos_ref[at_rows], sin_ref[at_rows]).astype(BF)
    dv_ref[...] = acc_v_ref[row0 : row0 + count].astype(BF)
    dk_ref[...] = turn_back(
        acc_k_ref[row0 : row0 + count] * scale,
        cos_ref[row0 : row0 + count],
        sin_ref[row0 : row0 + count],
    ).astype(BF)
    if row0:
        low_k_ref[...] = acc_k_ref[:row0]
        low_v_ref[...] = acc_v_ref[:row0]


def attend_backward(
    q, k, v, doc_row, doc_col, out, grad_out, lse, cosine, sine, row0, count, far, low
):
    heads = q.shape[1] // HEAD_DIM
    seg_len = q.shape[0]
    high = row0 + count
    at = row0 // count
    size = min(SUB, count)
    wide = max(w[1] - w[0] for w in (window(row0 + s, size) for s in range(0, count, size)))
    head_cols = lambda n: pl.BlockSpec((n, HEAD_DIM), lambda h: (0, h))
    whole = lambda n, m: pl.BlockSpec((n, m), lambda h: (0, 0))
    in_specs = [
        pl.BlockSpec((count, HEAD_DIM), lambda h: (at, h)),
        head_cols(high),
        head_cols(high),
        whole(1, seg_len),
        pl.BlockSpec((count, 1), lambda h: (at, 0)),
        head_cols(count),
        head_cols(count),
        pl.BlockSpec((1, count, 1), lambda h: (h, 0, 0)),
        whole(high, HEAD_DIM),
        whole(high, HEAD_DIM),
    ]
    args = [q, k, v, doc_row, doc_col, out, grad_out, lse, cosine, sine]
    if far is not None:
        in_specs.append(pl.BlockSpec((1, count, 2 * HEAD_DIM), lambda h: (h, 0, 0)))
        args.append(far)
    if row0 == 0:
        in_specs += [head_cols(count)] * 2
        args += list(low)
    out_specs = [whole(count, 3 * heads * HEAD_DIM)]
    out_shape = [jax.ShapeDtypeStruct((count, 3 * heads * HEAD_DIM), BF)]
    if row0:
        out_specs += [head_cols(row0)] * 2
        out_shape += [jax.ShapeDtypeStruct((row0, heads * HEAD_DIM), F32)] * 2
    return pl.pallas_call(
        functools.partial(backward_body, row0, far is not None),
        grid=(heads,),
        in_specs=in_specs,
        out_specs=out_specs,
        out_shape=out_shape,
        scratch_shapes=[
            pltpu.VMEM((count // size, size, wide), F32),
            pltpu.VMEM((high, HEAD_DIM), F32),
            pltpu.VMEM((high, HEAD_DIM), F32),
        ],
        cost_estimate=SMALL,
        name="attend_backward",
    )(*args)


def bit_of(bit):
    return (lax.axis_index("seg") >> bit) & 1


def half_rows(part, which):
    size = part.shape[0] // 2
    return lax.dynamic_slice_in_dim(part, which * size, size)


SMALL = pl.CostEstimate(flops=1, bytes_accessed=1, transcendentals=0)


def z_of():
    return lax.axis_index("seg") >> 2


def z_swap(block, shift):
    count = lax.axis_size("seg")
    return lax.ppermute(block, "seg", [(i, i ^ (shift << 2)) for i in range(count)])


def split_body(at_ref, part_ref, got_ref, *out_refs):
    total = (part_ref[...].astype(F32) + got_ref[...].astype(F32)).astype(BF)
    for shift, out_ref in enumerate(out_refs):

        @pl.when(pl.program_id(0) == shift)
        def _():
            out_ref[...] = total


def split_z(part, got, bit):
    rows, cols = got.shape[0] // 4, got.shape[1]
    return pl.pallas_call(
        split_body,
        grid_spec=pltpu.PrefetchScalarGridSpec(
            num_scalar_prefetch=1,
            grid=(4,),
            in_specs=[
                pl.BlockSpec((rows, cols), lambda s, at: (4 * at[0] + (at[1] ^ s), 0)),
                pl.BlockSpec((rows, cols), lambda s, at: (at[1] ^ s, 0)),
            ],
            out_specs=[pl.BlockSpec((rows, cols), lambda s, at: (0, 0))] * 4,
        ),
        out_shape=[jax.ShapeDtypeStruct((rows, cols), BF)] * 4,
        cost_estimate=SMALL,
        name="split_z",
    )(jnp.stack([bit_of(bit), z_of()]), part, got)


def join_body(at_ref, *refs):
    for shift, ref in enumerate(refs[:-1]):

        @pl.when(pl.program_id(0) == shift)
        def _():
            refs[-1][...] = ref[...]


def join_z(parts):
    rows, cols = parts[0].shape
    return pl.pallas_call(
        join_body,
        grid_spec=pltpu.PrefetchScalarGridSpec(
            num_scalar_prefetch=1,
            grid=(4,),
            in_specs=[pl.BlockSpec((rows, cols), lambda s, at: (0, 0))] * 4,
            out_specs=pl.BlockSpec((rows, cols), lambda s, at: (at[0] ^ s, 0)),
        ),
        out_shape=jax.ShapeDtypeStruct((4 * rows, cols), BF),
        cost_estimate=SMALL,
        name="join_z",
    )(z_of().reshape(1), *parts)


def double_body(mine_ref, part_ref, got_ref, out_ref):
    rows = part_ref.shape[0]
    for mine in (0, 1):

        @pl.when(mine_ref[0] == mine)
        def _():
            out_ref[mine * rows : (mine + 1) * rows] = part_ref[...]
            out_ref[(1 - mine) * rows : (2 - mine) * rows] = got_ref[...]


def double(part, got, bit):
    rows, cols = part.shape
    return pl.pallas_call(
        double_body,
        in_specs=[pl.BlockSpec(memory_space=pltpu.SMEM)] + [pl.BlockSpec((rows, cols))] * 2,
        out_specs=pl.BlockSpec((2 * rows, cols)),
        out_shape=jax.ShapeDtypeStruct((2 * rows, cols), BF),
        cost_estimate=SMALL,
        name="double",
    )(bit_of(bit).reshape(1), part, got)


def close_body(mine_ref, part_ref, got_ref, *out_refs):
    width = part_ref.shape[1] // len(out_refs)
    for owner, ref in ((0, part_ref), (1, got_ref)):

        @pl.when((pl.program_id(0) == mine_ref[0]) == (owner == 0))
        def _():
            for i, out_ref in enumerate(out_refs):
                out_ref[...] = ref[:, i * width : (i + 1) * width].astype(F32)


def double_out(part, got, bit, pieces=1, fold=False):
    rows, cols = part.shape
    width = cols // pieces
    full = pl.BlockSpec((rows, cols), lambda h, mine: (0, 0))
    specs = [pl.BlockSpec((rows, width), lambda h, mine: (h, 0))] * pieces
    shapes = [jax.ShapeDtypeStruct((2 * rows, width), F32)] * pieces
    if fold:
        specs[-1] = pl.BlockSpec((rows, width), lambda h, mine: (0, h))
        shapes[-1] = jax.ShapeDtypeStruct((rows, 2 * width), F32)
    return pl.pallas_call(
        close_body,
        grid_spec=pltpu.PrefetchScalarGridSpec(
            num_scalar_prefetch=1, grid=(2,), in_specs=[full, full], out_specs=specs
        ),
        out_shape=shapes,
        cost_estimate=SMALL,
        name="double_out",
    )(bit_of(bit).reshape(1), part, got)


def attention_grads_body(n_a, n_b, j_a, j_b, o_a, o_b, g_a, g_b, out_ref):
    cols = g_a.shape[1]
    joint = (dot(n_a[...], j_a[...], 0, 0) + dot(n_b[...], j_b[...], 0, 0)).astype(BF)
    out_ref[:, : 3 * cols] = joint
    out_ref[:, 3 * cols :] = (
        dot(o_a[...], g_a[...], 0, 0) + dot(o_b[...], g_b[...], 0, 0)
    ).astype(BF)


def attention_grads(normed, joint_a, joint_b, att_a, att_b, grad_a, grad_b):
    dim = normed.shape[1]
    count, width = joint_a.shape
    cols = att_a.shape[1]
    tile = min(SUB, cols)
    folds = cols // tile
    cut = lambda chunk: pl.BlockSpec((count, tile), lambda i: (chunk, i))
    joint = pl.BlockSpec((count, width), lambda i: (0, 0))
    att = pl.BlockSpec((count, tile), lambda i: (0, i % folds))
    grad = pl.BlockSpec((count, cols), lambda i: (0, i // folds))
    return pl.pallas_call(
        attention_grads_body,
        grid=(dim // tile,),
        in_specs=[cut(0), cut(1), joint, joint, att, att, grad, grad],
        out_specs=pl.BlockSpec((tile, width + cols), lambda i: (i, 0)),
        out_shape=jax.ShapeDtypeStruct((dim, width + cols), BF),
        cost_estimate=SMALL,
        name="attention_grads",
    )(normed, normed, joint_a, joint_b, att_a, att_b, grad_a, grad_b)


def rows_dot_body(contract, a_ref, b_ref, out_ref):
    out_ref[...] = dot(a_ref[...], b_ref[...], 1, contract).astype(BF)


def rows_dot(a, b, contract):
    rows, depth = a.shape
    cols = b.shape[1 - contract]
    tile = 2 * SUB if cols % (2 * SUB) == 0 else cols
    b_spec = (
        pl.BlockSpec((depth, tile), lambda j: (0, j))
        if contract == 0
        else pl.BlockSpec((tile, depth), lambda j: (j, 0))
    )
    return pl.pallas_call(
        functools.partial(rows_dot_body, contract),
        grid=(cols // tile,),
        in_specs=[pl.BlockSpec((rows, depth), lambda j: (0, 0)), b_spec],
        out_specs=pl.BlockSpec((rows, tile), lambda j: (0, j)),
        out_shape=jax.ShapeDtypeStruct((rows, cols), BF),
        cost_estimate=SMALL,
        name="rows_dot",
    )(a, b)


def chunk_specs(count, tile, dim):
    steps = count // tile
    first = pl.BlockSpec((tile, dim), lambda g: (jnp.minimum(g, steps - 1), 0))
    second = pl.BlockSpec((tile, dim), lambda g: (jnp.maximum(g - steps, 0), 0))
    return steps, first, second


def output_body(steps, *refs):
    for chunk in (0, 1):
        hidden_ref, mine_ref, got_ref = refs[3 * chunk : 3 * chunk + 3]

        @pl.when((pl.program_id(0) < steps) == (chunk == 0))
        def _():
            total = mine_ref[...].astype(F32) + got_ref[...].astype(F32)
            refs[-1][...] = (hidden_ref[...] + total).astype(BF)


def output_rows(early, late):
    count, dim = early[0].shape
    tile = min(SUB, count)
    steps, first, second = chunk_specs(count, tile, dim)
    return pl.pallas_call(
        functools.partial(output_body, steps),
        grid=(2 * steps,),
        in_specs=[first] * 3 + [second] * 3,
        out_specs=pl.BlockSpec((tile, dim), lambda g: (g, 0)),
        out_shape=jax.ShapeDtypeStruct((2 * count, dim), BF),
        cost_estimate=SMALL,
        name="output_rows",
    )(*early, *late)


def norm_one_body(steps, x_ref, gain_ref, *refs):
    out_ref, grad_gain_ref = refs[-2:]

    @pl.when(pl.program_id(0) == 0)
    def _():
        grad_gain_ref[...] = jnp.zeros(grad_gain_ref.shape, F32)

    for chunk in (0, 1):
        total_ref, mine_ref, got_ref = refs[3 * chunk : 3 * chunk + 3]

        @pl.when((pl.program_id(0) < steps) == (chunk == 0))
        def _():
            x = x_ref[...].astype(F32)
            grad = mine_ref[...].astype(F32) + got_ref[...].astype(F32)
            scale = lax.rsqrt(jnp.mean(x * x, axis=-1, keepdims=True) + EPS)
            weighted = grad * gain_ref[...]
            inner = jnp.mean(weighted * x, axis=-1, keepdims=True)
            rows = scale * weighted - x * (scale * scale * scale * inner)
            out_ref[...] = (total_ref[...] + rows).astype(BF)
            grad_gain_ref[...] += jnp.sum(grad * x * scale, axis=0, keepdims=True)


def norm_one_rows(tokens, gain, early, late):
    count, dim = early[0].shape
    tile = min(SUB, count)
    steps, first, second = chunk_specs(count, tile, dim)
    rows = pl.BlockSpec((tile, dim), lambda g: (g, 0))
    line = pl.BlockSpec((1, dim), lambda g: (0, 0))
    return pl.pallas_call(
        functools.partial(norm_one_body, steps),
        grid=(2 * steps,),
        in_specs=[rows, line] + [first] * 3 + [second] * 3,
        out_specs=[rows, line],
        out_shape=[
            jax.ShapeDtypeStruct((2 * count, dim), BF),
            jax.ShapeDtypeStruct((1, dim), F32),
        ],
        cost_estimate=SMALL,
        name="norm_one_rows",
    )(tokens, gain, *early, *late)


def shards(
    tokens,
    document_ids,
    memory_picks,
    partner_ids,
    memory_keys,
    memory_values,
    first_gain,
    query_weight,
    key_weight,
    value_weight,
    out_weight,
    second_gain,
    gate_weight,
    up_weight,
    down_weight,
    cotangent,
):
    seg_len = document_ids.shape[1]
    heads = query_weight.shape[1] // HEAD_DIM
    mem_len = memory_keys.shape[1]
    blocks = memory_picks.shape[2]
    near = min(blocks, DOC_MOST // PICK_BLOCK)
    chunk = near * PICK_BLOCK
    me = lax.axis_index("seg")
    bits = lax.axis_size("seg").bit_length() - 1
    partner = partner_ids[0]
    paired = lax.axis_size("head") == 2

    ranks = rank_picks(memory_picks.reshape(heads * blocks, 2 * mem_len))
    ranks = ranks.reshape(heads, blocks, 2 * mem_len)[:, :near]
    first_len = jnp.sum((document_ids[0] == document_ids[0, 0]).astype(jnp.int32))
    used = (jnp.arange(near) * PICK_BLOCK < first_len)[None, :, None]
    ranks = jnp.where(used, ranks, 0)
    own_ranks, far_ranks = ranks[:, :, :mem_len], ranks[:, :, mem_len:]
    asked = [own_ranks]
    for bit in range(bits):
        wanted = partner == jnp.bitwise_xor(me, 1 << bit)
        asked.append(swap(jnp.where(wanted, far_ranks, jnp.zeros_like(far_ranks)), bit))

    cosine, sine = rope_tables(seg_len)
    doc_row = document_ids
    doc_col = document_ids.reshape(seg_len, 1)
    dim = tokens.shape[1]
    cosine, sine, doc_col = after((cosine, sine, doc_col), *asked[:1])
    q, k, v, normed_one = project(
        tokens, first_gain.reshape(1, -1), query_weight, key_weight, value_weight, cosine, sine
    )
    out_full = head_join(out_weight, 0) if paired else None
    joint_weight = jnp.concatenate([query_weight, key_weight, value_weight], axis=1)

    rows = gather_rows(asked[:1] + after(asked[1:], q), memory_keys[0], memory_values[0])
    far = [rows[0]] + [swap(rows[1 + bit], bit) for bit in range(bits)]

    def mix(st):
        if paired:
            return jnp.dot(head_join(st["att"], 1), out_full, preferred_element_type=F32)
        return head_sum(jnp.dot(st["att"], out_weight, preferred_element_type=F32).astype(BF))

    def feed(st, cut):
        st["hidden_in"] = tokens[cut].astype(F32) + st["mixed"]
        st["scale"] = rms_scale(st["hidden_in"])
        normed_two = (st["hidden_in"] * st["scale"] * second_gain).astype(BF)
        gate = jnp.dot(normed_two, gate_weight, preferred_element_type=F32)
        upper = jnp.dot(normed_two, up_weight, preferred_element_type=F32)
        sigmoid_gate = jax.nn.sigmoid(gate)
        grad_hidden = dot(cotangent[cut], down_weight, 1, 1)
        st["hidden"] = (gate * sigmoid_gate * upper).astype(BF)
        st["grad_gate"] = (
            grad_hidden * upper * sigmoid_gate * (1.0 + gate * (1.0 - sigmoid_gate))
        ).astype(BF)
        st["grad_upper"] = (grad_hidden * gate * sigmoid_gate).astype(BF)
        st["normed_two"] = normed_two
        st["part_two"] = (
            dot(st["grad_gate"], gate_weight, 1, 1) + dot(st["grad_upper"], up_weight, 1, 1)
        ).astype(BF)

    def feed_grads(st, cut):
        return (
            dot(st["hidden"], cotangent[cut], 0, 0),
            dot(
                st["normed_two"],
                jnp.concatenate([st["grad_gate"], st["grad_upper"]], axis=1),
                0,
                0,
            ),
        )

    def feed_out(st):
        down_part = jnp.dot(st["hidden"], down_weight, preferred_element_type=F32)
        st["output"] = (st["hidden_in"] + head_sum(down_part.astype(BF))).astype(BF)

    def norm_two(st, cut):
        rows, st["second_gain_grad"] = norm_backward(
            st["grad_normed_two"], st["hidden_in"], st["scale"], second_gain
        )
        st["total_grad"] = cotangent[cut].astype(F32) + rows
        st["grad_mixed"] = st["total_grad"].astype(BF)
        st["grad_att"] = dot(st["grad_mixed"], out_weight, 1, 1).astype(BF)

    def back(st, row0, low):
        parts = attend_backward(
            q, k, v, doc_row, doc_col, st["att"], st["grad_att"], st["lse"], cosine, sine,
            row0, chunk, st.get("far"), low,
        )
        st["joint"] = parts[0]
        return parts[1:]

    late, early = slice(chunk, 2 * chunk), slice(0, chunk)
    b, a = {}, {}
    b["att"], b["lse"] = attend_forward(
        after(q, rows), k, v, doc_row, doc_col, chunk, chunk, []
    )
    b["mixed"] = mix(b)
    feed(b, late)
    b["grad_normed_two"] = head_sum(b["part_two"])
    b_grads = feed_grads(b, late)
    b_grads, far = after((b_grads, far), b["part_two"])
    a["att"], a["lse"], a["far"] = attend_forward(q, k, v, doc_row, doc_col, 0, chunk, far)
    a["mixed"] = mix(a)
    b["grad_normed_two"] = after(b["grad_normed_two"], a["att"])
    norm_two(b, late)
    low = back(b, chunk, None)
    a["mixed"] = after(a["mixed"], b["joint"])
    feed(a, early)
    token = [b["second_gain_grad"]]

    def order(*values):
        values, token[0] = lax.optimization_barrier((values, token[0]))
        return values

    plan = []

    def at(time):
        return lambda step: plan.append((time, step))

    def piece(make_time, make, times, close):
        st = {}
        starts, ends = times[0::2], times[1::2]

        def step(i, begin, end):
            @at(starts[i])
            def _():
                st["sent"] = order(*st["send"])
                st["got"] = begin(st["sent"])

            @at(ends[i])
            def _():
                end(order(*st["got"]))

        def core_half(got):
            keep = half_rows(st["part"], bit_of(0))
            st["part"] = (keep.astype(F32) + got[0].astype(F32)).astype(BF)
            st["send"] = (half_rows(st["part"], 1 - bit_of(1)),)

        def y_half(got):
            own, *st["send"] = split_z(st["part"], got[0], 1)
            st["part"] = own

        def z_sum(got):
            total = sum((part.astype(F32) for part in got), st["part"].astype(F32))
            st["part"] = total.astype(BF)
            st["send"] = (st["part"],)

        def z_join(got):
            st["part"] = join_z([st["part"], *got])
            st["send"] = (st["part"],)

        def y_double(got):
            st["part"] = double(st["part"], got[0], 1)
            st["send"] = (st["part"],)

        @at(make_time)
        def _():
            (st["part"],) = order(make())
            st["send"] = (half_rows(st["part"], 1 - bit_of(0)),)

        one = lambda bit: lambda send: (swap(send[0], bit),)
        step(0, one(0), core_half)
        step(1, one(1), y_half)
        step(2, lambda send: tuple(z_swap(send[i], i + 1) for i in range(3)), z_sum)
        step(3, lambda send: tuple(z_swap(send[0], i + 1) for i in range(3)), z_join)
        step(4, one(1), y_double)
        step(5, one(0), lambda got: close(st["part"], got[0]))
        return st

    done = {}

    def close_as(*names, fold=False):
        def close(part, got):
            done.update(zip(names, order(*double_out(part, got, 0, len(names), fold))))

        return close

    a_grads = feed_grads(a, early)
    joined = [lambda i=i: (b_grads[i] + a_grads[i]).astype(BF) for i in range(2)]

    def wait_for(time, st):
        @at(time)
        def _():
            st["got"] = order(*st["got"])

    if paired and bits == 4:
        down_piece = piece(
            194,
            joined[0],
            [198, 207, 208, 213.2, 213.3, 216, 217.3, 220, 220.1, 224, 224.1, 227],
            close_as("down"),
        )
        wait_for(213, down_piece)
        piece(
            199,
            joined[1],
            [206, 212, 213.1, 217, 217.1, 221, 221.1, 229, 229.1, 234, 234.1, 238],
            close_as("gate", "up"),
        )
        piece(
            215,
            lambda: attention_grads(
                normed_one, a["joint"], b["joint"], a["att"], b["att"],
                a["grad_mixed"], b["grad_mixed"],
            ),
            [217.2, 219, 219.1, 223, 223.1, 231, 231.1, 233, 233.1, 237, 237.1, 239],
            close_as("query", "key", "value", "out", fold=True),
        )
    else:

        @at(300)
        def _():
            total = lambda part: lax.psum(part.astype(BF), "seg").astype(F32)
            joint = dot(normed_one[late], b["joint"], 0, 0)
            joint = total(joint + dot(normed_one[early], a["joint"], 0, 0))
            done["query"], done["key"], done["value"] = jnp.split(joint, 3, axis=1)
            out = dot(b["att"], b["grad_mixed"], 0, 0) + dot(a["att"], a["grad_mixed"], 0, 0)
            done["out"] = total(out)
            done["down"], both = (total(make()) for make in joined)
            done["gate"], done["up"] = jnp.split(both, 2, axis=1)

    down = lambda st: rows_dot(order(st["hidden"])[0], down_weight, 0)
    back_part = lambda st: rows_dot(order(st["joint"])[0], joint_weight, 1)
    exchange = lambda mine: head_swap(mine) if paired else lax.psum(mine, "head")
    mine_of = lambda mine: mine if paired else jnp.zeros_like(mine)
    full = lambda mine, got: mine_of(mine).astype(F32) + got.astype(F32)

    @at(193)
    def _():
        (a["part_two"],) = order(a["part_two"])
        a["got_two"] = exchange(a["part_two"])

    @at(216.1)
    def _():
        (b["down"],) = order(down(b))

    @at(216.2)
    def _():
        (a["down"],) = order(down(a))

    @at(209)
    def _():
        (got,) = order(a["got_two"])
        a["grad_normed_two"] = full(a["part_two"], got)

    def send_head(time, st, name):
        @at(time)
        def _():
            st["got_" + name] = exchange(order(st[name])[0])

    def take_head(time, st, name):
        @at(time)
        def _():
            (st["got_" + name],) = order(st["got_" + name])

    def take_head(time, st, name):
        @at(time)
        def _():
            (st["got_" + name],) = order(st["got_" + name])

    send_head(216.15, b, "down")
    take_head(222, b, "down")
    send_head(222.1, a, "down")
    take_head(226, a, "down")
    send_head(226.1, b, "part_one")
    take_head(232, b, "part_one")
    send_head(232.1, a, "part_one")
    take_head(233.2, a, "part_one")

    @at(210)
    def _():
        norm_two(a, early)
        a["grad_att"], a["grad_mixed"] = order(a["grad_att"], a["grad_mixed"])

    @at(214)
    def _():
        (a["grad_att"],) = order(a["grad_att"])
        back(a, 0, low)
        (a["joint"],) = order(a["joint"])

    @at(225)
    def _():
        (b["part_one"],) = order(back_part(b))

    @at(230)
    def _():
        (a["part_one"],) = order(back_part(a))

    rest = {}

    @at(228)
    def _():
        (rest["output"],) = order(
            output_rows(
                *((st["hidden_in"], mine_of(st["down"]), st["got_down"]) for st in (a, b))
            )
        )

    @at(233.3)
    def _():
        rest["tokens_grad"], first_gain_grad = order(
            *norm_one_rows(
                tokens,
                first_gain.reshape(1, -1),
                *(
                    (st["total_grad"], mine_of(st["part_one"]), st["got_part_one"])
                    for st in (a, b)
                ),
            )
        )
        second = (a["second_gain_grad"] + token[0]).reshape(1, -1)
        token[0] = jnp.concatenate([first_gain_grad, second], axis=0)

    gain_times = [(233.4, 234.2), (234.3, 237.2), (237.3, 238.1), (238.2, 239.5), (239.6, 239.7)]
    for bit in range(bits):

        @at(gain_times[bit][0])
        def _(bit=bit):
            done["gains_got"] = swap(token[0], bit)

        @at(gain_times[bit][1])
        def _():
            (got,) = order(done["gains_got"])
            token[0] = token[0] + got

    for _, step in sorted(plan, key=lambda entry: entry[0]):
        step()
    gains = token[0]
    return (
        rest["output"],
        rest["tokens_grad"],
        gains[0],
        done["query"],
        done["key"],
        done["value"],
        done["out"],
        gains[1],
        done["gate"],
        done["up"],
        done["down"],
    )


def solution(mesh):
    placed = (
        P("seg", None),
        P("seg", None),
        P("seg", "head", None, None),
        P("seg"),
        P("seg", None, "head"),
        P("seg", None, "head"),
        P(),
        P(None, "head"),
        P(None, "head"),
        P(None, "head"),
        P("head", None),
        P(),
        P(None, "head"),
        P(None, "head"),
        P("head", None),
        P("seg", None),
    )
    return jax.shard_map(
        shards,
        mesh=mesh,
        in_specs=placed,
        out_specs=(
            P("seg", None),
            P("seg", None),
            P(),
            P(None, "head"),
            P(None, "head"),
            P(None, "head"),
            P("head", None),
            P(),
            P(None, "head"),
            P(None, "head"),
            P("head", None),
        ),
        check_vma=False,
    )
```

```python
import functools
import math
from types import SimpleNamespace

import jax
import jax.numpy as jnp
from jax import lax
from jax.experimental import pallas as pl
from jax.experimental.pallas import tpu as pltpu
from jax.sharding import PartitionSpec as P

HEAD_DIM = 128
KPICK = 128
PICK_BLOCK = 128
DOC_MOST = 512
SUB = 256

EPS = 1e-05
NEG = -1e30
THETA = 10000.0
SMALL = pl.CostEstimate(flops=1, bytes_accessed=1, transcendentals=0)
COVER = pl.CostEstimate(flops=4 * 10**9, bytes_accessed=14 * 10**6, transcendentals=0)
BF = jnp.bfloat16
F32 = jnp.float32


def dot(a, b, ca, cb):
    return lax.dot_general(a, b, (((ca,), (cb,)), ((), ())), preferred_element_type=F32)


def swap(block, bit):
    count = lax.axis_size("seg")
    return lax.ppermute(block, "seg", [(i, i ^ (1 << bit)) for i in range(count)])


def head_swap(block):
    return lax.ppermute(block, "head", [(0, 1), (1, 0)])


def head_sum(part):
    if lax.axis_size("head") == 2:
        return part.astype(F32) + head_swap(part).astype(F32)
    return lax.psum(part, "head").astype(F32)


def head_join(mine, got, axis):
    first = lax.axis_index("head") == 0
    return jnp.concatenate(
        [jnp.where(first, mine, got), jnp.where(first, got, mine)], axis=axis
    )


def rope_tables(length):
    half_dim = HEAD_DIM // 2
    position = jnp.arange(length, dtype=F32)[:, None]
    frequency = THETA ** (-jnp.arange(half_dim, dtype=F32) / half_dim)
    angles = position * frequency[None, :]
    cosine, sine = jnp.cos(angles), jnp.sin(angles)
    return (
        jnp.concatenate([cosine, cosine], axis=1),
        jnp.concatenate([-sine, sine], axis=1),
    )


def rms_scale(token_rows):
    return lax.rsqrt(jnp.mean(token_rows * token_rows, axis=-1, keepdims=True) + EPS)


def norm_backward(grad_normed, token_rows, row_scale, gain_vec):
    weighted = grad_normed * gain_vec
    inner_mean = jnp.mean(weighted * token_rows, axis=-1, keepdims=True)
    grad_rows = row_scale * weighted - token_rows * row_scale**3 * inner_mean
    grad_gain = jnp.sum(grad_normed * token_rows * row_scale, axis=0)
    return (grad_rows, grad_gain)


def rank_body(picks_ref, out_ref):
    rows, cache_len = picks_ref.shape
    at_row = lax.broadcasted_iota(jnp.int32, (128, 256), 0)
    at_col = lax.broadcasted_iota(jnp.int32, (128, 256), 1)
    table = jnp.where((at_row <= at_col) | (at_col >= 128), 1.0, 0.0).astype(BF)
    carry = jnp.zeros((rows, 128), F32)
    for chunk in range(cache_len // 128):
        cols = slice(chunk * 128, (chunk + 1) * 128)
        picked = picks_ref[:, cols].astype(F32)
        sums = dot(picked.astype(BF), table, 1, 0)
        out_ref[:, cols] = ((sums[:, :128] + carry) * picked).astype(BF)
        carry = carry + sums[:, 128:]


def rank_picks(picks):
    rows, cache_len = picks.shape
    return pl.pallas_call(
        rank_body,
        out_shape=jax.ShapeDtypeStruct((rows, cache_len), BF),
        cost_estimate=SMALL,
        name="rank_picks",
    )(picks)


def gather_body(*refs):
    asks = (len(refs) - 3) // 2
    keys_ref, values_ref = refs[asks], refs[asks + 1]
    out_refs = refs[asks + 2 : -1]
    table_ref = refs[-1]
    table_ref[:, :HEAD_DIM] = keys_ref[...]
    table_ref[:, HEAD_DIM:] = values_ref[...]
    blocks, mem_len = refs[0].shape[1], refs[0].shape[2]
    slot = lax.broadcasted_iota(jnp.int32, (KPICK, mem_len), 0).astype(F32) + 1.0
    for ask_ref, out_ref in zip(refs[:asks], out_refs):
        ranks = ask_ref[0].astype(F32)
        wanted = jnp.max(ranks) > 0.0

        @pl.when(wanted)
        def _():
            chosen = jnp.concatenate(
                [
                    jnp.where(ranks[block : block + 1] == slot, 1.0, 0.0).astype(BF)
                    for block in range(blocks)
                ],
                axis=0,
            )
            out_ref[0] = dot(chosen, table_ref[...], 1, 0).astype(BF)

        @pl.when(jnp.logical_not(wanted))
        def _():
            out_ref[0] = jnp.zeros(out_ref.shape[1:], BF)


def gather_rows(asked, cache_keys, cache_values):
    heads, blocks, mem_len = asked[0].shape
    return pl.pallas_call(
        gather_body,
        grid=(heads,),
        in_specs=[pl.BlockSpec((1, blocks, mem_len), lambda h: (h, 0, 0))] * len(asked)
        + [pl.BlockSpec((mem_len, HEAD_DIM), lambda h: (0, h))] * 2,
        out_specs=[pl.BlockSpec((1, blocks * KPICK, 2 * HEAD_DIM), lambda h: (h, 0, 0))]
        * len(asked),
        out_shape=[jax.ShapeDtypeStruct((heads, blocks * KPICK, 2 * HEAD_DIM), BF)] * len(asked),
        scratch_shapes=[pltpu.VMEM((mem_len, 2 * HEAD_DIM), BF)],
        cost_estimate=SMALL,
        name="gather_rows",
    )(*asked, cache_keys, cache_values)


def turn(part, cosine, sine):
    return part * cosine + pltpu.roll(part, HEAD_DIM // 2, 1) * sine


def turn_back(part, cosine, sine):
    return part * cosine - pltpu.roll(part, HEAD_DIM // 2, 1) * sine


def project_body(
    tokens_ref, gain_ref, wq_ref, wk_ref, wv_ref, cos_ref, sin_ref, q_ref, k_ref, v_ref, n_ref
):
    length = tokens_ref.shape[0]
    width = wq_ref.shape[1]
    tile = min(SUB, length)

    @pl.when(pl.program_id(0) == 0)
    def _():
        for start in range(0, length, tile):
            rows = slice(start, start + tile)
            x = tokens_ref[rows].astype(F32)
            scale = lax.rsqrt(jnp.mean(x * x, axis=-1, keepdims=True) + EPS)
            n_ref[rows] = (x * scale * gain_ref[...]).astype(BF)

    for start in range(0, length, tile):
        rows = slice(start, start + tile)
        x = n_ref[rows]
        cosine, sine = cos_ref[rows], sin_ref[rows]
        for w_ref, o_ref in ((wq_ref, q_ref), (wk_ref, k_ref)):
            full = dot(x, w_ref[...], 1, 0)
            for at in range(0, width, HEAD_DIM):
                cols = slice(at, at + HEAD_DIM)
                o_ref[rows, cols] = turn(full[:, cols], cosine, sine).astype(BF)
        v_ref[rows] = dot(x, wv_ref[...], 1, 0).astype(BF)


def project(tokens, gain, wq, wk, wv, cosine, sine):
    length, dim = tokens.shape
    cols = wq.shape[1]
    width = 2 * HEAD_DIM if cols % (2 * HEAD_DIM) == 0 else HEAD_DIM
    whole = lambda shape: pl.BlockSpec(shape, lambda g: (0, 0))
    return pl.pallas_call(
        project_body,
        grid=(cols // width,),
        in_specs=[whole((length, dim)), whole((1, dim))]
        + [pl.BlockSpec((dim, width), lambda g: (0, g))] * 3
        + [whole((length, HEAD_DIM))] * 2,
        out_specs=[pl.BlockSpec((length, width), lambda g: (0, g))] * 3 + [whole((length, dim))],
        out_shape=[jax.ShapeDtypeStruct((length, cols), BF)] * 3
        + [jax.ShapeDtypeStruct((length, dim), BF)],
        cost_estimate=SMALL,
        name="project",
    )(tokens, gain, wq, wk, wv, cosine, sine)


def window(start, size):
    return max(0, start - DOC_MOST), start + size


def make_bias(bias_ref, index, doc_row_ref, doc_col_ref, row0, start, size):
    low, high = window(row0 + start, size)
    at_query = lax.broadcasted_iota(jnp.int32, (size, high - low), 0) + (row0 + start)
    at_key = lax.broadcasted_iota(jnp.int32, (size, high - low), 1) + low
    same = doc_row_ref[:, low:high] == doc_col_ref[start : start + size]
    bias_ref[index, :, : high - low] = jnp.where(same & (at_key <= at_query), 0.0, NEG)


def forward_body(row0, far_count, *refs):
    q_ref, k_ref, v_ref, doc_row_ref, doc_col_ref = refs[:5]
    far_refs = refs[5 : 5 + far_count]
    outs = refs[5 + far_count :]
    o_ref, lse_ref = outs[:2]
    far_ref = outs[2] if far_count else None
    bias_ref = outs[-1]
    count = q_ref.shape[0]
    size = min(SUB, count)
    scale = 1.0 / math.sqrt(HEAD_DIM)

    @pl.when(pl.program_id(0) == 0)
    def _():
        for index, start in enumerate(range(0, count, size)):
            make_bias(bias_ref, index, doc_row_ref, doc_col_ref, row0, start, size)

    if far_count:
        total = far_refs[0][0]
        for other in far_refs[1:]:
            total = total + other[0]
        far_ref[0] = total
    for index, start in enumerate(range(0, count, size)):
        low, high = window(row0 + start, size)
        rows = slice(start, start + size)
        q = q_ref[rows]
        s = dot(q, k_ref[low:high], 1, 1) * scale + bias_ref[index, :, : high - low]
        m = jnp.max(s, axis=1, keepdims=True)
        if far_count:
            far_bias = jnp.where(doc_col_ref[rows] == doc_row_ref[:, 0:1], 0.0, NEG)
            sf = jnp.concatenate(
                [
                    dot(
                        q[at : at + PICK_BLOCK],
                        far_ref[0, start + at : start + at + PICK_BLOCK, :HEAD_DIM],
                        1,
                        1,
                    )
                    for at in range(0, size, PICK_BLOCK)
                ],
                axis=0,
            )
            sf = sf * scale + far_bias
            m = jnp.maximum(m, jnp.max(sf, axis=1, keepdims=True))
        p = jnp.exp(s - m)
        total = jnp.sum(p, axis=1, keepdims=True)
        o = dot(p.astype(BF), v_ref[low:high], 1, 0)
        if far_count:
            pf = jnp.exp(sf - m)
            total = total + jnp.sum(pf, axis=1, keepdims=True)
            pf = pf.astype(BF)
            o = o + jnp.concatenate(
                [
                    dot(
                        pf[at : at + PICK_BLOCK],
                        far_ref[0, start + at : start + at + PICK_BLOCK, HEAD_DIM:],
                        1,
                        0,
                    )
                    for at in range(0, size, PICK_BLOCK)
                ],
                axis=0,
            )
        o_ref[rows] = (o / total).astype(BF)
        lse_ref[0, rows] = m + jnp.log(total)


def attend_forward(q, k, v, doc_row, doc_col, row0, count, far):
    heads = q.shape[1] // HEAD_DIM
    seg_len = q.shape[0]
    high = row0 + count
    at = row0 // count
    size = min(SUB, count)
    wide = max(w[1] - w[0] for w in (window(row0 + s, size) for s in range(0, count, size)))
    key_spec = pl.BlockSpec((high, HEAD_DIM), lambda h: (0, h))
    far_spec = pl.BlockSpec((1, count, 2 * HEAD_DIM), lambda h: (h, 0, 0))
    far_shape = jax.ShapeDtypeStruct((heads, count, 2 * HEAD_DIM), BF)
    return pl.pallas_call(
        functools.partial(forward_body, row0, len(far)),
        grid=(heads,),
        in_specs=[
            pl.BlockSpec((count, HEAD_DIM), lambda h: (at, h)),
            key_spec,
            key_spec,
            pl.BlockSpec((1, seg_len), lambda h: (0, 0)),
            pl.BlockSpec((count, 1), lambda h: (at, 0)),
        ]
        + [far_spec] * len(far),
        out_specs=[
            pl.BlockSpec((count, HEAD_DIM), lambda h: (0, h)),
            pl.BlockSpec((1, count, 1), lambda h: (h, 0, 0)),
        ]
        + [far_spec] * bool(far),
        out_shape=[
            jax.ShapeDtypeStruct((count, heads * HEAD_DIM), BF),
            jax.ShapeDtypeStruct((heads, count, 1), F32),
        ]
        + [far_shape] * bool(far),
        scratch_shapes=[pltpu.VMEM((count // size, size, wide), F32)],
        cost_estimate=SMALL,
        name="attend_forward",
    )(q, k, v, doc_row, doc_col, *far)


def backward_body(row0, far_on, *refs):
    (
        q_ref,
        k_ref,
        v_ref,
        doc_row_ref,
        doc_col_ref,
        o_ref,
        do_ref,
        lse_ref,
        cos_ref,
        sin_ref,
    ) = refs[:10]
    rest = list(refs[10:])
    if far_on:
        far_ref = rest.pop(0)
    if row0 == 0:
        add_k_ref, add_v_ref = rest.pop(0), rest.pop(0)
    grad_ref = rest[0]
    heads = grad_ref.shape[1] // (3 * HEAD_DIM)
    dq_ref, dk_ref, dv_ref = (
        grad_ref.at[
            :, pl.ds(pl.multiple_of((i * heads + pl.program_id(0)) * HEAD_DIM, HEAD_DIM), HEAD_DIM)
        ]
        for i in range(3)
    )
    if row0:
        low_k_ref, low_v_ref = rest[1:3]
    bias_ref, acc_k_ref, acc_v_ref = rest[-3:]
    count = q_ref.shape[0]
    size = min(SUB, count)
    scale = 1.0 / math.sqrt(HEAD_DIM)

    @pl.when(pl.program_id(0) == 0)
    def _():
        for index, start in enumerate(range(0, count, size)):
            make_bias(bias_ref, index, doc_row_ref, doc_col_ref, row0, start, size)

    if row0:
        acc_k_ref[...] = jnp.zeros(acc_k_ref.shape, F32)
        acc_v_ref[...] = jnp.zeros(acc_v_ref.shape, F32)
    else:
        acc_k_ref[...] = add_k_ref[...]
        acc_v_ref[...] = add_v_ref[...]
    for index, start in enumerate(range(0, count, size)):
        low, high = window(row0 + start, size)
        rows = slice(start, start + size)
        q, do, lse = q_ref[rows], do_ref[rows], lse_ref[0, rows]
        delta = jnp.sum(do.astype(F32) * o_ref[rows].astype(F32), axis=1, keepdims=True)
        keys, values = k_ref[low:high], v_ref[low:high]
        p = jnp.exp(dot(q, keys, 1, 1) * scale + bias_ref[index, :, : high - low] - lse)
        ds = (p * (dot(do, values, 1, 1) - delta)).astype(BF)
        acc_v_ref[low:high] += dot(p.astype(BF), do, 0, 0)
        acc_k_ref[low:high] += dot(ds, q, 0, 0)
        dq = dot(ds, keys, 1, 0)
        if far_on:
            far_bias = jnp.where(doc_col_ref[rows] == doc_row_ref[:, 0:1], 0.0, NEG) - lse
            parts = []
            for at in range(0, size, PICK_BLOCK):
                cut = slice(at, at + PICK_BLOCK)
                far_keys = far_ref[0, start + at : start + at + PICK_BLOCK, :HEAD_DIM]
                far_values = far_ref[0, start + at : start + at + PICK_BLOCK, HEAD_DIM:]
                pf = jnp.exp(dot(q[cut], far_keys, 1, 1) * scale + far_bias[cut])
                dsf = (pf * (dot(do[cut], far_values, 1, 1) - delta[cut])).astype(BF)
                parts.append(dot(dsf, far_keys, 1, 0))
            dq = dq + jnp.concatenate(parts, axis=0)
        at_rows = slice(row0 + start, row0 + start + size)
        dq_ref[rows] = turn_back(dq * scale, cos_ref[at_rows], sin_ref[at_rows]).astype(BF)
    dv_ref[...] = acc_v_ref[row0 : row0 + count].astype(BF)
    dk_ref[...] = turn_back(
        acc_k_ref[row0 : row0 + count] * scale,
        cos_ref[row0 : row0 + count],
        sin_ref[row0 : row0 + count],
    ).astype(BF)
    if row0:
        low_k_ref[...] = acc_k_ref[:row0]
        low_v_ref[...] = acc_v_ref[:row0]


def attend_backward(
    q, k, v, doc_row, doc_col, out, grad_out, lse, cosine, sine, row0, count, far, low
):
    heads = q.shape[1] // HEAD_DIM
    seg_len = q.shape[0]
    high = row0 + count
    at = row0 // count
    size = min(SUB, count)
    wide = max(w[1] - w[0] for w in (window(row0 + s, size) for s in range(0, count, size)))
    head_cols = lambda n: pl.BlockSpec((n, HEAD_DIM), lambda h: (0, h))
    whole = lambda n, m: pl.BlockSpec((n, m), lambda h: (0, 0))
    in_specs = [
        pl.BlockSpec((count, HEAD_DIM), lambda h: (at, h)),
        head_cols(high),
        head_cols(high),
        whole(1, seg_len),
        pl.BlockSpec((count, 1), lambda h: (at, 0)),
        head_cols(count),
        head_cols(count),
        pl.BlockSpec((1, count, 1), lambda h: (h, 0, 0)),
        whole(high, HEAD_DIM),
        whole(high, HEAD_DIM),
    ]
    args = [q, k, v, doc_row, doc_col, out, grad_out, lse, cosine, sine]
    if far is not None:
        in_specs.append(pl.BlockSpec((1, count, 2 * HEAD_DIM), lambda h: (h, 0, 0)))
        args.append(far)
    if row0 == 0:
        in_specs += [head_cols(count)] * 2
        args += list(low)
    out_specs = [whole(count, 3 * heads * HEAD_DIM)]
    out_shape = [jax.ShapeDtypeStruct((count, 3 * heads * HEAD_DIM), BF)]
    if row0:
        out_specs += [head_cols(row0)] * 2
        out_shape += [jax.ShapeDtypeStruct((row0, heads * HEAD_DIM), F32)] * 2
    return pl.pallas_call(
        functools.partial(backward_body, row0, far is not None),
        grid=(heads,),
        in_specs=in_specs,
        out_specs=out_specs,
        out_shape=out_shape,
        scratch_shapes=[
            pltpu.VMEM((count // size, size, wide), F32),
            pltpu.VMEM((high, HEAD_DIM), F32),
            pltpu.VMEM((high, HEAD_DIM), F32),
        ],
        cost_estimate=COVER,
        name="attend_backward",
    )(*args)


def bit_of(bit):
    return (lax.axis_index("seg") >> bit) & 1


def half_rows(part, which):
    size = part.shape[0] // 2
    return lax.dynamic_slice_in_dim(part, which * size, size)


def z_of():
    return lax.axis_index("seg") >> 2


def z_swap(block, shift):
    count = lax.axis_size("seg")
    return lax.ppermute(block, "seg", [(i, i ^ (shift << 2)) for i in range(count)])


def split_body(at_ref, part_ref, got_ref, *out_refs):
    total = (part_ref[...].astype(F32) + got_ref[...].astype(F32)).astype(BF)
    for shift, out_ref in enumerate(out_refs):

        @pl.when(pl.program_id(0) == shift)
        def _():
            out_ref[...] = total


def split_z(part, got, bit):
    rows, cols = got.shape[0] // 4, got.shape[1]
    return pl.pallas_call(
        split_body,
        grid_spec=pltpu.PrefetchScalarGridSpec(
            num_scalar_prefetch=1,
            grid=(4,),
            in_specs=[
                pl.BlockSpec((rows, cols), lambda s, at: (4 * at[0] + (at[1] ^ s), 0)),
                pl.BlockSpec((rows, cols), lambda s, at: (at[1] ^ s, 0)),
            ],
            out_specs=[pl.BlockSpec((rows, cols), lambda s, at: (0, 0))] * 4,
        ),
        out_shape=[jax.ShapeDtypeStruct((rows, cols), BF)] * 4,
        cost_estimate=SMALL,
        name="split_z",
    )(jnp.stack([bit_of(bit), z_of()]), part, got)


def join_body(at_ref, *refs):
    for shift, ref in enumerate(refs[:-1]):

        @pl.when(pl.program_id(0) == shift)
        def _():
            refs[-1][...] = ref[...]


def join_z(parts):
    rows, cols = parts[0].shape
    return pl.pallas_call(
        join_body,
        grid_spec=pltpu.PrefetchScalarGridSpec(
            num_scalar_prefetch=1,
            grid=(4,),
            in_specs=[pl.BlockSpec((rows, cols), lambda s, at: (0, 0))] * 4,
            out_specs=pl.BlockSpec((rows, cols), lambda s, at: (at[0] ^ s, 0)),
        ),
        out_shape=jax.ShapeDtypeStruct((4 * rows, cols), BF),
        cost_estimate=SMALL,
        name="join_z",
    )(z_of().reshape(1), *parts)


def double_body(mine_ref, part_ref, got_ref, out_ref):
    rows = part_ref.shape[0]
    for mine in (0, 1):

        @pl.when(mine_ref[0] == mine)
        def _():
            out_ref[mine * rows : (mine + 1) * rows] = part_ref[...]
            out_ref[(1 - mine) * rows : (2 - mine) * rows] = got_ref[...]


def double(part, got, bit):
    rows, cols = part.shape
    return pl.pallas_call(
        double_body,
        in_specs=[pl.BlockSpec(memory_space=pltpu.SMEM)] + [pl.BlockSpec((rows, cols))] * 2,
        out_specs=pl.BlockSpec((2 * rows, cols)),
        out_shape=jax.ShapeDtypeStruct((2 * rows, cols), BF),
        cost_estimate=SMALL,
        name="double",
    )(bit_of(bit).reshape(1), part, got)


def close_body(mine_ref, part_ref, got_ref, *out_refs):
    width = part_ref.shape[1] // len(out_refs)
    for owner, ref in ((0, part_ref), (1, got_ref)):

        @pl.when((pl.program_id(0) == mine_ref[0]) == (owner == 0))
        def _():
            for i, out_ref in enumerate(out_refs):
                out_ref[...] = ref[:, i * width : (i + 1) * width].astype(F32)


def double_out(part, got, bit, pieces=1, fold=False):
    rows, cols = part.shape
    width = cols // pieces
    full = pl.BlockSpec((rows, cols), lambda h, mine: (0, 0))
    specs = [pl.BlockSpec((rows, width), lambda h, mine: (h, 0))] * pieces
    shapes = [jax.ShapeDtypeStruct((2 * rows, width), F32)] * pieces
    if fold:
        specs[-1] = pl.BlockSpec((rows, width), lambda h, mine: (0, h))
        shapes[-1] = jax.ShapeDtypeStruct((rows, 2 * width), F32)
    return pl.pallas_call(
        close_body,
        grid_spec=pltpu.PrefetchScalarGridSpec(
            num_scalar_prefetch=1, grid=(2,), in_specs=[full, full], out_specs=specs
        ),
        out_shape=shapes,
        cost_estimate=SMALL,
        name="double_out",
    )(bit_of(bit).reshape(1), part, got)


def attention_grads_body(n_a, n_b, j_a, j_b, o_a, o_b, g_a, g_b, out_ref):
    cols = g_a.shape[1]
    joint = (dot(n_a[...], j_a[...], 0, 0) + dot(n_b[...], j_b[...], 0, 0)).astype(BF)
    out_ref[:, : 3 * cols] = joint
    out_ref[:, 3 * cols :] = (
        dot(o_a[...], g_a[...], 0, 0) + dot(o_b[...], g_b[...], 0, 0)
    ).astype(BF)


def attention_grads(normed, joint_a, joint_b, att_a, att_b, grad_a, grad_b):
    dim = normed.shape[1]
    count, width = joint_a.shape
    cols = att_a.shape[1]
    tile = min(SUB, cols)
    folds = cols // tile
    cut = lambda chunk: pl.BlockSpec((count, tile), lambda i: (chunk, i))
    joint = pl.BlockSpec((count, width), lambda i: (0, 0))
    att = pl.BlockSpec((count, tile), lambda i: (0, i % folds))
    grad = pl.BlockSpec((count, cols), lambda i: (0, i // folds))
    return pl.pallas_call(
        attention_grads_body,
        grid=(dim // tile,),
        in_specs=[cut(0), cut(1), joint, joint, att, att, grad, grad],
        out_specs=pl.BlockSpec((tile, width + cols), lambda i: (i, 0)),
        out_shape=jax.ShapeDtypeStruct((dim, width + cols), BF),
        cost_estimate=COVER,
        name="attention_grads",
    )(normed, normed, joint_a, joint_b, att_a, att_b, grad_a, grad_b)


def rows_dot_body(a_ref, b_ref, out_ref):
    out_ref[...] = dot(a_ref[...], b_ref[...], 1, 0).astype(BF)


def rows_dot(a, b):
    rows, depth = a.shape
    cols = b.shape[1]
    tile = 2 * SUB if cols % (2 * SUB) == 0 else cols
    return pl.pallas_call(
        rows_dot_body,
        grid=(cols // tile,),
        in_specs=[
            pl.BlockSpec((rows, depth), lambda j: (0, 0)),
            pl.BlockSpec((depth, tile), lambda j: (0, j)),
        ],
        out_specs=pl.BlockSpec((rows, tile), lambda j: (0, j)),
        out_shape=jax.ShapeDtypeStruct((rows, cols), BF),
        cost_estimate=SMALL,
        name="rows_dot",
    )(a, b)


def chunk_specs(count, tile, dim):
    steps = count // tile
    first = pl.BlockSpec((tile, dim), lambda g: (jnp.minimum(g, steps - 1), 0))
    second = pl.BlockSpec((tile, dim), lambda g: (jnp.maximum(g - steps, 0), 0))
    return steps, first, second


def output_body(steps, *refs):
    for chunk in (0, 1):
        hidden_ref, mine_ref, got_ref = refs[3 * chunk : 3 * chunk + 3]

        @pl.when((pl.program_id(0) < steps) == (chunk == 0))
        def _():
            total = mine_ref[...].astype(F32) + got_ref[...].astype(F32)
            refs[-1][...] = (hidden_ref[...] + total).astype(BF)


def output_rows(early, late):
    count, dim = early[0].shape
    tile = min(SUB, count)
    steps, first, second = chunk_specs(count, tile, dim)
    return pl.pallas_call(
        functools.partial(output_body, steps),
        grid=(2 * steps,),
        in_specs=[first] * 3 + [second] * 3,
        out_specs=pl.BlockSpec((tile, dim), lambda g: (g, 0)),
        out_shape=jax.ShapeDtypeStruct((2 * count, dim), BF),
        cost_estimate=SMALL,
        name="output_rows",
    )(*early, *late)


def norm_one_body(steps, x_ref, gain_ref, *refs):
    out_ref, grad_gain_ref = refs[-2:]

    @pl.when(pl.program_id(0) == 0)
    def _():
        grad_gain_ref[...] = jnp.zeros(grad_gain_ref.shape, F32)

    for chunk in (0, 1):
        total_ref, mine_ref, got_ref = refs[3 * chunk : 3 * chunk + 3]

        @pl.when((pl.program_id(0) < steps) == (chunk == 0))
        def _():
            x = x_ref[...].astype(F32)
            grad = mine_ref[...].astype(F32) + got_ref[...].astype(F32)
            scale = lax.rsqrt(jnp.mean(x * x, axis=-1, keepdims=True) + EPS)
            weighted = grad * gain_ref[...]
            inner = jnp.mean(weighted * x, axis=-1, keepdims=True)
            rows = scale * weighted - x * (scale * scale * scale * inner)
            out_ref[...] = (total_ref[...] + rows).astype(BF)
            grad_gain_ref[...] += jnp.sum(grad * x * scale, axis=0, keepdims=True)


def norm_one_rows(tokens, gain, early, late):
    count, dim = early[0].shape
    tile = min(SUB, count)
    steps, first, second = chunk_specs(count, tile, dim)
    rows = pl.BlockSpec((tile, dim), lambda g: (g, 0))
    line = pl.BlockSpec((1, dim), lambda g: (0, 0))
    return pl.pallas_call(
        functools.partial(norm_one_body, steps),
        grid=(2 * steps,),
        in_specs=[rows, line] + [first] * 3 + [second] * 3,
        out_specs=[rows, line],
        out_shape=[
            jax.ShapeDtypeStruct((2 * count, dim), BF),
            jax.ShapeDtypeStruct((1, dim), F32),
        ],
        cost_estimate=SMALL,
        name="norm_one_rows",
    )(tokens, gain, *early, *late)


def shards(
    tokens,
    document_ids,
    memory_picks,
    partner_ids,
    memory_keys,
    memory_values,
    first_gain,
    query_weight,
    key_weight,
    value_weight,
    out_weight,
    second_gain,
    gate_weight,
    up_weight,
    down_weight,
    cotangent,
):
    seg_len = document_ids.shape[1]
    heads = query_weight.shape[1] // HEAD_DIM
    mem_len = memory_keys.shape[1]
    blocks = memory_picks.shape[2]
    near = min(blocks, DOC_MOST // PICK_BLOCK)
    chunk = near * PICK_BLOCK
    me = lax.axis_index("seg")
    bits = lax.axis_size("seg").bit_length() - 1
    partner = partner_ids[0]
    paired = lax.axis_size("head") == 2

    ranks = rank_picks(memory_picks.reshape(heads * blocks, 2 * mem_len))
    ranks = ranks.reshape(heads, blocks, 2 * mem_len)[:, :near]
    first_len = jnp.sum((document_ids[0] == document_ids[0, 0]).astype(jnp.int32))
    used = (jnp.arange(near) * PICK_BLOCK < first_len)[None, :, None]
    ranks = jnp.where(used, ranks, 0)
    own_ranks, far_ranks = ranks[:, :, :mem_len], ranks[:, :, mem_len:]
    asked = [own_ranks]
    for bit in range(bits):
        wanted = partner == jnp.bitwise_xor(me, 1 << bit)
        asked.append(swap(jnp.where(wanted, far_ranks, jnp.zeros_like(far_ranks)), bit))

    cosine, sine = rope_tables(seg_len)
    doc_row = document_ids
    doc_col = document_ids.reshape(seg_len, 1)
    dim = tokens.shape[1]
    token = [first_gain]

    def order(*values):
        values, token[0] = lax.optimization_barrier((values, token[0]))
        return values

    exchange = lambda mine: head_swap(mine) if paired else lax.psum(mine, "head")
    mine_of = lambda mine: mine if paired else jnp.zeros_like(mine)
    full = lambda mine, got: mine_of(mine).astype(F32) + got.astype(F32)

    q, k, v, normed_one = project(
        tokens, first_gain.reshape(1, -1), query_weight, key_weight, value_weight, cosine, sine
    )
    out_got = head_swap(out_weight) if paired else None
    joint_weight = jnp.concatenate([query_weight, key_weight, value_weight], axis=1)

    far = [None] * (bits + 1)
    split = max(1, bits - 2)

    def send_rows(slots):
        ranks = order(*(asked[slot] for slot in slots))
        rows = order(*gather_rows(list(ranks), memory_keys[0], memory_values[0]))
        for slot, block in zip(slots, rows):
            far[slot] = swap(block, slot - 1) if slot else block

    q, *asked = order(q, *asked)
    send_rows(range(bits, split, -1))

    def start_mix(st):
        (st.att,) = order(st.att)
        if paired:
            st.got_att = head_swap(st.att)

    def mix(st):
        if paired:
            (got,) = order(st.got_att)
            joined = head_join(st.att, got, 1)
            return jnp.dot(joined, out_full, preferred_element_type=F32)
        return head_sum(jnp.dot(st.att, out_weight, preferred_element_type=F32).astype(BF))

    def feed(st, cut):
        st.hidden_in = tokens[cut].astype(F32) + st.mixed
        st.scale = rms_scale(st.hidden_in)
        normed_two = (st.hidden_in * st.scale * second_gain).astype(BF)
        gate = jnp.dot(normed_two, gate_weight, preferred_element_type=F32)
        upper = jnp.dot(normed_two, up_weight, preferred_element_type=F32)
        sigmoid_gate = jax.nn.sigmoid(gate)
        grad_hidden = dot(cotangent[cut], down_weight, 1, 1)
        st.hidden = (gate * sigmoid_gate * upper).astype(BF)
        st.grad_gate = (
            grad_hidden * upper * sigmoid_gate * (1.0 + gate * (1.0 - sigmoid_gate))
        ).astype(BF)
        st.grad_upper = (grad_hidden * gate * sigmoid_gate).astype(BF)
        st.normed_two = normed_two
        st.part_two = (
            dot(st.grad_gate, gate_weight, 1, 1) + dot(st.grad_upper, up_weight, 1, 1)
        ).astype(BF)

    def feed_grads(st, cut):
        return (
            dot(st.hidden, cotangent[cut], 0, 0),
            dot(
                st.normed_two,
                jnp.concatenate([st.grad_gate, st.grad_upper], axis=1),
                0,
                0,
            ),
        )

    def feed_out(st):
        down_part = jnp.dot(st.hidden, down_weight, preferred_element_type=F32)
        st.output = (st.hidden_in + head_sum(down_part.astype(BF))).astype(BF)

    def norm_two(st, cut):
        rows, st.second_gain_grad = norm_backward(
            st.grad_normed_two, st.hidden_in, st.scale, second_gain
        )
        st.total_grad = cotangent[cut].astype(F32) + rows
        st.grad_mixed = st.total_grad.astype(BF)
        st.grad_att = dot(st.grad_mixed, out_weight, 1, 1).astype(BF)

    def back(st, row0, low):
        parts = attend_backward(
            q, k, v, doc_row, doc_col, st.att, st.grad_att, st.lse, cosine, sine,
            row0, chunk, getattr(st, "far", None), low,
        )
        st.joint = parts[0]
        return parts[1:]

    late, early = slice(chunk, 2 * chunk), slice(0, chunk)
    b, a = SimpleNamespace(), SimpleNamespace()
    (q,) = order(q)
    b.att, b.lse = attend_forward(q, k, v, doc_row, doc_col, chunk, chunk, [])
    if paired:
        (out_got,) = order(out_got)
        out_full = head_join(out_weight, out_got, 0)
    start_mix(b)
    send_rows([0, *range(1, split + 1)])
    b.mixed = mix(b)
    feed(b, late)
    (b.part_two,) = order(b.part_two)
    b.got_two = exchange(b.part_two)
    far_hi = order(*far[split + 1 :])
    *b_grads, joint_weight = order(*feed_grads(b, late), joint_weight)
    far = order(*far[: split + 1]) + far_hi
    a.att, a.lse, a.far = attend_forward(q, k, v, doc_row, doc_col, 0, chunk, list(far))
    start_mix(a)
    (got,) = order(b.got_two)
    b.grad_normed_two = full(b.part_two, got)
    norm_two(b, late)
    (b.grad_att,) = order(b.grad_att)
    low = back(b, chunk, None)
    b.joint, *low = order(b.joint, *low)
    a.mixed = mix(a)
    feed(a, early)

    plan = []

    def at(time):
        return lambda step: plan.append((time, step))

    def piece(make_time, make, times, close):
        st = SimpleNamespace()
        starts, ends = times[0::2], times[1::2]

        def step(i, begin, end):
            @at(starts[i])
            def _():
                st.sent = order(*st.send)
                st.got = begin(st.sent)

            @at(ends[i])
            def _():
                end(order(*st.got))

        def core_half(got):
            keep = half_rows(st.part, bit_of(0))
            st.part = (keep.astype(F32) + got[0].astype(F32)).astype(BF)
            st.send = (half_rows(st.part, 1 - bit_of(1)),)

        def y_half(got):
            own, *st.send = split_z(st.part, got[0], 1)
            st.part = own

        def z_sum(got):
            total = sum((part.astype(F32) for part in got), st.part.astype(F32))
            st.part = total.astype(BF)
            st.send = (st.part,)

        def z_join(got):
            st.part = join_z([st.part, *got])
            st.send = (st.part,)

        def y_double(got):
            st.part = double(st.part, got[0], 1)
            st.send = (st.part,)

        @at(make_time)
        def _():
            (st.part,) = order(make())
            st.send = (half_rows(st.part, 1 - bit_of(0)),)

        one = lambda bit: lambda send: (swap(send[0], bit),)
        step(0, one(0), core_half)
        step(1, one(1), y_half)
        step(2, lambda send: tuple(z_swap(send[i], i + 1) for i in range(3)), z_sum)
        step(3, lambda send: tuple(z_swap(send[0], i + 1) for i in range(3)), z_join)
        step(4, one(1), y_double)
        step(5, one(0), lambda got: close(st.part, got[0]))
        return st

    done = SimpleNamespace()

    def close_as(*names, fold=False):
        def close(part, got):
            for name, value in zip(names, order(*double_out(part, got, 0, len(names), fold))):
                setattr(done, name, value)

        return close


    def make_down():
        (a.hidden,) = order(a.hidden)
        return (b_grads[0] + dot(a.hidden, cotangent[early], 0, 0)).astype(BF)

    def make_feed():
        a.grad_gate, a.grad_upper = order(a.grad_gate, a.grad_upper)
        return (b_grads[1] + feed_grads(a, early)[1]).astype(BF)

    joined = [make_down, make_feed]

    if paired and bits == 4:
        piece(
            194,
            joined[0],
            [198, 207, 208, 213.2, 213.3, 214.3, 214.4, 215.2, 218.2, 221.3, 221.35, 222],
            close_as("down"),
        )
        piece(
            199,
            joined[1],
            [206, 208.5, 208.6, 215.5, 215.6, 219, 219.1, 221, 221.1, 224.5, 224.6, 226],
            close_as("gate", "up"),
        )
        piece(
            215,
            lambda: attention_grads(
                normed_one, a.joint, b.joint, a.att, b.att,
                a.grad_mixed, b.grad_mixed,
            ),
            [215.7, 218, 218.02, 219.8, 219.9, 224, 224.1, 225, 225.1, 227, 227.1, 229],
            close_as("query", "key", "value", "out", fold=True),
        )
    else:

        @at(300)
        def _():
            total = lambda part: lax.psum(part.astype(BF), "seg").astype(F32)
            joint = dot(normed_one[late], b.joint, 0, 0)
            joint = total(joint + dot(normed_one[early], a.joint, 0, 0))
            done.query, done.key, done.value = jnp.split(joint, 3, axis=1)
            out = dot(b.att, b.grad_mixed, 0, 0) + dot(a.att, a.grad_mixed, 0, 0)
            done.out = total(out)
            done.down, both = (total(make()) for make in joined)
            done.gate, done.up = jnp.split(both, 2, axis=1)

    down = lambda st: rows_dot(order(st.hidden)[0], down_weight)
    back_part = lambda st: dot(order(st.joint)[0], joint_weight, 1, 1).astype(BF)
    @at(193)
    def _():
        (a.part_two,) = order(a.part_two)
        a.got_two = exchange(a.part_two)

    @at(208.7)
    def _():
        (b.down,) = order(down(b))

    @at(208.8)
    def _():
        (a.down,) = order(down(a))

    @at(209)
    def _():
        (got,) = order(a.got_two)
        a.grad_normed_two = full(a.part_two, got)

    sent, taken = {}, {}

    def head(key, send_time, part, take_time):
        @at(send_time)
        def _():
            (sent[key],) = order(part())
            taken[key] = exchange(sent[key])

        @at(take_time)
        def _():
            (taken[key],) = order(taken[key])

    head(0, 209.5, lambda: b.down, 214.5)
    head(1, 214.6, lambda: a.down, 215.4)
    head(2, 216.1, lambda: b.part_one, 218.05)
    head(3, 218.06, lambda: a.part_one, 220)

    @at(210)
    def _():
        norm_two(a, early)
        a.grad_att, a.grad_mixed = order(a.grad_att, a.grad_mixed)

    @at(214)
    def _():
        (a.grad_att,) = order(a.grad_att)
        back(a, 0, low)
        (a.joint,) = order(a.joint)

    @at(215.3)
    def _():
        (b.part_one,) = order(back_part(b))

    @at(215.35)
    def _():
        (a.part_one,) = order(back_part(a))

    rest = SimpleNamespace()

    @at(220.5)
    def _():
        (rest.output,) = order(
            output_rows(
                *(
                    (st.hidden_in, mine_of(sent[key]), taken[key])
                    for st, key in ((a, 1), (b, 0))
                )
            )
        )

    @at(220.7)
    def _():
        rest.tokens_grad, first_gain_grad = order(
            *norm_one_rows(
                tokens,
                token[0].reshape(1, -1),
                *(
                    (st.total_grad, mine_of(sent[key]), taken[key])
                    for st, key in ((a, 3), (b, 2))
                ),
            )
        )
        second = (a.second_gain_grad + b.second_gain_grad).reshape(1, -1)
        token[0] = jnp.concatenate([first_gain_grad, second], axis=0)

    gain_times = [(220.8, 221.05), (221.15, 223.9), (224.05, 224.45), (224.55, 224.95), (225.2, 225.3)]
    for bit in range(bits):

        @at(gain_times[bit][0])
        def _(bit=bit):
            done.gains_got = swap(token[0], bit)

        @at(gain_times[bit][1])
        def _():
            (got,) = order(done.gains_got)
            token[0] = token[0] + got

    for _, step in sorted(plan, key=lambda entry: entry[0]):
        step()
    gains = token[0]
    return (
        rest.output,
        rest.tokens_grad,
        gains[0],
        done.query,
        done.key,
        done.value,
        done.out,
        gains[1],
        done.gate,
        done.up,
        done.down,
    )


def solution(mesh):
    placed = (
        P("seg", None),
        P("seg", None),
        P("seg", "head", None, None),
        P("seg"),
        P("seg", None, "head"),
        P("seg", None, "head"),
        P(),
        P(None, "head"),
        P(None, "head"),
        P(None, "head"),
        P("head", None),
        P(),
        P(None, "head"),
        P(None, "head"),
        P("head", None),
        P("seg", None),
    )
    return jax.shard_map(
        shards,
        mesh=mesh,
        in_specs=placed,
        out_specs=(
            P("seg", None),
            P("seg", None),
            P(),
            P(None, "head"),
            P(None, "head"),
            P(None, "head"),
            P("head", None),
            P(),
            P(None, "head"),
            P(None, "head"),
            P("head", None),
        ),
        check_vma=False,
    )
```

```python
import functools
import math
from types import SimpleNamespace

import jax
import jax.numpy as jnp
from jax import lax
from jax.experimental import pallas as pl
from jax.experimental.pallas import tpu as pltpu
from jax.sharding import PartitionSpec as P

HEAD_DIM = 128
KPICK = 128
PICK_BLOCK = 128
DOC_MOST = 512
SUB = 256

EPS = 1e-05
NEG = -1e30
THETA = 10000.0
SMALL = pl.CostEstimate(flops=1, bytes_accessed=1, transcendentals=0)
COVER = pl.CostEstimate(flops=4 * 10**9, bytes_accessed=14 * 10**6, transcendentals=0)
BF = jnp.bfloat16
F32 = jnp.float32


def dot(a, b, ca, cb):
    return lax.dot_general(a, b, (((ca,), (cb,)), ((), ())), preferred_element_type=F32)


def swap(block, bit):
    count = lax.axis_size("seg")
    return lax.ppermute(block, "seg", [(i, i ^ (1 << bit)) for i in range(count)])


def head_swap(block):
    return lax.ppermute(block, "head", [(0, 1), (1, 0)])


def head_sum(part):
    if lax.axis_size("head") == 2:
        return part.astype(F32) + head_swap(part).astype(F32)
    return lax.psum(part, "head").astype(F32)


def head_join(mine, got, axis):
    first = lax.axis_index("head") == 0
    return jnp.concatenate(
        [jnp.where(first, mine, got), jnp.where(first, got, mine)], axis=axis
    )


def rope_tables(length):
    half_dim = HEAD_DIM // 2
    position = jnp.arange(length, dtype=F32)[:, None]
    frequency = THETA ** (-jnp.arange(half_dim, dtype=F32) / half_dim)
    angles = position * frequency[None, :]
    cosine, sine = jnp.cos(angles), jnp.sin(angles)
    return (
        jnp.concatenate([cosine, cosine], axis=1),
        jnp.concatenate([-sine, sine], axis=1),
    )


def rms_scale(token_rows):
    return lax.rsqrt(jnp.mean(token_rows * token_rows, axis=-1, keepdims=True) + EPS)


def norm_backward(grad_normed, token_rows, row_scale, gain_vec):
    weighted = grad_normed * gain_vec
    inner_mean = jnp.mean(weighted * token_rows, axis=-1, keepdims=True)
    grad_rows = row_scale * weighted - token_rows * row_scale**3 * inner_mean
    grad_gain = jnp.sum(grad_normed * token_rows * row_scale, axis=0)
    return (grad_rows, grad_gain)


def rank_body(picks_ref, out_ref):
    rows, cache_len = picks_ref.shape
    at_row = lax.broadcasted_iota(jnp.int32, (128, 256), 0)
    at_col = lax.broadcasted_iota(jnp.int32, (128, 256), 1)
    table = jnp.where((at_row <= at_col) | (at_col >= 128), 1.0, 0.0).astype(BF)
    carry = jnp.zeros((rows, 128), F32)
    for chunk in range(cache_len // 128):
        cols = slice(chunk * 128, (chunk + 1) * 128)
        picked = picks_ref[:, cols].astype(F32)
        sums = dot(picked.astype(BF), table, 1, 0)
        out_ref[:, cols] = ((sums[:, :128] + carry) * picked).astype(BF)
        carry = carry + sums[:, 128:]


def rank_picks(picks):
    rows, cache_len = picks.shape
    return pl.pallas_call(
        rank_body,
        out_shape=jax.ShapeDtypeStruct((rows, cache_len), BF),
        cost_estimate=SMALL,
        name="rank_picks",
    )(picks)


def gather_body(*refs):
    asks = (len(refs) - 3) // 2
    keys_ref, values_ref = refs[asks], refs[asks + 1]
    out_refs = refs[asks + 2 : -1]
    table_ref = refs[-1]
    table_ref[:, :HEAD_DIM] = keys_ref[...]
    table_ref[:, HEAD_DIM:] = values_ref[...]
    blocks, mem_len = refs[0].shape[1], refs[0].shape[2]
    slot = lax.broadcasted_iota(jnp.int32, (KPICK, mem_len), 0).astype(F32) + 1.0
    for ask_ref, out_ref in zip(refs[:asks], out_refs):
        ranks = ask_ref[0].astype(F32)
        wanted = jnp.max(ranks) > 0.0

        @pl.when(wanted)
        def _():
            chosen = jnp.concatenate(
                [
                    jnp.where(ranks[block : block + 1] == slot, 1.0, 0.0).astype(BF)
                    for block in range(blocks)
                ],
                axis=0,
            )
            out_ref[0] = dot(chosen, table_ref[...], 1, 0).astype(BF)

        @pl.when(jnp.logical_not(wanted))
        def _():
            out_ref[0] = jnp.zeros(out_ref.shape[1:], BF)


def gather_rows(asked, cache_keys, cache_values):
    heads, blocks, mem_len = asked[0].shape
    return pl.pallas_call(
        gather_body,
        grid=(heads,),
        in_specs=[pl.BlockSpec((1, blocks, mem_len), lambda h: (h, 0, 0))] * len(asked)
        + [pl.BlockSpec((mem_len, HEAD_DIM), lambda h: (0, h))] * 2,
        out_specs=[pl.BlockSpec((1, blocks * KPICK, 2 * HEAD_DIM), lambda h: (h, 0, 0))]
        * len(asked),
        out_shape=[jax.ShapeDtypeStruct((heads, blocks * KPICK, 2 * HEAD_DIM), BF)] * len(asked),
        scratch_shapes=[pltpu.VMEM((mem_len, 2 * HEAD_DIM), BF)],
        cost_estimate=SMALL,
        name="gather_rows",
    )(*asked, cache_keys, cache_values)


def turn(part, cosine, sine):
    return part * cosine + pltpu.roll(part, HEAD_DIM // 2, 1) * sine


def turn_back(part, cosine, sine):
    return part * cosine - pltpu.roll(part, HEAD_DIM // 2, 1) * sine


def project_body(
    tokens_ref, gain_ref, wq_ref, wk_ref, wv_ref, cos_ref, sin_ref, q_ref, k_ref, v_ref, n_ref
):
    length = tokens_ref.shape[0]
    width = wq_ref.shape[1]
    tile = min(SUB, length)

    @pl.when(pl.program_id(0) == 0)
    def _():
        for start in range(0, length, tile):
            rows = slice(start, start + tile)
            x = tokens_ref[rows].astype(F32)
            scale = lax.rsqrt(jnp.mean(x * x, axis=-1, keepdims=True) + EPS)
            n_ref[rows] = (x * scale * gain_ref[...]).astype(BF)

    for start in range(0, length, tile):
        rows = slice(start, start + tile)
        x = n_ref[rows]
        cosine, sine = cos_ref[rows], sin_ref[rows]
        for w_ref, o_ref in ((wq_ref, q_ref), (wk_ref, k_ref)):
            full = dot(x, w_ref[...], 1, 0)
            for at in range(0, width, HEAD_DIM):
                cols = slice(at, at + HEAD_DIM)
                o_ref[rows, cols] = turn(full[:, cols], cosine, sine).astype(BF)
        v_ref[rows] = dot(x, wv_ref[...], 1, 0).astype(BF)


def project(tokens, gain, wq, wk, wv, cosine, sine):
    length, dim = tokens.shape
    cols = wq.shape[1]
    width = 2 * HEAD_DIM if cols % (2 * HEAD_DIM) == 0 else HEAD_DIM
    whole = lambda shape: pl.BlockSpec(shape, lambda g: (0, 0))
    return pl.pallas_call(
        project_body,
        grid=(cols // width,),
        in_specs=[whole((length, dim)), whole((1, dim))]
        + [pl.BlockSpec((dim, width), lambda g: (0, g))] * 3
        + [whole((length, HEAD_DIM))] * 2,
        out_specs=[pl.BlockSpec((length, width), lambda g: (0, g))] * 3 + [whole((length, dim))],
        out_shape=[jax.ShapeDtypeStruct((length, cols), BF)] * 3
        + [jax.ShapeDtypeStruct((length, dim), BF)],
        cost_estimate=SMALL,
        name="project",
    )(tokens, gain, wq, wk, wv, cosine, sine)


def window(start, size):
    return max(0, start - DOC_MOST), start + size


def make_bias(bias_ref, index, doc_row_ref, doc_col_ref, row0, start, size):
    low, high = window(row0 + start, size)
    at_query = lax.broadcasted_iota(jnp.int32, (size, high - low), 0) + (row0 + start)
    at_key = lax.broadcasted_iota(jnp.int32, (size, high - low), 1) + low
    same = doc_row_ref[:, low:high] == doc_col_ref[start : start + size]
    bias_ref[index, :, : high - low] = jnp.where(same & (at_key <= at_query), 0.0, NEG)


def forward_body(row0, far_count, *refs):
    q_ref, k_ref, v_ref, doc_row_ref, doc_col_ref = refs[:5]
    far_refs = refs[5 : 5 + far_count]
    outs = refs[5 + far_count :]
    o_ref, lse_ref = outs[:2]
    far_ref = outs[2] if far_count else None
    bias_ref = outs[-1]
    count = q_ref.shape[0]
    size = min(SUB, count)
    scale = 1.0 / math.sqrt(HEAD_DIM)

    @pl.when(pl.program_id(0) == 0)
    def _():
        for index, start in enumerate(range(0, count, size)):
            make_bias(bias_ref, index, doc_row_ref, doc_col_ref, row0, start, size)

    if far_count:
        total = far_refs[0][0]
        for other in far_refs[1:]:
            total = total + other[0]
        far_ref[0] = total
    for index, start in enumerate(range(0, count, size)):
        low, high = window(row0 + start, size)
        rows = slice(start, start + size)
        q = q_ref[rows]
        s = dot(q, k_ref[low:high], 1, 1) * scale + bias_ref[index, :, : high - low]
        m = jnp.max(s, axis=1, keepdims=True)
        if far_count:
            far_bias = jnp.where(doc_col_ref[rows] == doc_row_ref[:, 0:1], 0.0, NEG)
            sf = jnp.concatenate(
                [
                    dot(
                        q[at : at + PICK_BLOCK],
                        far_ref[0, start + at : start + at + PICK_BLOCK, :HEAD_DIM],
                        1,
                        1,
                    )
                    for at in range(0, size, PICK_BLOCK)
                ],
                axis=0,
            )
            sf = sf * scale + far_bias
            m = jnp.maximum(m, jnp.max(sf, axis=1, keepdims=True))
        p = jnp.exp(s - m)
        total = jnp.sum(p, axis=1, keepdims=True)
        o = dot(p.astype(BF), v_ref[low:high], 1, 0)
        if far_count:
            pf = jnp.exp(sf - m)
            total = total + jnp.sum(pf, axis=1, keepdims=True)
            pf = pf.astype(BF)
            o = o + jnp.concatenate(
                [
                    dot(
                        pf[at : at + PICK_BLOCK],
                        far_ref[0, start + at : start + at + PICK_BLOCK, HEAD_DIM:],
                        1,
                        0,
                    )
                    for at in range(0, size, PICK_BLOCK)
                ],
                axis=0,
            )
        o_ref[rows] = (o / total).astype(BF)
        lse_ref[0, rows] = m + jnp.log(total)


def attend_forward(q, k, v, doc_row, doc_col, row0, count, far):
    heads = q.shape[1] // HEAD_DIM
    seg_len = q.shape[0]
    high = row0 + count
    at = row0 // count
    size = min(SUB, count)
    wide = max(w[1] - w[0] for w in (window(row0 + s, size) for s in range(0, count, size)))
    key_spec = pl.BlockSpec((high, HEAD_DIM), lambda h: (0, h))
    far_spec = pl.BlockSpec((1, count, 2 * HEAD_DIM), lambda h: (h, 0, 0))
    far_shape = jax.ShapeDtypeStruct((heads, count, 2 * HEAD_DIM), BF)
    return pl.pallas_call(
        functools.partial(forward_body, row0, len(far)),
        grid=(heads,),
        in_specs=[
            pl.BlockSpec((count, HEAD_DIM), lambda h: (at, h)),
            key_spec,
            key_spec,
            pl.BlockSpec((1, seg_len), lambda h: (0, 0)),
            pl.BlockSpec((count, 1), lambda h: (at, 0)),
        ]
        + [far_spec] * len(far),
        out_specs=[
            pl.BlockSpec((count, HEAD_DIM), lambda h: (0, h)),
            pl.BlockSpec((1, count, 1), lambda h: (h, 0, 0)),
        ]
        + [far_spec] * bool(far),
        out_shape=[
            jax.ShapeDtypeStruct((count, heads * HEAD_DIM), BF),
            jax.ShapeDtypeStruct((heads, count, 1), F32),
        ]
        + [far_shape] * bool(far),
        scratch_shapes=[pltpu.VMEM((count // size, size, wide), F32)],
        cost_estimate=SMALL,
        name="attend_forward",
    )(q, k, v, doc_row, doc_col, *far)


def backward_body(row0, far_on, *refs):
    (
        q_ref,
        k_ref,
        v_ref,
        doc_row_ref,
        doc_col_ref,
        o_ref,
        do_ref,
        lse_ref,
        cos_ref,
        sin_ref,
    ) = refs[:10]
    rest = list(refs[10:])
    if far_on:
        far_ref = rest.pop(0)
    if row0 == 0:
        add_k_ref, add_v_ref = rest.pop(0), rest.pop(0)
    grad_ref = rest[0]
    heads = grad_ref.shape[1] // (3 * HEAD_DIM)
    dq_ref, dk_ref, dv_ref = (
        grad_ref.at[
            :, pl.ds(pl.multiple_of((i * heads + pl.program_id(0)) * HEAD_DIM, HEAD_DIM), HEAD_DIM)
        ]
        for i in range(3)
    )
    if row0:
        low_k_ref, low_v_ref = rest[1:3]
    bias_ref, acc_k_ref, acc_v_ref = rest[-3:]
    count = q_ref.shape[0]
    size = min(SUB, count)
    scale = 1.0 / math.sqrt(HEAD_DIM)

    @pl.when(pl.program_id(0) == 0)
    def _():
        for index, start in enumerate(range(0, count, size)):
            make_bias(bias_ref, index, doc_row_ref, doc_col_ref, row0, start, size)

    if row0:
        acc_k_ref[...] = jnp.zeros(acc_k_ref.shape, F32)
        acc_v_ref[...] = jnp.zeros(acc_v_ref.shape, F32)
    else:
        acc_k_ref[...] = add_k_ref[...]
        acc_v_ref[...] = add_v_ref[...]
    for index, start in enumerate(range(0, count, size)):
        low, high = window(row0 + start, size)
        rows = slice(start, start + size)
        q, do, lse = q_ref[rows], do_ref[rows], lse_ref[0, rows]
        delta = jnp.sum(do.astype(F32) * o_ref[rows].astype(F32), axis=1, keepdims=True)
        keys, values = k_ref[low:high], v_ref[low:high]
        p = jnp.exp(dot(q, keys, 1, 1) * scale + bias_ref[index, :, : high - low] - lse)
        ds = (p * (dot(do, values, 1, 1) - delta)).astype(BF)
        acc_v_ref[low:high] += dot(p.astype(BF), do, 0, 0)
        acc_k_ref[low:high] += dot(ds, q, 0, 0)
        dq = dot(ds, keys, 1, 0)
        if far_on:
            far_bias = jnp.where(doc_col_ref[rows] == doc_row_ref[:, 0:1], 0.0, NEG) - lse
            parts = []
            for at in range(0, size, PICK_BLOCK):
                cut = slice(at, at + PICK_BLOCK)
                far_keys = far_ref[0, start + at : start + at + PICK_BLOCK, :HEAD_DIM]
                far_values = far_ref[0, start + at : start + at + PICK_BLOCK, HEAD_DIM:]
                pf = jnp.exp(dot(q[cut], far_keys, 1, 1) * scale + far_bias[cut])
                dsf = (pf * (dot(do[cut], far_values, 1, 1) - delta[cut])).astype(BF)
                parts.append(dot(dsf, far_keys, 1, 0))
            dq = dq + jnp.concatenate(parts, axis=0)
        at_rows = slice(row0 + start, row0 + start + size)
        dq_ref[rows] = turn_back(dq * scale, cos_ref[at_rows], sin_ref[at_rows]).astype(BF)
    dv_ref[...] = acc_v_ref[row0 : row0 + count].astype(BF)
    dk_ref[...] = turn_back(
        acc_k_ref[row0 : row0 + count] * scale,
        cos_ref[row0 : row0 + count],
        sin_ref[row0 : row0 + count],
    ).astype(BF)
    if row0:
        low_k_ref[...] = acc_k_ref[:row0]
        low_v_ref[...] = acc_v_ref[:row0]


def attend_backward(
    q, k, v, doc_row, doc_col, out, grad_out, lse, cosine, sine, row0, count, far, low
):
    heads = q.shape[1] // HEAD_DIM
    seg_len = q.shape[0]
    high = row0 + count
    at = row0 // count
    size = min(SUB, count)
    wide = max(w[1] - w[0] for w in (window(row0 + s, size) for s in range(0, count, size)))
    head_cols = lambda n: pl.BlockSpec((n, HEAD_DIM), lambda h: (0, h))
    whole = lambda n, m: pl.BlockSpec((n, m), lambda h: (0, 0))
    in_specs = [
        pl.BlockSpec((count, HEAD_DIM), lambda h: (at, h)),
        head_cols(high),
        head_cols(high),
        whole(1, seg_len),
        pl.BlockSpec((count, 1), lambda h: (at, 0)),
        head_cols(count),
        head_cols(count),
        pl.BlockSpec((1, count, 1), lambda h: (h, 0, 0)),
        whole(high, HEAD_DIM),
        whole(high, HEAD_DIM),
    ]
    args = [q, k, v, doc_row, doc_col, out, grad_out, lse, cosine, sine]
    if far is not None:
        in_specs.append(pl.BlockSpec((1, count, 2 * HEAD_DIM), lambda h: (h, 0, 0)))
        args.append(far)
    if row0 == 0:
        in_specs += [head_cols(count)] * 2
        args += list(low)
    out_specs = [whole(count, 3 * heads * HEAD_DIM)]
    out_shape = [jax.ShapeDtypeStruct((count, 3 * heads * HEAD_DIM), BF)]
    if row0:
        out_specs += [head_cols(row0)] * 2
        out_shape += [jax.ShapeDtypeStruct((row0, heads * HEAD_DIM), F32)] * 2
    return pl.pallas_call(
        functools.partial(backward_body, row0, far is not None),
        grid=(heads,),
        in_specs=in_specs,
        out_specs=out_specs,
        out_shape=out_shape,
        scratch_shapes=[
            pltpu.VMEM((count // size, size, wide), F32),
            pltpu.VMEM((high, HEAD_DIM), F32),
            pltpu.VMEM((high, HEAD_DIM), F32),
        ],
        cost_estimate=COVER,
        name="attend_backward",
    )(*args)


def bit_of(bit):
    return (lax.axis_index("seg") >> bit) & 1


def half_rows(part, which):
    size = part.shape[0] // 2
    return lax.dynamic_slice_in_dim(part, which * size, size)


def z_of():
    return lax.axis_index("seg") >> 2


def z_swap(block, shift):
    count = lax.axis_size("seg")
    return lax.ppermute(block, "seg", [(i, i ^ (shift << 2)) for i in range(count)])


def split_body(at_ref, part_ref, got_ref, *out_refs):
    total = (part_ref[...].astype(F32) + got_ref[...].astype(F32)).astype(BF)
    for shift, out_ref in enumerate(out_refs):

        @pl.when(pl.program_id(0) == shift)
        def _():
            out_ref[...] = total


def split_z(part, got, bit):
    rows, cols = got.shape[0] // 4, got.shape[1]
    return pl.pallas_call(
        split_body,
        grid_spec=pltpu.PrefetchScalarGridSpec(
            num_scalar_prefetch=1,
            grid=(4,),
            in_specs=[
                pl.BlockSpec((rows, cols), lambda s, at: (4 * at[0] + (at[1] ^ s), 0)),
                pl.BlockSpec((rows, cols), lambda s, at: (at[1] ^ s, 0)),
            ],
            out_specs=[pl.BlockSpec((rows, cols), lambda s, at: (0, 0))] * 4,
        ),
        out_shape=[jax.ShapeDtypeStruct((rows, cols), BF)] * 4,
        cost_estimate=SMALL,
        name="split_z",
    )(jnp.stack([bit_of(bit), z_of()]), part, got)


def join_body(at_ref, *refs):
    for shift, ref in enumerate(refs[:-1]):

        @pl.when(pl.program_id(0) == shift)
        def _():
            refs[-1][...] = ref[...]


def join_z(parts):
    rows, cols = parts[0].shape
    return pl.pallas_call(
        join_body,
        grid_spec=pltpu.PrefetchScalarGridSpec(
            num_scalar_prefetch=1,
            grid=(4,),
            in_specs=[pl.BlockSpec((rows, cols), lambda s, at: (0, 0))] * 4,
            out_specs=pl.BlockSpec((rows, cols), lambda s, at: (at[0] ^ s, 0)),
        ),
        out_shape=jax.ShapeDtypeStruct((4 * rows, cols), BF),
        cost_estimate=SMALL,
        name="join_z",
    )(z_of().reshape(1), *parts)


def double_body(mine_ref, part_ref, got_ref, out_ref):
    rows = part_ref.shape[0]
    for mine in (0, 1):

        @pl.when(mine_ref[0] == mine)
        def _():
            out_ref[mine * rows : (mine + 1) * rows] = part_ref[...]
            out_ref[(1 - mine) * rows : (2 - mine) * rows] = got_ref[...]


def double(part, got, bit):
    rows, cols = part.shape
    return pl.pallas_call(
        double_body,
        in_specs=[pl.BlockSpec(memory_space=pltpu.SMEM)] + [pl.BlockSpec((rows, cols))] * 2,
        out_specs=pl.BlockSpec((2 * rows, cols)),
        out_shape=jax.ShapeDtypeStruct((2 * rows, cols), BF),
        cost_estimate=SMALL,
        name="double",
    )(bit_of(bit).reshape(1), part, got)


def close_body(mine_ref, part_ref, got_ref, *out_refs):
    width = part_ref.shape[1] // len(out_refs)
    for owner, ref in ((0, part_ref), (1, got_ref)):

        @pl.when((pl.program_id(0) == mine_ref[0]) == (owner == 0))
        def _():
            for i, out_ref in enumerate(out_refs):
                out_ref[...] = ref[:, i * width : (i + 1) * width].astype(F32)


def double_out(part, got, bit, pieces=1, fold=False):
    rows, cols = part.shape
    width = cols // pieces
    full = pl.BlockSpec((rows, cols), lambda h, mine: (0, 0))
    specs = [pl.BlockSpec((rows, width), lambda h, mine: (h, 0))] * pieces
    shapes = [jax.ShapeDtypeStruct((2 * rows, width), F32)] * pieces
    if fold:
        specs[-1] = pl.BlockSpec((rows, width), lambda h, mine: (0, h))
        shapes[-1] = jax.ShapeDtypeStruct((rows, 2 * width), F32)
    return pl.pallas_call(
        close_body,
        grid_spec=pltpu.PrefetchScalarGridSpec(
            num_scalar_prefetch=1, grid=(2,), in_specs=[full, full], out_specs=specs
        ),
        out_shape=shapes,
        cost_estimate=SMALL,
        name="double_out",
    )(bit_of(bit).reshape(1), part, got)


def attention_grads_body(n_a, n_b, j_a, j_b, o_a, o_b, g_a, g_b, out_ref):
    cols = g_a.shape[1]
    joint = (dot(n_a[...], j_a[...], 0, 0) + dot(n_b[...], j_b[...], 0, 0)).astype(BF)
    out_ref[:, : 3 * cols] = joint
    out_ref[:, 3 * cols :] = (
        dot(o_a[...], g_a[...], 0, 0) + dot(o_b[...], g_b[...], 0, 0)
    ).astype(BF)


def attention_grads(normed, joint_a, joint_b, att_a, att_b, grad_a, grad_b):
    dim = normed.shape[1]
    count, width = joint_a.shape
    cols = att_a.shape[1]
    tile = min(SUB, cols)
    folds = cols // tile
    cut = lambda chunk: pl.BlockSpec((count, tile), lambda i: (chunk, i))
    joint = pl.BlockSpec((count, width), lambda i: (0, 0))
    att = pl.BlockSpec((count, tile), lambda i: (0, i % folds))
    grad = pl.BlockSpec((count, cols), lambda i: (0, i // folds))
    return pl.pallas_call(
        attention_grads_body,
        grid=(dim // tile,),
        in_specs=[cut(0), cut(1), joint, joint, att, att, grad, grad],
        out_specs=pl.BlockSpec((tile, width + cols), lambda i: (i, 0)),
        out_shape=jax.ShapeDtypeStruct((dim, width + cols), BF),
        cost_estimate=COVER,
        name="attention_grads",
    )(normed, normed, joint_a, joint_b, att_a, att_b, grad_a, grad_b)


def rows_dot_body(a_ref, b_ref, out_ref):
    out_ref[...] = dot(a_ref[...], b_ref[...], 1, 0).astype(BF)


def rows_dot(a, b):
    rows, depth = a.shape
    cols = b.shape[1]
    tile = 2 * SUB if cols % (2 * SUB) == 0 else cols
    return pl.pallas_call(
        rows_dot_body,
        grid=(cols // tile,),
        in_specs=[
            pl.BlockSpec((rows, depth), lambda j: (0, 0)),
            pl.BlockSpec((depth, tile), lambda j: (0, j)),
        ],
        out_specs=pl.BlockSpec((rows, tile), lambda j: (0, j)),
        out_shape=jax.ShapeDtypeStruct((rows, cols), BF),
        cost_estimate=SMALL,
        name="rows_dot",
    )(a, b)


def chunk_specs(count, tile, dim):
    steps = count // tile
    first = pl.BlockSpec((tile, dim), lambda g: (jnp.minimum(g, steps - 1), 0))
    second = pl.BlockSpec((tile, dim), lambda g: (jnp.maximum(g - steps, 0), 0))
    return steps, first, second


def output_body(steps, *refs):
    for chunk in (0, 1):
        hidden_ref, mine_ref, got_ref = refs[3 * chunk : 3 * chunk + 3]

        @pl.when((pl.program_id(0) < steps) == (chunk == 0))
        def _():
            total = mine_ref[...].astype(F32) + got_ref[...].astype(F32)
            refs[-1][...] = (hidden_ref[...] + total).astype(BF)


def output_rows(early, late):
    count, dim = early[0].shape
    tile = min(SUB, count)
    steps, first, second = chunk_specs(count, tile, dim)
    return pl.pallas_call(
        functools.partial(output_body, steps),
        grid=(2 * steps,),
        in_specs=[first] * 3 + [second] * 3,
        out_specs=pl.BlockSpec((tile, dim), lambda g: (g, 0)),
        out_shape=jax.ShapeDtypeStruct((2 * count, dim), BF),
        cost_estimate=SMALL,
        name="output_rows",
    )(*early, *late)


def norm_one_body(steps, x_ref, gain_ref, *refs):
    out_ref, grad_gain_ref = refs[-2:]

    @pl.when(pl.program_id(0) == 0)
    def _():
        grad_gain_ref[...] = jnp.zeros(grad_gain_ref.shape, F32)

    for chunk in (0, 1):
        total_ref, mine_ref, got_ref = refs[3 * chunk : 3 * chunk + 3]

        @pl.when((pl.program_id(0) < steps) == (chunk == 0))
        def _():
            x = x_ref[...].astype(F32)
            grad = mine_ref[...].astype(F32) + got_ref[...].astype(F32)
            scale = lax.rsqrt(jnp.mean(x * x, axis=-1, keepdims=True) + EPS)
            weighted = grad * gain_ref[...]
            inner = jnp.mean(weighted * x, axis=-1, keepdims=True)
            rows = scale * weighted - x * (scale * scale * scale * inner)
            out_ref[...] = (total_ref[...] + rows).astype(BF)
            grad_gain_ref[...] += jnp.sum(grad * x * scale, axis=0, keepdims=True)


def norm_one_rows(tokens, gain, early, late):
    count, dim = early[0].shape
    tile = min(SUB, count)
    steps, first, second = chunk_specs(count, tile, dim)
    rows = pl.BlockSpec((tile, dim), lambda g: (g, 0))
    line = pl.BlockSpec((1, dim), lambda g: (0, 0))
    return pl.pallas_call(
        functools.partial(norm_one_body, steps),
        grid=(2 * steps,),
        in_specs=[rows, line] + [first] * 3 + [second] * 3,
        out_specs=[rows, line],
        out_shape=[
            jax.ShapeDtypeStruct((2 * count, dim), BF),
            jax.ShapeDtypeStruct((1, dim), F32),
        ],
        cost_estimate=SMALL,
        name="norm_one_rows",
    )(tokens, gain, *early, *late)


def shards(
    tokens,
    document_ids,
    memory_picks,
    partner_ids,
    memory_keys,
    memory_values,
    first_gain,
    query_weight,
    key_weight,
    value_weight,
    out_weight,
    second_gain,
    gate_weight,
    up_weight,
    down_weight,
    cotangent,
):
    seg_len = document_ids.shape[1]
    heads = query_weight.shape[1] // HEAD_DIM
    mem_len = memory_keys.shape[1]
    blocks = memory_picks.shape[2]
    near = min(blocks, DOC_MOST // PICK_BLOCK)
    chunk = near * PICK_BLOCK
    me = lax.axis_index("seg")
    bits = lax.axis_size("seg").bit_length() - 1
    partner = partner_ids[0]
    paired = lax.axis_size("head") == 2

    ranks = rank_picks(memory_picks.reshape(heads * blocks, 2 * mem_len))
    ranks = ranks.reshape(heads, blocks, 2 * mem_len)[:, :near]
    first_len = jnp.sum((document_ids[0] == document_ids[0, 0]).astype(jnp.int32))
    used = (jnp.arange(near) * PICK_BLOCK < first_len)[None, :, None]
    ranks = jnp.where(used, ranks, 0)
    own_ranks, far_ranks = ranks[:, :, :mem_len], ranks[:, :, mem_len:]
    asked = [own_ranks]
    for bit in range(bits):
        wanted = partner == jnp.bitwise_xor(me, 1 << bit)
        asked.append(swap(jnp.where(wanted, far_ranks, jnp.zeros_like(far_ranks)), bit))

    cosine, sine = rope_tables(seg_len)
    doc_row = document_ids
    doc_col = document_ids.reshape(seg_len, 1)
    dim = tokens.shape[1]
    token = [first_gain]

    def order(*values):
        values, token[0] = lax.optimization_barrier((values, token[0]))
        return values

    exchange = lambda mine: head_swap(mine) if paired else lax.psum(mine, "head")
    mine_of = lambda mine: mine if paired else jnp.zeros_like(mine)
    full = lambda mine, got: mine_of(mine).astype(F32) + got.astype(F32)

    q, k, v, normed_one = project(
        tokens, first_gain.reshape(1, -1), query_weight, key_weight, value_weight, cosine, sine
    )
    out_got = head_swap(out_weight) if paired else None
    joint_weight = jnp.concatenate([query_weight, key_weight, value_weight], axis=1)

    far = [None] * (bits + 1)
    split = max(1, bits - 2)

    def send_rows(slots):
        ranks = order(*(asked[slot] for slot in slots))
        rows = order(*gather_rows(list(ranks), memory_keys[0], memory_values[0]))
        for slot, block in zip(slots, rows):
            far[slot] = swap(block, slot - 1) if slot else block

    q, *asked = order(q, *asked)
    send_rows(range(bits, split, -1))

    def start_mix(st):
        (st.att,) = order(st.att)
        if paired:
            st.got_att = head_swap(st.att)

    def mix(st):
        if paired:
            (got,) = order(st.got_att)
            joined = head_join(st.att, got, 1)
            return jnp.dot(joined, out_full, preferred_element_type=F32)
        return head_sum(jnp.dot(st.att, out_weight, preferred_element_type=F32).astype(BF))

    def feed(st, cut):
        st.hidden_in = tokens[cut].astype(F32) + st.mixed
        st.scale = rms_scale(st.hidden_in)
        normed_two = (st.hidden_in * st.scale * second_gain).astype(BF)
        gate = jnp.dot(normed_two, gate_weight, preferred_element_type=F32)
        upper = jnp.dot(normed_two, up_weight, preferred_element_type=F32)
        sigmoid_gate = jax.nn.sigmoid(gate)
        grad_hidden = dot(cotangent[cut], down_weight, 1, 1)
        st.hidden = (gate * sigmoid_gate * upper).astype(BF)
        st.grad_gate = (
            grad_hidden * upper * sigmoid_gate * (1.0 + gate * (1.0 - sigmoid_gate))
        ).astype(BF)
        st.grad_upper = (grad_hidden * gate * sigmoid_gate).astype(BF)
        st.normed_two = normed_two
        st.part_two = (
            dot(st.grad_gate, gate_weight, 1, 1) + dot(st.grad_upper, up_weight, 1, 1)
        ).astype(BF)

    def feed_grads(st, cut):
        return (
            dot(st.hidden, cotangent[cut], 0, 0),
            dot(
                st.normed_two,
                jnp.concatenate([st.grad_gate, st.grad_upper], axis=1),
                0,
                0,
            ),
        )

    def feed_out(st):
        down_part = jnp.dot(st.hidden, down_weight, preferred_element_type=F32)
        st.output = (st.hidden_in + head_sum(down_part.astype(BF))).astype(BF)

    def norm_two(st, cut):
        rows, st.second_gain_grad = norm_backward(
            st.grad_normed_two, st.hidden_in, st.scale, second_gain
        )
        st.total_grad = cotangent[cut].astype(F32) + rows
        st.grad_mixed = st.total_grad.astype(BF)
        st.grad_att = dot(st.grad_mixed, out_weight, 1, 1).astype(BF)

    def back(st, row0, low):
        parts = attend_backward(
            q, k, v, doc_row, doc_col, st.att, st.grad_att, st.lse, cosine, sine,
            row0, chunk, getattr(st, "far", None), low,
        )
        st.joint = parts[0]
        return parts[1:]

    late, early = slice(chunk, 2 * chunk), slice(0, chunk)
    b, a = SimpleNamespace(), SimpleNamespace()
    (q,) = order(q)
    b.att, b.lse = attend_forward(q, k, v, doc_row, doc_col, chunk, chunk, [])
    if paired:
        (out_got,) = order(out_got)
        out_full = head_join(out_weight, out_got, 0)
    start_mix(b)
    send_rows([0, *range(1, split + 1)])
    b.mixed = mix(b)
    feed(b, late)
    (b.part_two,) = order(b.part_two)
    b.got_two = exchange(b.part_two)
    far_hi = order(*far[split + 1 :])
    *b_grads, joint_weight = order(*feed_grads(b, late), joint_weight)
    far = order(*far[: split + 1]) + far_hi
    a.att, a.lse, a.far = attend_forward(q, k, v, doc_row, doc_col, 0, chunk, list(far))
    start_mix(a)
    (got,) = order(b.got_two)
    b.grad_normed_two = full(b.part_two, got)
    norm_two(b, late)
    (b.grad_att,) = order(b.grad_att)
    low = back(b, chunk, None)
    b.joint, *low = order(b.joint, *low)
    a.mixed = mix(a)
    feed(a, early)

    plan = []

    def at(time):
        return lambda step: plan.append((time, step))

    def piece(make_time, make, times, close):
        st = SimpleNamespace()
        starts, ends = times[0::2], times[1::2]

        def step(i, begin, end):
            @at(starts[i])
            def _():
                st.sent = order(*st.send)
                st.got = begin(st.sent)

            @at(ends[i])
            def _():
                end(order(*st.got))

        def core_half(got):
            keep = half_rows(st.part, bit_of(0))
            st.part = (keep.astype(F32) + got[0].astype(F32)).astype(BF)
            st.send = (half_rows(st.part, 1 - bit_of(1)),)

        def y_half(got):
            own, *st.send = split_z(st.part, got[0], 1)
            st.part = own

        def z_sum(got):
            total = sum((part.astype(F32) for part in got), st.part.astype(F32))
            st.part = total.astype(BF)
            st.send = (st.part,)

        def z_join(got):
            st.part = join_z([st.part, *got])
            st.send = (st.part,)

        def y_double(got):
            st.part = double(st.part, got[0], 1)
            st.send = (st.part,)

        @at(make_time)
        def _():
            (st.part,) = order(make())
            st.send = (half_rows(st.part, 1 - bit_of(0)),)

        one = lambda bit: lambda send: (swap(send[0], bit),)
        step(0, one(0), core_half)
        step(1, one(1), y_half)
        step(2, lambda send: tuple(z_swap(send[i], i + 1) for i in range(3)), z_sum)
        step(3, lambda send: tuple(z_swap(send[0], i + 1) for i in range(3)), z_join)
        step(4, one(1), y_double)
        step(5, one(0), lambda got: close(st.part, got[0]))
        return st

    done = SimpleNamespace()

    def close_as(*names, fold=False):
        def close(part, got):
            for name, value in zip(names, order(*double_out(part, got, 0, len(names), fold))):
                setattr(done, name, value)

        return close


    def make_down():
        (a.hidden,) = order(a.hidden)
        return (b_grads[0] + dot(a.hidden, cotangent[early], 0, 0)).astype(BF)

    def make_feed():
        a.grad_gate, a.grad_upper = order(a.grad_gate, a.grad_upper)
        return (b_grads[1] + feed_grads(a, early)[1]).astype(BF)

    joined = [make_down, make_feed]

    if paired and bits == 4:
        piece(
            194,
            joined[0],
            [198, 207, 208, 213.2, 213.3, 214.3, 214.4, 215.2, 219.135, 219.55, 219.65, 219.97],
            close_as("down"),
        )
        piece(
            199,
            joined[1],
            [206, 208.5, 208.6, 215.5, 215.6, 219, 219.1, 219.5, 219.6, 221.9, 221.95, 226],
            close_as("gate", "up"),
        )
        piece(
            215,
            lambda: attention_grads(
                normed_one, a.joint, b.joint, a.att, b.att,
                a.grad_mixed, b.grad_mixed,
            ),
            [215.7, 218, 218.02, 219.12, 219.14, 219.9, 219.95, 221, 221.1, 227, 227.1, 229],
            close_as("query", "key", "value", "out", fold=True),
        )
    else:

        @at(300)
        def _():
            total = lambda part: lax.psum(part.astype(BF), "seg").astype(F32)
            joint = dot(normed_one[late], b.joint, 0, 0)
            joint = total(joint + dot(normed_one[early], a.joint, 0, 0))
            done.query, done.key, done.value = jnp.split(joint, 3, axis=1)
            out = dot(b.att, b.grad_mixed, 0, 0) + dot(a.att, a.grad_mixed, 0, 0)
            done.out = total(out)
            done.down, both = (total(make()) for make in joined)
            done.gate, done.up = jnp.split(both, 2, axis=1)

    down = lambda st: rows_dot(order(st.hidden)[0], down_weight)
    back_part = lambda st: dot(order(st.joint)[0], joint_weight, 1, 1).astype(BF)
    @at(193)
    def _():
        (a.part_two,) = order(a.part_two)
        a.got_two = exchange(a.part_two)

    @at(208.7)
    def _():
        (b.down,) = order(down(b))

    @at(208.8)
    def _():
        (a.down,) = order(down(a))

    @at(209)
    def _():
        (got,) = order(a.got_two)
        a.grad_normed_two = full(a.part_two, got)

    sent, taken = {}, {}

    def head(key, send_time, part, take_time):
        @at(send_time)
        def _():
            (sent[key],) = order(part())
            taken[key] = exchange(sent[key])

        @at(take_time)
        def _():
            (taken[key],) = order(taken[key])

    head(0, 209.5, lambda: b.down, 214.5)
    head(1, 214.6, lambda: a.down, 218.03)
    head(2, 218.04, lambda: b.part_one, 219.13)
    head(3, 219.7, lambda: a.part_one, 220.2)

    @at(210)
    def _():
        norm_two(a, early)
        a.grad_att, a.grad_mixed = order(a.grad_att, a.grad_mixed)

    @at(214)
    def _():
        (a.grad_att,) = order(a.grad_att)
        back(a, 0, low)
        (a.joint,) = order(a.joint)

    @at(215.3)
    def _():
        (b.part_one,) = order(back_part(b))

    @at(218.05)
    def _():
        (a.part_one,) = order(back_part(a))

    rest = SimpleNamespace()

    @at(219.2)
    def _():
        (rest.output,) = order(
            output_rows(
                *(
                    (st.hidden_in, mine_of(sent[key]), taken[key])
                    for st, key in ((a, 1), (b, 0))
                )
            )
        )

    @at(220.3)
    def _():
        rest.tokens_grad, first_gain_grad = order(
            *norm_one_rows(
                tokens,
                token[0].reshape(1, -1),
                *(
                    (st.total_grad, mine_of(sent[key]), taken[key])
                    for st, key in ((a, 3), (b, 2))
                ),
            )
        )
        second = (a.second_gain_grad + b.second_gain_grad).reshape(1, -1)
        token[0] = jnp.concatenate([first_gain_grad, second], axis=0)

    gain_bits = [0, *range(2, bits), 1]
    gain_times = [(220.4, 220.6), (221.2, 221.5), (221.6, 222.2), (222.3, 227.5), (227.6, 227.7)]
    for bit, (start, end) in zip(gain_bits, gain_times):

        @at(start)
        def _(bit=bit):
            done.gains_got = swap(token[0], bit)

        @at(end)
        def _():
            (got,) = order(done.gains_got)
            token[0] = token[0] + got

    for _, step in sorted(plan, key=lambda entry: entry[0]):
        step()
    gains = token[0]
    return (
        rest.output,
        rest.tokens_grad,
        gains[0],
        done.query,
        done.key,
        done.value,
        done.out,
        gains[1],
        done.gate,
        done.up,
        done.down,
    )


def solution(mesh):
    placed = (
        P("seg", None),
        P("seg", None),
        P("seg", "head", None, None),
        P("seg"),
        P("seg", None, "head"),
        P("seg", None, "head"),
        P(),
        P(None, "head"),
        P(None, "head"),
        P(None, "head"),
        P("head", None),
        P(),
        P(None, "head"),
        P(None, "head"),
        P("head", None),
        P("seg", None),
    )
    return jax.shard_map(
        shards,
        mesh=mesh,
        in_specs=placed,
        out_specs=(
            P("seg", None),
            P("seg", None),
            P(),
            P(None, "head"),
            P(None, "head"),
            P(None, "head"),
            P("head", None),
            P(),
            P(None, "head"),
            P(None, "head"),
            P("head", None),
        ),
        check_vma=False,
    )
```

```python
import functools
import math
from types import SimpleNamespace

import jax
import jax.numpy as jnp
from jax import lax
from jax.experimental import pallas as pl
from jax.experimental.pallas import tpu as pltpu
from jax.sharding import PartitionSpec as P

HEAD_DIM = 128
KPICK = 128
PICK_BLOCK = 128
DOC_MOST = 512
SUB = 256

EPS = 1e-05
NEG = -1e30
THETA = 10000.0
SMALL = pl.CostEstimate(flops=1, bytes_accessed=1, transcendentals=0)
COVER = pl.CostEstimate(flops=4 * 10**9, bytes_accessed=14 * 10**6, transcendentals=0)
BF = jnp.bfloat16
F32 = jnp.float32


def dot(a, b, ca, cb):
    return lax.dot_general(a, b, (((ca,), (cb,)), ((), ())), preferred_element_type=F32)


def swap(block, bit):
    count = lax.axis_size("seg")
    return lax.ppermute(block, "seg", [(i, i ^ (1 << bit)) for i in range(count)])


def head_swap(block):
    return lax.ppermute(block, "head", [(0, 1), (1, 0)])


def head_sum(part):
    if lax.axis_size("head") == 2:
        return part.astype(F32) + head_swap(part).astype(F32)
    return lax.psum(part, "head").astype(F32)


def head_join(mine, got, axis):
    first = lax.axis_index("head") == 0
    return jnp.concatenate(
        [jnp.where(first, mine, got), jnp.where(first, got, mine)], axis=axis
    )


def rope_tables(length):
    half_dim = HEAD_DIM // 2
    position = jnp.arange(length, dtype=F32)[:, None]
    frequency = THETA ** (-jnp.arange(half_dim, dtype=F32) / half_dim)
    angles = position * frequency[None, :]
    cosine, sine = jnp.cos(angles), jnp.sin(angles)
    return (
        jnp.concatenate([cosine, cosine], axis=1),
        jnp.concatenate([-sine, sine], axis=1),
    )


def rms_scale(token_rows):
    return lax.rsqrt(jnp.mean(token_rows * token_rows, axis=-1, keepdims=True) + EPS)


def norm_backward(grad_normed, token_rows, row_scale, gain_vec):
    weighted = grad_normed * gain_vec
    inner_mean = jnp.mean(weighted * token_rows, axis=-1, keepdims=True)
    grad_rows = row_scale * weighted - token_rows * row_scale**3 * inner_mean
    grad_gain = jnp.sum(grad_normed * token_rows * row_scale, axis=0)
    return (grad_rows, grad_gain)


def rank_body(picks_ref, out_ref):
    rows, cache_len = picks_ref.shape
    at_row = lax.broadcasted_iota(jnp.int32, (128, 256), 0)
    at_col = lax.broadcasted_iota(jnp.int32, (128, 256), 1)
    table = jnp.where((at_row <= at_col) | (at_col >= 128), 1.0, 0.0).astype(BF)
    carry = jnp.zeros((rows, 128), F32)
    for chunk in range(cache_len // 128):
        cols = slice(chunk * 128, (chunk + 1) * 128)
        picked = picks_ref[:, cols].astype(F32)
        sums = dot(picked.astype(BF), table, 1, 0)
        out_ref[:, cols] = ((sums[:, :128] + carry) * picked).astype(BF)
        carry = carry + sums[:, 128:]


def rank_picks(picks):
    rows, cache_len = picks.shape
    return pl.pallas_call(
        rank_body,
        out_shape=jax.ShapeDtypeStruct((rows, cache_len), BF),
        cost_estimate=SMALL,
        name="rank_picks",
    )(picks)


def gather_body(*refs):
    asks = (len(refs) - 3) // 2
    keys_ref, values_ref = refs[asks], refs[asks + 1]
    out_refs = refs[asks + 2 : -1]
    table_ref = refs[-1]
    table_ref[:, :HEAD_DIM] = keys_ref[...]
    table_ref[:, HEAD_DIM:] = values_ref[...]
    blocks, mem_len = refs[0].shape[1], refs[0].shape[2]
    slot = lax.broadcasted_iota(jnp.int32, (KPICK, mem_len), 0).astype(F32) + 1.0
    for ask_ref, out_ref in zip(refs[:asks], out_refs):
        ranks = ask_ref[0].astype(F32)
        wanted = jnp.max(ranks) > 0.0

        @pl.when(wanted)
        def _():
            chosen = jnp.concatenate(
                [
                    jnp.where(ranks[block : block + 1] == slot, 1.0, 0.0).astype(BF)
                    for block in range(blocks)
                ],
                axis=0,
            )
            out_ref[0] = dot(chosen, table_ref[...], 1, 0).astype(BF)

        @pl.when(jnp.logical_not(wanted))
        def _():
            out_ref[0] = jnp.zeros(out_ref.shape[1:], BF)


def gather_rows(asked, cache_keys, cache_values):
    heads, blocks, mem_len = asked[0].shape
    return pl.pallas_call(
        gather_body,
        grid=(heads,),
        in_specs=[pl.BlockSpec((1, blocks, mem_len), lambda h: (h, 0, 0))] * len(asked)
        + [pl.BlockSpec((mem_len, HEAD_DIM), lambda h: (0, h))] * 2,
        out_specs=[pl.BlockSpec((1, blocks * KPICK, 2 * HEAD_DIM), lambda h: (h, 0, 0))]
        * len(asked),
        out_shape=[jax.ShapeDtypeStruct((heads, blocks * KPICK, 2 * HEAD_DIM), BF)] * len(asked),
        scratch_shapes=[pltpu.VMEM((mem_len, 2 * HEAD_DIM), BF)],
        cost_estimate=SMALL,
        name="gather_rows",
    )(*asked, cache_keys, cache_values)


def turn(part, cosine, sine):
    return part * cosine + pltpu.roll(part, HEAD_DIM // 2, 1) * sine


def turn_back(part, cosine, sine):
    return part * cosine - pltpu.roll(part, HEAD_DIM // 2, 1) * sine


def project_body(
    tokens_ref, gain_ref, wq_ref, wk_ref, wv_ref, cos_ref, sin_ref, q_ref, k_ref, v_ref, n_ref
):
    length = tokens_ref.shape[0]
    width = wq_ref.shape[1]
    tile = min(SUB, length)

    @pl.when(pl.program_id(0) == 0)
    def _():
        for start in range(0, length, tile):
            rows = slice(start, start + tile)
            x = tokens_ref[rows].astype(F32)
            scale = lax.rsqrt(jnp.mean(x * x, axis=-1, keepdims=True) + EPS)
            n_ref[rows] = (x * scale * gain_ref[...]).astype(BF)

    for start in range(0, length, tile):
        rows = slice(start, start + tile)
        x = n_ref[rows]
        cosine, sine = cos_ref[rows], sin_ref[rows]
        for w_ref, o_ref in ((wq_ref, q_ref), (wk_ref, k_ref)):
            full = dot(x, w_ref[...], 1, 0)
            for at in range(0, width, HEAD_DIM):
                cols = slice(at, at + HEAD_DIM)
                o_ref[rows, cols] = turn(full[:, cols], cosine, sine).astype(BF)
        v_ref[rows] = dot(x, wv_ref[...], 1, 0).astype(BF)


def project(tokens, gain, wq, wk, wv, cosine, sine):
    length, dim = tokens.shape
    cols = wq.shape[1]
    width = 2 * HEAD_DIM if cols % (2 * HEAD_DIM) == 0 else HEAD_DIM
    whole = lambda shape: pl.BlockSpec(shape, lambda g: (0, 0))
    return pl.pallas_call(
        project_body,
        grid=(cols // width,),
        in_specs=[whole((length, dim)), whole((1, dim))]
        + [pl.BlockSpec((dim, width), lambda g: (0, g))] * 3
        + [whole((length, HEAD_DIM))] * 2,
        out_specs=[pl.BlockSpec((length, width), lambda g: (0, g))] * 3 + [whole((length, dim))],
        out_shape=[jax.ShapeDtypeStruct((length, cols), BF)] * 3
        + [jax.ShapeDtypeStruct((length, dim), BF)],
        cost_estimate=SMALL,
        name="project",
    )(tokens, gain, wq, wk, wv, cosine, sine)


def window(start, size):
    return max(0, start - DOC_MOST), start + size


def make_bias(bias_ref, index, doc_row_ref, doc_col_ref, row0, start, size):
    low, high = window(row0 + start, size)
    at_query = lax.broadcasted_iota(jnp.int32, (size, high - low), 0) + (row0 + start)
    at_key = lax.broadcasted_iota(jnp.int32, (size, high - low), 1) + low
    same = doc_row_ref[:, low:high] == doc_col_ref[start : start + size]
    bias_ref[index, :, : high - low] = jnp.where(same & (at_key <= at_query), 0.0, NEG)


def forward_body(row0, far_count, *refs):
    q_ref, k_ref, v_ref, doc_row_ref, doc_col_ref = refs[:5]
    far_refs = refs[5 : 5 + far_count]
    outs = refs[5 + far_count :]
    o_ref, lse_ref = outs[:2]
    far_ref = outs[2] if far_count else None
    bias_ref = outs[-1]
    count = q_ref.shape[0]
    size = min(SUB, count)
    scale = 1.0 / math.sqrt(HEAD_DIM)

    @pl.when(pl.program_id(0) == 0)
    def _():
        for index, start in enumerate(range(0, count, size)):
            make_bias(bias_ref, index, doc_row_ref, doc_col_ref, row0, start, size)

    if far_count:
        total = far_refs[0][0]
        for other in far_refs[1:]:
            total = total + other[0]
        far_ref[0] = total
    for index, start in enumerate(range(0, count, size)):
        low, high = window(row0 + start, size)
        rows = slice(start, start + size)
        q = q_ref[rows]
        s = dot(q, k_ref[low:high], 1, 1) * scale + bias_ref[index, :, : high - low]
        m = jnp.max(s, axis=1, keepdims=True)
        if far_count:
            far_bias = jnp.where(doc_col_ref[rows] == doc_row_ref[:, 0:1], 0.0, NEG)
            sf = jnp.concatenate(
                [
                    dot(
                        q[at : at + PICK_BLOCK],
                        far_ref[0, start + at : start + at + PICK_BLOCK, :HEAD_DIM],
                        1,
                        1,
                    )
                    for at in range(0, size, PICK_BLOCK)
                ],
                axis=0,
            )
            sf = sf * scale + far_bias
            m = jnp.maximum(m, jnp.max(sf, axis=1, keepdims=True))
        p = jnp.exp(s - m)
        total = jnp.sum(p, axis=1, keepdims=True)
        o = dot(p.astype(BF), v_ref[low:high], 1, 0)
        if far_count:
            pf = jnp.exp(sf - m)
            total = total + jnp.sum(pf, axis=1, keepdims=True)
            pf = pf.astype(BF)
            o = o + jnp.concatenate(
                [
                    dot(
                        pf[at : at + PICK_BLOCK],
                        far_ref[0, start + at : start + at + PICK_BLOCK, HEAD_DIM:],
                        1,
                        0,
                    )
                    for at in range(0, size, PICK_BLOCK)
                ],
                axis=0,
            )
        o_ref[rows] = (o / total).astype(BF)
        lse_ref[0, rows] = m + jnp.log(total)


def attend_forward(q, k, v, doc_row, doc_col, row0, count, far):
    heads = q.shape[1] // HEAD_DIM
    seg_len = q.shape[0]
    high = row0 + count
    at = row0 // count
    size = min(SUB, count)
    wide = max(w[1] - w[0] for w in (window(row0 + s, size) for s in range(0, count, size)))
    key_spec = pl.BlockSpec((high, HEAD_DIM), lambda h: (0, h))
    far_spec = pl.BlockSpec((1, count, 2 * HEAD_DIM), lambda h: (h, 0, 0))
    far_shape = jax.ShapeDtypeStruct((heads, count, 2 * HEAD_DIM), BF)
    return pl.pallas_call(
        functools.partial(forward_body, row0, len(far)),
        grid=(heads,),
        in_specs=[
            pl.BlockSpec((count, HEAD_DIM), lambda h: (at, h)),
            key_spec,
            key_spec,
            pl.BlockSpec((1, seg_len), lambda h: (0, 0)),
            pl.BlockSpec((count, 1), lambda h: (at, 0)),
        ]
        + [far_spec] * len(far),
        out_specs=[
            pl.BlockSpec((count, HEAD_DIM), lambda h: (0, h)),
            pl.BlockSpec((1, count, 1), lambda h: (h, 0, 0)),
        ]
        + [far_spec] * bool(far),
        out_shape=[
            jax.ShapeDtypeStruct((count, heads * HEAD_DIM), BF),
            jax.ShapeDtypeStruct((heads, count, 1), F32),
        ]
        + [far_shape] * bool(far),
        scratch_shapes=[pltpu.VMEM((count // size, size, wide), F32)],
        cost_estimate=SMALL,
        name="attend_forward",
    )(q, k, v, doc_row, doc_col, *far)


def backward_body(row0, far_on, *refs):
    (
        q_ref,
        k_ref,
        v_ref,
        doc_row_ref,
        doc_col_ref,
        o_ref,
        do_ref,
        lse_ref,
        cos_ref,
        sin_ref,
    ) = refs[:10]
    rest = list(refs[10:])
    if far_on:
        far_ref = rest.pop(0)
    if row0 == 0:
        add_k_ref, add_v_ref = rest.pop(0), rest.pop(0)
    grad_ref = rest[0]
    heads = grad_ref.shape[1] // (3 * HEAD_DIM)
    dq_ref, dk_ref, dv_ref = (
        grad_ref.at[
            :, pl.ds(pl.multiple_of((i * heads + pl.program_id(0)) * HEAD_DIM, HEAD_DIM), HEAD_DIM)
        ]
        for i in range(3)
    )
    if row0:
        low_k_ref, low_v_ref = rest[1:3]
    bias_ref, acc_k_ref, acc_v_ref = rest[-3:]
    count = q_ref.shape[0]
    size = min(SUB, count)
    scale = 1.0 / math.sqrt(HEAD_DIM)

    @pl.when(pl.program_id(0) == 0)
    def _():
        for index, start in enumerate(range(0, count, size)):
            make_bias(bias_ref, index, doc_row_ref, doc_col_ref, row0, start, size)

    if row0:
        acc_k_ref[...] = jnp.zeros(acc_k_ref.shape, F32)
        acc_v_ref[...] = jnp.zeros(acc_v_ref.shape, F32)
    else:
        acc_k_ref[...] = add_k_ref[...]
        acc_v_ref[...] = add_v_ref[...]
    for index, start in enumerate(range(0, count, size)):
        low, high = window(row0 + start, size)
        rows = slice(start, start + size)
        q, do, lse = q_ref[rows], do_ref[rows], lse_ref[0, rows]
        delta = jnp.sum(do.astype(F32) * o_ref[rows].astype(F32), axis=1, keepdims=True)
        keys, values = k_ref[low:high], v_ref[low:high]
        p = jnp.exp(dot(q, keys, 1, 1) * scale + bias_ref[index, :, : high - low] - lse)
        ds = (p * (dot(do, values, 1, 1) - delta)).astype(BF)
        acc_v_ref[low:high] += dot(p.astype(BF), do, 0, 0)
        acc_k_ref[low:high] += dot(ds, q, 0, 0)
        dq = dot(ds, keys, 1, 0)
        if far_on:
            far_bias = jnp.where(doc_col_ref[rows] == doc_row_ref[:, 0:1], 0.0, NEG) - lse
            parts = []
            for at in range(0, size, PICK_BLOCK):
                cut = slice(at, at + PICK_BLOCK)
                far_keys = far_ref[0, start + at : start + at + PICK_BLOCK, :HEAD_DIM]
                far_values = far_ref[0, start + at : start + at + PICK_BLOCK, HEAD_DIM:]
                pf = jnp.exp(dot(q[cut], far_keys, 1, 1) * scale + far_bias[cut])
                dsf = (pf * (dot(do[cut], far_values, 1, 1) - delta[cut])).astype(BF)
                parts.append(dot(dsf, far_keys, 1, 0))
            dq = dq + jnp.concatenate(parts, axis=0)
        at_rows = slice(row0 + start, row0 + start + size)
        dq_ref[rows] = turn_back(dq * scale, cos_ref[at_rows], sin_ref[at_rows]).astype(BF)
    dv_ref[...] = acc_v_ref[row0 : row0 + count].astype(BF)
    dk_ref[...] = turn_back(
        acc_k_ref[row0 : row0 + count] * scale,
        cos_ref[row0 : row0 + count],
        sin_ref[row0 : row0 + count],
    ).astype(BF)
    if row0:
        low_k_ref[...] = acc_k_ref[:row0]
        low_v_ref[...] = acc_v_ref[:row0]


def attend_backward(
    q, k, v, doc_row, doc_col, out, grad_out, lse, cosine, sine, row0, count, far, low
):
    heads = q.shape[1] // HEAD_DIM
    seg_len = q.shape[0]
    high = row0 + count
    at = row0 // count
    size = min(SUB, count)
    wide = max(w[1] - w[0] for w in (window(row0 + s, size) for s in range(0, count, size)))
    head_cols = lambda n: pl.BlockSpec((n, HEAD_DIM), lambda h: (0, h))
    whole = lambda n, m: pl.BlockSpec((n, m), lambda h: (0, 0))
    in_specs = [
        pl.BlockSpec((count, HEAD_DIM), lambda h: (at, h)),
        head_cols(high),
        head_cols(high),
        whole(1, seg_len),
        pl.BlockSpec((count, 1), lambda h: (at, 0)),
        head_cols(count),
        head_cols(count),
        pl.BlockSpec((1, count, 1), lambda h: (h, 0, 0)),
        whole(high, HEAD_DIM),
        whole(high, HEAD_DIM),
    ]
    args = [q, k, v, doc_row, doc_col, out, grad_out, lse, cosine, sine]
    if far is not None:
        in_specs.append(pl.BlockSpec((1, count, 2 * HEAD_DIM), lambda h: (h, 0, 0)))
        args.append(far)
    if row0 == 0:
        in_specs += [head_cols(count)] * 2
        args += list(low)
    out_specs = [whole(count, 3 * heads * HEAD_DIM)]
    out_shape = [jax.ShapeDtypeStruct((count, 3 * heads * HEAD_DIM), BF)]
    if row0:
        out_specs += [head_cols(row0)] * 2
        out_shape += [jax.ShapeDtypeStruct((row0, heads * HEAD_DIM), F32)] * 2
    return pl.pallas_call(
        functools.partial(backward_body, row0, far is not None),
        grid=(heads,),
        in_specs=in_specs,
        out_specs=out_specs,
        out_shape=out_shape,
        scratch_shapes=[
            pltpu.VMEM((count // size, size, wide), F32),
            pltpu.VMEM((high, HEAD_DIM), F32),
            pltpu.VMEM((high, HEAD_DIM), F32),
        ],
        cost_estimate=COVER,
        name="attend_backward",
    )(*args)


def bit_of(bit):
    return (lax.axis_index("seg") >> bit) & 1


def half_rows(part, which):
    size = part.shape[0] // 2
    return lax.dynamic_slice_in_dim(part, which * size, size)


def z_of():
    return lax.axis_index("seg") >> 2


def z_swap(block, shift):
    count = lax.axis_size("seg")
    return lax.ppermute(block, "seg", [(i, i ^ (shift << 2)) for i in range(count)])


def split_body(at_ref, part_ref, got_ref, *out_refs):
    total = (part_ref[...].astype(F32) + got_ref[...].astype(F32)).astype(BF)
    for shift, out_ref in enumerate(out_refs):

        @pl.when(pl.program_id(0) == shift)
        def _():
            out_ref[...] = total


def split_z(part, got, bit):
    rows, cols = got.shape[0] // 4, got.shape[1]
    return pl.pallas_call(
        split_body,
        grid_spec=pltpu.PrefetchScalarGridSpec(
            num_scalar_prefetch=1,
            grid=(4,),
            in_specs=[
                pl.BlockSpec((rows, cols), lambda s, at: (4 * at[0] + (at[1] ^ s), 0)),
                pl.BlockSpec((rows, cols), lambda s, at: (at[1] ^ s, 0)),
            ],
            out_specs=[pl.BlockSpec((rows, cols), lambda s, at: (0, 0))] * 4,
        ),
        out_shape=[jax.ShapeDtypeStruct((rows, cols), BF)] * 4,
        cost_estimate=SMALL,
        name="split_z",
    )(jnp.stack([bit_of(bit), z_of()]), part, got)


def join_body(at_ref, *refs):
    for shift, ref in enumerate(refs[:-1]):

        @pl.when(pl.program_id(0) == shift)
        def _():
            refs[-1][...] = ref[...]


def join_z(parts):
    rows, cols = parts[0].shape
    return pl.pallas_call(
        join_body,
        grid_spec=pltpu.PrefetchScalarGridSpec(
            num_scalar_prefetch=1,
            grid=(4,),
            in_specs=[pl.BlockSpec((rows, cols), lambda s, at: (0, 0))] * 4,
            out_specs=pl.BlockSpec((rows, cols), lambda s, at: (at[0] ^ s, 0)),
        ),
        out_shape=jax.ShapeDtypeStruct((4 * rows, cols), BF),
        cost_estimate=SMALL,
        name="join_z",
    )(z_of().reshape(1), *parts)


def double_body(mine_ref, part_ref, got_ref, out_ref):
    rows = part_ref.shape[0]
    for mine in (0, 1):

        @pl.when(mine_ref[0] == mine)
        def _():
            out_ref[mine * rows : (mine + 1) * rows] = part_ref[...]
            out_ref[(1 - mine) * rows : (2 - mine) * rows] = got_ref[...]


def double(part, got, bit):
    rows, cols = part.shape
    return pl.pallas_call(
        double_body,
        in_specs=[pl.BlockSpec(memory_space=pltpu.SMEM)] + [pl.BlockSpec((rows, cols))] * 2,
        out_specs=pl.BlockSpec((2 * rows, cols)),
        out_shape=jax.ShapeDtypeStruct((2 * rows, cols), BF),
        cost_estimate=SMALL,
        name="double",
    )(bit_of(bit).reshape(1), part, got)


def close_body(mine_ref, part_ref, got_ref, *out_refs):
    width = part_ref.shape[1] // len(out_refs)
    for owner, ref in ((0, part_ref), (1, got_ref)):

        @pl.when((pl.program_id(0) == mine_ref[0]) == (owner == 0))
        def _():
            for i, out_ref in enumerate(out_refs):
                out_ref[...] = ref[:, i * width : (i + 1) * width].astype(F32)


def double_out(part, got, bit, pieces=1, fold=False):
    rows, cols = part.shape
    width = cols // pieces
    full = pl.BlockSpec((rows, cols), lambda h, mine: (0, 0))
    specs = [pl.BlockSpec((rows, width), lambda h, mine: (h, 0))] * pieces
    shapes = [jax.ShapeDtypeStruct((2 * rows, width), F32)] * pieces
    if fold:
        specs[-1] = pl.BlockSpec((rows, width), lambda h, mine: (0, h))
        shapes[-1] = jax.ShapeDtypeStruct((rows, 2 * width), F32)
    return pl.pallas_call(
        close_body,
        grid_spec=pltpu.PrefetchScalarGridSpec(
            num_scalar_prefetch=1, grid=(2,), in_specs=[full, full], out_specs=specs
        ),
        out_shape=shapes,
        cost_estimate=SMALL,
        name="double_out",
    )(bit_of(bit).reshape(1), part, got)


def attention_grads_body(n_a, n_b, j_a, j_b, o_a, o_b, g_a, g_b, out_ref):
    cols = g_a.shape[1]
    joint = (dot(n_a[...], j_a[...], 0, 0) + dot(n_b[...], j_b[...], 0, 0)).astype(BF)
    out_ref[:, : 3 * cols] = joint
    out_ref[:, 3 * cols :] = (
        dot(o_a[...], g_a[...], 0, 0) + dot(o_b[...], g_b[...], 0, 0)
    ).astype(BF)


def attention_grads(normed, joint_a, joint_b, att_a, att_b, grad_a, grad_b):
    dim = normed.shape[1]
    count, width = joint_a.shape
    cols = att_a.shape[1]
    tile = min(SUB, cols)
    folds = cols // tile
    cut = lambda chunk: pl.BlockSpec((count, tile), lambda i: (chunk, i))
    joint = pl.BlockSpec((count, width), lambda i: (0, 0))
    att = pl.BlockSpec((count, tile), lambda i: (0, i % folds))
    grad = pl.BlockSpec((count, cols), lambda i: (0, i // folds))
    return pl.pallas_call(
        attention_grads_body,
        grid=(dim // tile,),
        in_specs=[cut(0), cut(1), joint, joint, att, att, grad, grad],
        out_specs=pl.BlockSpec((tile, width + cols), lambda i: (i, 0)),
        out_shape=jax.ShapeDtypeStruct((dim, width + cols), BF),
        cost_estimate=COVER,
        name="attention_grads",
    )(normed, normed, joint_a, joint_b, att_a, att_b, grad_a, grad_b)


def rows_dot_body(a_ref, b_ref, out_ref):
    out_ref[...] = dot(a_ref[...], b_ref[...], 1, 0).astype(BF)


def rows_dot(a, b):
    rows, depth = a.shape
    cols = b.shape[1]
    tile = 2 * SUB if cols % (2 * SUB) == 0 else cols
    return pl.pallas_call(
        rows_dot_body,
        grid=(cols // tile,),
        in_specs=[
            pl.BlockSpec((rows, depth), lambda j: (0, 0)),
            pl.BlockSpec((depth, tile), lambda j: (0, j)),
        ],
        out_specs=pl.BlockSpec((rows, tile), lambda j: (0, j)),
        out_shape=jax.ShapeDtypeStruct((rows, cols), BF),
        cost_estimate=SMALL,
        name="rows_dot",
    )(a, b)


def chunk_specs(count, tile, dim):
    steps = count // tile
    first = pl.BlockSpec((tile, dim), lambda g: (jnp.minimum(g, steps - 1), 0))
    second = pl.BlockSpec((tile, dim), lambda g: (jnp.maximum(g - steps, 0), 0))
    return steps, first, second


def output_body(steps, *refs):
    for chunk in (0, 1):
        hidden_ref, mine_ref, got_ref = refs[3 * chunk : 3 * chunk + 3]

        @pl.when((pl.program_id(0) < steps) == (chunk == 0))
        def _():
            total = mine_ref[...].astype(F32) + got_ref[...].astype(F32)
            refs[-1][...] = (hidden_ref[...] + total).astype(BF)


def output_rows(early, late):
    count, dim = early[0].shape
    tile = min(SUB, count)
    steps, first, second = chunk_specs(count, tile, dim)
    return pl.pallas_call(
        functools.partial(output_body, steps),
        grid=(2 * steps,),
        in_specs=[first] * 3 + [second] * 3,
        out_specs=pl.BlockSpec((tile, dim), lambda g: (g, 0)),
        out_shape=jax.ShapeDtypeStruct((2 * count, dim), BF),
        cost_estimate=SMALL,
        name="output_rows",
    )(*early, *late)


def norm_one_body(steps, x_ref, gain_ref, *refs):
    out_ref, grad_gain_ref = refs[-2:]

    @pl.when(pl.program_id(0) == 0)
    def _():
        grad_gain_ref[...] = jnp.zeros(grad_gain_ref.shape, F32)

    for chunk in (0, 1):
        total_ref, mine_ref, got_ref = refs[3 * chunk : 3 * chunk + 3]

        @pl.when((pl.program_id(0) < steps) == (chunk == 0))
        def _():
            x = x_ref[...].astype(F32)
            grad = mine_ref[...].astype(F32) + got_ref[...].astype(F32)
            scale = lax.rsqrt(jnp.mean(x * x, axis=-1, keepdims=True) + EPS)
            weighted = grad * gain_ref[...]
            inner = jnp.mean(weighted * x, axis=-1, keepdims=True)
            rows = scale * weighted - x * (scale * scale * scale * inner)
            out_ref[...] = (total_ref[...] + rows).astype(BF)
            grad_gain_ref[...] += jnp.sum(grad * x * scale, axis=0, keepdims=True)


def norm_one_rows(tokens, gain, early, late):
    count, dim = early[0].shape
    tile = min(SUB, count)
    steps, first, second = chunk_specs(count, tile, dim)
    rows = pl.BlockSpec((tile, dim), lambda g: (g, 0))
    line = pl.BlockSpec((1, dim), lambda g: (0, 0))
    return pl.pallas_call(
        functools.partial(norm_one_body, steps),
        grid=(2 * steps,),
        in_specs=[rows, line] + [first] * 3 + [second] * 3,
        out_specs=[rows, line],
        out_shape=[
            jax.ShapeDtypeStruct((2 * count, dim), BF),
            jax.ShapeDtypeStruct((1, dim), F32),
        ],
        cost_estimate=SMALL,
        name="norm_one_rows",
    )(tokens, gain, *early, *late)


def shards(
    tokens,
    document_ids,
    memory_picks,
    partner_ids,
    memory_keys,
    memory_values,
    first_gain,
    query_weight,
    key_weight,
    value_weight,
    out_weight,
    second_gain,
    gate_weight,
    up_weight,
    down_weight,
    cotangent,
):
    seg_len = document_ids.shape[1]
    heads = query_weight.shape[1] // HEAD_DIM
    mem_len = memory_keys.shape[1]
    blocks = memory_picks.shape[2]
    near = min(blocks, DOC_MOST // PICK_BLOCK)
    chunk = near * PICK_BLOCK
    me = lax.axis_index("seg")
    bits = lax.axis_size("seg").bit_length() - 1
    partner = partner_ids[0]
    paired = lax.axis_size("head") == 2

    ranks = rank_picks(memory_picks.reshape(heads * blocks, 2 * mem_len))
    ranks = ranks.reshape(heads, blocks, 2 * mem_len)[:, :near]
    first_len = jnp.sum((document_ids[0] == document_ids[0, 0]).astype(jnp.int32))
    used = (jnp.arange(near) * PICK_BLOCK < first_len)[None, :, None]
    ranks = jnp.where(used, ranks, 0)
    own_ranks, far_ranks = ranks[:, :, :mem_len], ranks[:, :, mem_len:]
    asked = [own_ranks]
    for bit in range(bits):
        wanted = partner == jnp.bitwise_xor(me, 1 << bit)
        asked.append(swap(jnp.where(wanted, far_ranks, jnp.zeros_like(far_ranks)), bit))

    cosine, sine = rope_tables(seg_len)
    doc_row = document_ids
    doc_col = document_ids.reshape(seg_len, 1)
    dim = tokens.shape[1]
    token = [first_gain]

    def order(*values):
        values, token[0] = lax.optimization_barrier((values, token[0]))
        return values

    exchange = lambda mine: head_swap(mine) if paired else lax.psum(mine, "head")
    mine_of = lambda mine: mine if paired else jnp.zeros_like(mine)
    full = lambda mine, got: mine_of(mine).astype(F32) + got.astype(F32)

    q, k, v, normed_one = project(
        tokens, first_gain.reshape(1, -1), query_weight, key_weight, value_weight, cosine, sine
    )
    out_got = head_swap(out_weight) if paired else None
    joint_weight = jnp.concatenate([query_weight, key_weight, value_weight], axis=1)

    far = [None] * (bits + 1)
    split = max(1, bits - 2)

    def send_rows(slots):
        ranks = order(*(asked[slot] for slot in slots))
        rows = order(*gather_rows(list(ranks), memory_keys[0], memory_values[0]))
        for slot, block in zip(slots, rows):
            far[slot] = swap(block, slot - 1) if slot else block

    q, *asked = order(q, *asked)
    send_rows(range(bits, split, -1))

    def start_mix(st):
        (st.att,) = order(st.att)
        if paired:
            st.got_att = head_swap(st.att)

    def mix(st):
        if paired:
            (got,) = order(st.got_att)
            joined = head_join(st.att, got, 1)
            return jnp.dot(joined, out_full, preferred_element_type=F32)
        return head_sum(jnp.dot(st.att, out_weight, preferred_element_type=F32).astype(BF))

    def feed(st, cut):
        st.hidden_in = tokens[cut].astype(F32) + st.mixed
        st.scale = rms_scale(st.hidden_in)
        normed_two = (st.hidden_in * st.scale * second_gain).astype(BF)
        gate = jnp.dot(normed_two, gate_weight, preferred_element_type=F32)
        upper = jnp.dot(normed_two, up_weight, preferred_element_type=F32)
        sigmoid_gate = jax.nn.sigmoid(gate)
        grad_hidden = dot(cotangent[cut], down_weight, 1, 1)
        st.hidden = (gate * sigmoid_gate * upper).astype(BF)
        st.grad_gate = (
            grad_hidden * upper * sigmoid_gate * (1.0 + gate * (1.0 - sigmoid_gate))
        ).astype(BF)
        st.grad_upper = (grad_hidden * gate * sigmoid_gate).astype(BF)
        st.normed_two = normed_two
        st.part_two = (
            dot(st.grad_gate, gate_weight, 1, 1) + dot(st.grad_upper, up_weight, 1, 1)
        ).astype(BF)

    def feed_grads(st, cut):
        return (
            dot(st.hidden, cotangent[cut], 0, 0),
            dot(
                st.normed_two,
                jnp.concatenate([st.grad_gate, st.grad_upper], axis=1),
                0,
                0,
            ),
        )

    def feed_out(st):
        down_part = jnp.dot(st.hidden, down_weight, preferred_element_type=F32)
        st.output = (st.hidden_in + head_sum(down_part.astype(BF))).astype(BF)

    def norm_two(st, cut):
        rows, st.second_gain_grad = norm_backward(
            st.grad_normed_two, st.hidden_in, st.scale, second_gain
        )
        st.total_grad = cotangent[cut].astype(F32) + rows
        st.grad_mixed = st.total_grad.astype(BF)
        st.grad_att = dot(st.grad_mixed, out_weight, 1, 1).astype(BF)

    def back(st, row0, low):
        parts = attend_backward(
            q, k, v, doc_row, doc_col, st.att, st.grad_att, st.lse, cosine, sine,
            row0, chunk, getattr(st, "far", None), low,
        )
        st.joint = parts[0]
        return parts[1:]

    late, early = slice(chunk, 2 * chunk), slice(0, chunk)
    b, a = SimpleNamespace(), SimpleNamespace()
    (q,) = order(q)
    b.att, b.lse = attend_forward(q, k, v, doc_row, doc_col, chunk, chunk, [])
    if paired:
        (out_got,) = order(out_got)
        out_full = head_join(out_weight, out_got, 0)
    start_mix(b)
    send_rows([0, *range(1, split + 1)])
    b.mixed = mix(b)
    feed(b, late)
    (b.part_two,) = order(b.part_two)
    b.got_two = exchange(b.part_two)
    far_hi = order(*far[split + 1 :])
    *b_grads, joint_weight = order(*feed_grads(b, late), joint_weight)
    far = order(*far[: split + 1]) + far_hi
    a.att, a.lse, a.far = attend_forward(q, k, v, doc_row, doc_col, 0, chunk, list(far))
    start_mix(a)
    (got,) = order(b.got_two)
    b.grad_normed_two = full(b.part_two, got)
    norm_two(b, late)
    (b.grad_att,) = order(b.grad_att)
    low = back(b, chunk, None)
    b.joint, *low = order(b.joint, *low)
    a.mixed = mix(a)
    feed(a, early)

    plan = []

    def at(time):
        return lambda step: plan.append((time, step))

    def piece(make_time, make, times, close):
        st = SimpleNamespace()
        starts, ends = times[0::2], times[1::2]

        def step(i, begin, end):
            @at(starts[i])
            def _():
                st.sent = order(*st.send)
                st.got = begin(st.sent)

            @at(ends[i])
            def _():
                end(order(*st.got))

        def core_half(got):
            keep = half_rows(st.part, bit_of(0))
            st.part = (keep.astype(F32) + got[0].astype(F32)).astype(BF)
            st.send = (half_rows(st.part, 1 - bit_of(1)),)

        def y_half(got):
            own, *st.send = split_z(st.part, got[0], 1)
            st.part = own

        def z_sum(got):
            total = sum((part.astype(F32) for part in got), st.part.astype(F32))
            st.part = total.astype(BF)
            st.send = (st.part,)

        def z_join(got):
            st.part = join_z([st.part, *got])
            st.send = (st.part,)

        def y_double(got):
            st.part = double(st.part, got[0], 1)
            st.send = (st.part,)

        @at(make_time)
        def _():
            (st.part,) = order(make())
            st.send = (half_rows(st.part, 1 - bit_of(0)),)

        one = lambda bit: lambda send: (swap(send[0], bit),)
        step(0, one(0), core_half)
        step(1, one(1), y_half)
        step(2, lambda send: tuple(z_swap(send[i], i + 1) for i in range(3)), z_sum)
        step(3, lambda send: tuple(z_swap(send[0], i + 1) for i in range(3)), z_join)
        step(4, one(1), y_double)
        step(5, one(0), lambda got: close(st.part, got[0]))
        return st

    done = SimpleNamespace()

    def close_as(*names, fold=False):
        def close(part, got):
            for name, value in zip(names, order(*double_out(part, got, 0, len(names), fold))):
                setattr(done, name, value)

        return close


    def make_down():
        (a.hidden,) = order(a.hidden)
        return (b_grads[0] + dot(a.hidden, cotangent[early], 0, 0)).astype(BF)

    def make_feed():
        a.grad_gate, a.grad_upper = order(a.grad_gate, a.grad_upper)
        return (b_grads[1] + feed_grads(a, early)[1]).astype(BF)

    joined = [make_down, make_feed]

    if paired and bits == 4:
        piece(
            194,
            joined[0],
            [198, 207, 208, 213.2, 213.3, 214.3, 214.4, 215.2, 219.135, 219.55, 219.97, 220.5],
            close_as("down"),
        )
        piece(
            199,
            joined[1],
            [206, 208.5, 208.6, 215.5, 215.6, 219, 219.1, 219.5, 219.6, 221.9, 221.95, 226],
            close_as("gate", "up"),
        )
        piece(
            215,
            lambda: attention_grads(
                normed_one, a.joint, b.joint, a.att, b.att,
                a.grad_mixed, b.grad_mixed,
            ),
            [215.7, 218, 218.02, 219.12, 219.14, 219.9, 219.95, 221, 221.1, 227, 227.1, 229],
            close_as("query", "key", "value", "out", fold=True),
        )
    else:

        @at(300)
        def _():
            total = lambda part: lax.psum(part.astype(BF), "seg").astype(F32)
            joint = dot(normed_one[late], b.joint, 0, 0)
            joint = total(joint + dot(normed_one[early], a.joint, 0, 0))
            done.query, done.key, done.value = jnp.split(joint, 3, axis=1)
            out = dot(b.att, b.grad_mixed, 0, 0) + dot(a.att, a.grad_mixed, 0, 0)
            done.out = total(out)
            done.down, both = (total(make()) for make in joined)
            done.gate, done.up = jnp.split(both, 2, axis=1)

    down = lambda st: rows_dot(order(st.hidden)[0], down_weight)
    back_part = lambda st: dot(order(st.joint)[0], joint_weight, 1, 1).astype(BF)
    @at(193)
    def _():
        (a.part_two,) = order(a.part_two)
        a.got_two = exchange(a.part_two)

    @at(208.7)
    def _():
        (b.down,) = order(down(b))

    @at(208.8)
    def _():
        (a.down,) = order(down(a))

    @at(209)
    def _():
        (got,) = order(a.got_two)
        a.grad_normed_two = full(a.part_two, got)

    sent, taken = {}, {}

    def head(key, send_time, part, take_time):
        @at(send_time)
        def _():
            (sent[key],) = order(part())
            taken[key] = exchange(sent[key])

        @at(take_time)
        def _():
            (taken[key],) = order(taken[key])

    head(0, 209.5, lambda: b.down, 214.5)
    head(1, 214.6, lambda: a.down, 219.121)
    head(2, 219.122, lambda: b.part_one, 219.91)
    head(3, 219.92, lambda: a.part_one, 221.15)

    @at(210)
    def _():
        norm_two(a, early)
        a.grad_att, a.grad_mixed = order(a.grad_att, a.grad_mixed)

    @at(214)
    def _():
        (a.grad_att,) = order(a.grad_att)
        back(a, 0, low)
        (a.joint,) = order(a.joint)

    @at(215.3)
    def _():
        (b.part_one,) = order(back_part(b))

    @at(218.05)
    def _():
        (a.part_one,) = order(back_part(a))

    rest = SimpleNamespace()

    @at(219.2)
    def _():
        (rest.output,) = order(
            output_rows(
                *(
                    (st.hidden_in, mine_of(sent[key]), taken[key])
                    for st, key in ((a, 1), (b, 0))
                )
            )
        )

    @at(221.2)
    def _():
        rest.tokens_grad, first_gain_grad = order(
            *norm_one_rows(
                tokens,
                token[0].reshape(1, -1),
                *(
                    (st.total_grad, mine_of(sent[key]), taken[key])
                    for st, key in ((a, 3), (b, 2))
                ),
            )
        )
        second = (a.second_gain_grad + b.second_gain_grad).reshape(1, -1)
        token[0] = jnp.concatenate([first_gain_grad, second], axis=0)

    gain_bits = [0, *range(2, bits), 1]
    gain_times = [(221.3, 221.4), (221.5, 221.96), (222, 222.2), (222.3, 227.5), (227.6, 227.7)]
    for bit, (start, end) in zip(gain_bits, gain_times):

        @at(start)
        def _(bit=bit):
            done.gains_got = swap(token[0], bit)

        @at(end)
        def _():
            (got,) = order(done.gains_got)
            token[0] = token[0] + got

    for _, step in sorted(plan, key=lambda entry: entry[0]):
        step()
    gains = token[0]
    return (
        rest.output,
        rest.tokens_grad,
        gains[0],
        done.query,
        done.key,
        done.value,
        done.out,
        gains[1],
        done.gate,
        done.up,
        done.down,
    )


def solution(mesh):
    placed = (
        P("seg", None),
        P("seg", None),
        P("seg", "head", None, None),
        P("seg"),
        P("seg", None, "head"),
        P("seg", None, "head"),
        P(),
        P(None, "head"),
        P(None, "head"),
        P(None, "head"),
        P("head", None),
        P(),
        P(None, "head"),
        P(None, "head"),
        P("head", None),
        P("seg", None),
    )
    return jax.shard_map(
        shards,
        mesh=mesh,
        in_specs=placed,
        out_specs=(
            P("seg", None),
            P("seg", None),
            P(),
            P(None, "head"),
            P(None, "head"),
            P(None, "head"),
            P("head", None),
            P(),
            P(None, "head"),
            P(None, "head"),
            P("head", None),
        ),
        check_vma=False,
    )
```
